32 devices in a mesh: dp: 8 (over z, x), tensor: 4 (over y, core).
Axes of the slice: x: 2, y: 2, z: 4, core: 2. Of those that a mesh axis runs over, the one named last changes fastest.
Arguments:
- tokens: bfloat16 [16384, 768], P(('dp', 'tensor')), may hold values from -6 to 6
- cotangent: bfloat16 [16384, 768], P(('dp', 'tensor')), may hold values from -6 to 6
- seq_lengths: int32 [8, 2], P('dp'), may hold values from 256 to 1792, as said below
- w_query: bfloat16 [768, 768], P('dp', 'tensor'), may hold values from -0.21875 to 0.21875
- w_keyvalue: bfloat16 [768, 128], P('dp'), may hold values from -0.21875 to 0.21875
- w_out: bfloat16 [768, 768], P('dp', 'tensor'), may hold values from -3.5 to 3.5
- w_up: bfloat16 [768, 3072], P('dp', 'tensor'), may hold values from -0.21875 to 0.21875
- w_down: bfloat16 [768, 3072], P('dp', 'tensor'), may hold values from -0.109375 to 0.109375
- norm1_gain: bfloat16 [768], P('dp'), may hold values from 0.5 to 1.5
- norm1_bias: bfloat16 [768], P('dp'), may hold values from -3 to 3
- norm2_gain: bfloat16 [768], P('dp'), may hold values from 0.5 to 1.5
- norm2_bias: bfloat16 [768], P('dp'), may hold values from -3 to 3
Outputs:
- out_tokens: bfloat16 [16384, 768], P(('dp', 'tensor'))
- d_tokens: float32 [16384, 768], P(('dp', 'tensor'))
- d_query: float32 [768, 768], P('dp', 'tensor')
- d_keyvalue: float32 [768, 128], P('dp')
- d_out_weight: float32 [768, 768], P('dp', 'tensor')
- d_up: float32 [768, 3072], P('dp', 'tensor')
- d_down: float32 [768, 3072], P('dp', 'tensor')
- d_norm1_gain: float32 [768], P('dp')
- d_norm1_bias: float32 [768], P('dp')
- d_norm2_gain: float32 [768], P('dp')
- d_norm2_bias: float32 [768], P('dp')
The draws below stay inside these ranges and needn't reach their ends.
Inputs may be any that keep to these rules, and one draw needn't show every extreme that they name: `seq_lengths`: each row holds the length of its pack's one sequence, from 1024 to 1792, then the padding after it; a row sums to 2048, and in some row the sequence is exactly 1792 long.
All inputs are finite; a program needn't handle non-finite values.
Results may differ from the reference program's by a relative error of at most 0.011.
Values may be sent and summed in bfloat16 or wider, within the bound.
A program may use at most 256 MiB of HBM per device.

```python
import math
import jax
import jax.numpy as jnp
from jax import lax

D = 768
HEADS = 12
HEAD = 64
FF = 3072
ROT = 16
PACK = 2048
SEQ_LEAST = 1024
SEQ_MOST = 1792
TOKENS = 16384
N_DP = 8
N_TENSOR = 4


def draw_seq_lengths(key, part):
    lengths = jax.random.randint(jax.random.fold_in(key, 11), (N_DP,), SEQ_LEAST, SEQ_MOST + 1).astype(jnp.int32)
    chosen = jax.random.randint(jax.random.fold_in(key, 12), (), 0, N_DP).astype(jnp.int32)
    lengths = jnp.where(lax.iota(jnp.int32, N_DP) == chosen, SEQ_MOST, lengths).astype(jnp.int32)
    return jnp.stack([lengths, PACK - lengths], axis=1).astype(jnp.int32)


def raised(values, stream_key, source, target, parts, factor):
    owner, partner = [(jnp.arange(values.shape[dim]) // (values.shape[dim] // parts)).reshape([-1 if axis == dim else 1 for axis in range(values.ndim)]) for dim in (source, target)]
    chosen = jax.random.permutation(stream_key, parts)[partner]
    strong = (owner == chosen) | (owner == (partner + parts // 2) % parts)
    return jnp.where(strong, factor * values, values)


def levels(stream_key, extent, cuts, smallest, high):
    loudness, own = 1.0, jax.random.fold_in(stream_key, 6)
    for axis_at, parts in cuts:
        steps = jnp.exp(jax.random.uniform(jax.random.fold_in(own, axis_at), (parts,), jnp.float32, smallest / len(cuts), high / len(cuts)))
        loudness = loudness * jnp.repeat(steps, extent[axis_at] // parts).reshape([-1 if axis == axis_at else 1 for axis in range(len(extent))])
    return loudness


def noise(stream_key, extent, width, bound, cuts=(), dtype=jnp.bfloat16):
    drawn = width * jax.random.normal(stream_key, extent, jnp.float32)
    if cuts:
        drawn = drawn * levels(stream_key, extent, cuts, -0.22, 0.18)
    return jnp.clip(drawn, -bound, bound).astype(dtype)


def heavy_noise(rng, extent, scale, reach, cuts, heavy, held_as=jnp.bfloat16):
    drawn = scale * jax.random.normal(rng, extent, jnp.float32)
    if cuts:
        drawn = drawn * levels(rng, extent, cuts, -0.22, 0.18)
    return jnp.clip(raised(drawn, jax.random.fold_in(rng, 3), *heavy), -reach, reach).astype(held_as)


def setup_inputs(seed: int = 0) -> dict:
    key_list = jax.random.split(jax.random.key(seed), 13)
    return {
        "tokens": noise(key_list[0], (TOKENS, D), 1.0, 6.0, ((0, 32),)),
        "cotangent": heavy_noise(key_list[1], (TOKENS, D), 1.0, 6.0, ((0, 32),), (0, 1, 32, 2.75)),
        "seq_lengths": draw_seq_lengths(jax.random.fold_in(key_list[12], 71), 0),
        "w_query": noise(key_list[3], (D, HEADS * HEAD), D ** -0.5, 0.21875, ((0, 8), (1, 4))),
        "w_keyvalue": noise(key_list[4], (D, 2 * HEAD), D ** -0.5, 0.21875, ((0, 8),)),
        "w_out": noise(key_list[5], (D, HEADS * HEAD), (HEADS * HEAD * 8 // PACK) ** -0.5, 3.5, ((0, 8), (1, 4))),
        "w_up": noise(key_list[6], (D, FF), D ** -0.5, 0.21875, ((0, 8), (1, 4))),
        "w_down": noise(key_list[7], (D, FF), FF ** -0.5, 0.109375, ((0, 8), (1, 4))),
        "norm1_gain": jnp.clip(1.0 + 0.1 * jax.random.normal(key_list[8], (D,), jnp.float32), 0.5, 1.5).astype(jnp.bfloat16),
        "norm1_bias": noise(key_list[9], (D,), 0.5, 3.0, ((0, 8),)),
        "norm2_gain": jnp.clip(1.0 + 0.1 * jax.random.normal(key_list[10], (D,), jnp.float32), 0.5, 1.5).astype(jnp.bfloat16),
        "norm2_bias": noise(key_list[11], (D,), 0.5, 3.0, ((0, 8),)),
    }


@jax.custom_vjp
def low(v):
    return lax.optimization_barrier(v.astype(jnp.bfloat16)).astype(jnp.float32)

@jax.custom_vjp
def low_back(v):
    return v

def low_keep(v):
    return (low(v), None)

def low_pass(kept, grad):
    return (grad,)

def back_keep(v):
    return (v, None)

def back_low(kept, grad):
    return (low(grad),)
low.defvjp(low_keep, low_pass)
low_back.defvjp(back_keep, back_low)
EPS = 1e-05
NEG = -1e+30
HIGH = lax.Precision.HIGHEST

def slot_tables(seq_lengths, pack_rows):
    seq_sizes = seq_lengths.reshape(-1).astype(jnp.int32)
    seq_ends = jnp.cumsum(seq_sizes).astype(jnp.int32)
    slot_index = lax.iota(jnp.int32, pack_rows)
    passed = (slot_index[:, None] >= seq_ends[None, :]).astype(jnp.int32)
    segment = lax.optimization_barrier(jnp.sum(passed, axis=1)).astype(jnp.int32)
    position = (slot_index - lax.optimization_barrier(jnp.sum(passed * seq_sizes[None, :], axis=1))).astype(jnp.int32)
    valid = (segment < seq_sizes.shape[0] - 1).astype(jnp.float32)
    return (segment, position, valid)

def rotary_tables(position, rot):
    half_rot = rot // 2
    exponent = lax.iota(jnp.int32, half_rot).astype(jnp.float32) * (-2.0 / rot)
    inv_freq = jnp.exp(exponent * math.log(10000.0))
    angles = position.astype(jnp.float32)[:, None] * inv_freq[None, :]
    return (jnp.cos(angles), jnp.sin(angles))

def rotate(field, cosine, sine, rot):
    half_rot = rot // 2
    first = field[..., :half_rot]
    second = field[..., half_rot:rot]
    cos_b = cosine[:, None, :]
    sin_b = sine[:, None, :]
    return jnp.concatenate([first * cos_b - second * sin_b, second * cos_b + first * sin_b, field[..., rot:]], axis=-1)

def layer_norm(token_f, gain, bias):
    mean = lax.optimization_barrier(jnp.mean(token_f, axis=-1, keepdims=True))
    centered = token_f - mean
    inv_std = lax.rsqrt(lax.optimization_barrier(jnp.mean(centered * centered, axis=-1, keepdims=True)) + EPS)
    return centered * inv_std * gain + bias

def matmul(left, right):
    return jnp.dot(left, right, precision=HIGH)

def matmul_t(left, right):
    return lax.dot_general(left, right, (((1,), (1,)), ((), ())), precision=HIGH)

def pack_forward(weights, token_f, seq_lengths):
    w_query, w_keyvalue, w_out, w_up, w_down, gain1, bias1, gain2, bias2 = weights
    segment, position, valid = slot_tables(seq_lengths, PACK)
    normed1 = low(layer_norm(token_f, gain1, bias1))
    normed2 = low(layer_norm(token_f, gain2, bias2))
    query_pre = low_back(matmul(normed1, w_query))
    kv_pre = matmul(normed1, w_keyvalue)
    cosine, sine = rotary_tables(position, ROT)
    queries = low(rotate(query_pre.reshape(PACK, HEADS, HEAD), cosine, sine, ROT))
    slot_index = lax.iota(jnp.int32, PACK)
    allowed = (segment[:, None] == segment[None, :]) & (slot_index[None, :] <= slot_index[:, None])
    group_heads = HEADS // N_TENSOR
    pieces = []
    for group in range(N_TENSOR):
        kv_group = low_back(kv_pre)
        keys = low(rotate(kv_group[:, None, :HEAD], cosine, sine, ROT)[:, 0])
        values = low(kv_group[:, HEAD:])
        q_group = queries[:, group * group_heads:(group + 1) * group_heads]
        scores = low_back(jnp.einsum('qhd,kd->hqk', q_group, keys, precision=HIGH) * HEAD ** (-0.5))
        scores = jnp.where(allowed[None], scores, NEG)
        top = lax.optimization_barrier(jnp.max(scores, axis=-1, keepdims=True))
        expd = jnp.exp(scores - top)
        probs = low(expd / lax.optimization_barrier(jnp.sum(expd, axis=-1, keepdims=True)))
        pieces.append(jnp.einsum('hqk,kd->qhd', probs, values, precision=HIGH))
    attended = low(low_back(jnp.concatenate(pieces, axis=1).reshape(PACK, HEADS * HEAD)))
    up_pre = low_back(matmul(normed2, w_up))
    hidden = low(jax.nn.gelu(up_pre, approximate=False))
    mixed = low_back(matmul_t(attended, w_out) + matmul_t(hidden, w_down))
    return token_f + mixed

def reference(tokens, cotangent, seq_lengths, w_query, w_keyvalue, w_out, w_up, w_down, norm1_gain, norm1_bias, norm2_gain, norm2_bias):
    weights = tuple((w.astype(jnp.float32) for w in (w_query, w_keyvalue, w_out, w_up, w_down, norm1_gain, norm1_bias, norm2_gain, norm2_bias)))
    token_f = tokens.astype(jnp.float32).reshape(N_DP, PACK, D)

    def forward(weight_set, token_all):

        def one_pack(pair):
            return pack_forward(weight_set, pair[0], pair[1])
        return lax.map(jax.checkpoint(one_pack), (token_all, seq_lengths))
    result, pullback = jax.vjp(forward, weights, token_f)
    valid = jax.vmap(lambda row: slot_tables(row, PACK)[2])(seq_lengths)
    grad_in = cotangent.astype(jnp.float32).reshape(N_DP, PACK, D) * valid[..., None]
    d_weights, d_token_all = pullback(grad_in)
    out_tokens = result.reshape(TOKENS, D).astype(jnp.bfloat16)
    d_tokens = d_token_all.reshape(TOKENS, D)
    return (out_tokens, d_tokens, d_weights[0], d_weights[1], d_weights[2], d_weights[3], d_weights[4], d_weights[5], d_weights[6], d_weights[7], d_weights[8])
```

```python
import functools
import math

import jax
import jax.numpy as jnp
from jax import lax
from jax.experimental import pallas as pl
from jax.experimental.pallas import tpu as pltpu
from jax.sharding import PartitionSpec as P

ROT = 16
BLOCK = 512


EPS = 1e-05
NEG = -1e30


def slot_tables(seq_lengths, pack_rows):
    seq_sizes = seq_lengths.reshape(-1)
    seq_ends = jnp.cumsum(seq_sizes)
    slot_index = lax.iota(jnp.int32, pack_rows)
    passed = (slot_index[:, None] >= seq_ends[None, :]).astype(jnp.int32)
    segment = jnp.sum(passed, axis=1)
    position = slot_index - jnp.sum(passed * seq_sizes[None, :], axis=1)
    valid = (segment < seq_sizes.shape[0] - 1).astype(jnp.float32)
    return (segment, position, valid)


def rotary_tables(position, rot):
    half_rot = rot // 2
    exponent = lax.iota(jnp.int32, half_rot).astype(jnp.float32) * (-2.0 / rot)
    inv_freq = jnp.exp(exponent * math.log(10000.0))
    angles = position.astype(jnp.float32)[:, None] * inv_freq[None, :]
    return (jnp.cos(angles), jnp.sin(angles))


def rotate(field, cosine, sine, rot):
    half_rot = rot // 2
    first = field[..., :half_rot]
    second = field[..., half_rot:rot]
    cos_b = cosine[:, None, :]
    sin_b = sine[:, None, :]
    return jnp.concatenate(
        [first * cos_b - second * sin_b, second * cos_b + first * sin_b, field[..., rot:]], axis=-1
    )


def rotate_back(grad, cosine, sine, rot):
    half_rot = rot // 2
    first = grad[..., :half_rot]
    second = grad[..., half_rot:rot]
    cos_b = cosine[:, None, :]
    sin_b = sine[:, None, :]
    return jnp.concatenate(
        [first * cos_b + second * sin_b, second * cos_b - first * sin_b, grad[..., rot:]], axis=-1
    )


def norm_stats(token_f):
    mean = jnp.mean(token_f, axis=-1, keepdims=True)
    centered = token_f - mean
    inv_std = lax.rsqrt(jnp.mean(centered * centered, axis=-1, keepdims=True) + EPS)
    return (centered * inv_std, inv_std)


def norm_back(d_scaled, scaled, inv_std):
    return inv_std * (
        d_scaled
        - jnp.mean(d_scaled, axis=-1, keepdims=True)
        - scaled * jnp.mean(d_scaled * scaled, axis=-1, keepdims=True)
    )


def contract_rows(left, right):
    return lax.dot_general(
        left, right, (((0,), (0,)), ((), ())), preferred_element_type=jnp.float32
    )


def contract_cols(left, right):
    return lax.dot_general(
        left, right, (((1,), (1,)), ((), ())), preferred_element_type=jnp.float32
    )


def visible(segment, first, block_rows, key_len):
    row_index = first + lax.iota(jnp.int32, block_rows)
    key_index = lax.iota(jnp.int32, key_len)
    same = segment[first : first + block_rows][:, None] == segment[:key_len][None, :]
    return same & (key_index[None, :] <= row_index[:, None])


def block_scores(q_block, keys, segment, first, block_rows, scale):
    key_len = first + block_rows
    scores = (
        jnp.einsum("qhd,kd->hqk", q_block, keys[:key_len], preferred_element_type=jnp.float32)
        * scale
    )
    return jnp.where(visible(segment, first, block_rows, key_len)[None], scores, NEG)


def attend_forward(queries, keys, values, segment, block_rows, scale):
    outputs = []
    totals = []
    for index in range(queries.shape[0] // block_rows):
        first = index * block_rows
        key_len = first + block_rows
        scores = block_scores(queries[first:key_len], keys, segment, first, block_rows, scale)
        top = jnp.max(scores, axis=-1, keepdims=True)
        expd = jnp.exp(scores - top)
        total = jnp.sum(expd, axis=-1, keepdims=True)
        probs = (expd / total).astype(jnp.bfloat16)
        outputs.append(
            jnp.einsum("hqk,kd->qhd", probs, values[:key_len], preferred_element_type=jnp.float32)
        )
        totals.append(top + jnp.log(total))
    return (jnp.concatenate(outputs, axis=0), totals)


def attend_backward(queries, keys, values, d_attended, segment, totals, block_rows, scale):
    pack_rows, heads_dev, head = queries.shape
    d_queries = []
    d_keys = jnp.zeros((pack_rows, head), jnp.float32)
    d_values = jnp.zeros((pack_rows, head), jnp.float32)
    for index in range(pack_rows // block_rows):
        first = index * block_rows
        key_len = first + block_rows
        q_block = queries[first:key_len]
        scores = block_scores(q_block, keys, segment, first, block_rows, scale)
        probs = jnp.exp(scores - totals[index])
        d_block = d_attended[first:key_len]
        d_probs = jnp.einsum(
            "qhd,kd->hqk", d_block, values[:key_len], preferred_element_type=jnp.float32
        )
        delta = jnp.sum(probs * d_probs, axis=-1, keepdims=True)
        d_scores = (probs * (d_probs - delta)).astype(jnp.bfloat16)
        d_values = d_values.at[:key_len].add(
            jnp.einsum(
                "hqk,qhd->kd",
                probs.astype(jnp.bfloat16),
                d_block,
                preferred_element_type=jnp.float32,
            )
        )
        d_queries.append(
            jnp.einsum("hqk,kd->qhd", d_scores, keys[:key_len], preferred_element_type=jnp.float32)
            * scale
        )
        d_keys = d_keys.at[:key_len].add(
            jnp.einsum("hqk,qhd->kd", d_scores, q_block, preferred_element_type=jnp.float32) * scale
        )
    return (jnp.concatenate(d_queries, axis=0), d_keys, d_values)


MESH = pl.DeviceIdType.MESH
ANY = pl.BlockSpec(memory_space=pl.ANY)
INVMEM = pl.BlockSpec(memory_space=pltpu.VMEM)


class Axis:
    def __init__(self, name, size):
        self.name, self.size, self.half = name, size, size // 2
        self.me = lax.axis_index(name)
        self.row, self.par = self.me // 2, self.me % 2
        self.pair = self.me + 1 - 2 * self.par

    def line(self, step):
        return lax.rem(self.row + step + self.half, self.half) * 2 + self.par

    def pair_line(self, step):
        return lax.rem(self.row + step + self.half, self.half) * 2 + 1 - self.par

    def greet(self, barrier):
        for step in range(1, self.size):
            peer = lax.rem(self.me + step, self.size)
            pl.semaphore_signal(barrier, inc=1, device_id={self.name: peer}, device_id_type=MESH)
        return self.size - 1


def remote(src, dst, send, recv, axis, peer):
    return pltpu.make_async_remote_copy(
        src_ref=src, dst_ref=dst, send_sem=send, recv_sem=recv, device_id={axis.name: peer}, device_id_type=MESH
    )


class Gather:
    def __init__(self, axis, src, dst, send, recv):
        self.axis, self.src, self.dst, self.send, self.recv = axis, src, dst, send, recv

    def own(self, index):
        peer = self.axis.pair if index == 0 else self.axis.line(index)
        return remote(self.src, self.dst.at[self.axis.me], self.send.at[index], self.recv.at[index], self.axis, peer)

    def forward(self, step):
        slot, index = self.dst.at[self.axis.line(-step)], self.axis.half + step
        return remote(slot, slot, self.send.at[index], self.recv.at[index], self.axis, self.axis.pair)

    def start_line(self):
        for step in range(1, self.axis.half):
            self.own(step).start()

    def start_pair(self):
        self.own(0).start()

    def pass_on(self):
        for step in range(1, self.axis.half):
            self.own(step).wait_recv()
            self.forward(step).start()

    def finish(self):
        self.own(0).wait_recv()
        for step in range(1, self.axis.half):
            self.forward(step).wait_recv()
        for step in range(self.axis.half):
            self.own(step).wait_send()
        for step in range(1, self.axis.half):
            self.forward(step).wait_send()


def gather_kernel(sizes, names, *refs):
    count = len(names)
    srcs, dsts = refs[:count], refs[count : 2 * count]
    sends, recvs = refs[2 * count : 3 * count], refs[3 * count : 4 * count]
    local = refs[4 * count]
    axes = {name: Axis(name, size) for name, size in sizes.items()}
    barrier = pltpu.get_barrier_semaphore()
    pl.semaphore_wait(barrier, sum(axis.greet(barrier) for axis in axes.values()))
    gathers = [Gather(axes[n], *four) for n, *four in zip(names, srcs, dsts, sends, recvs)]
    for gather in gathers:
        gather.start_line()
        gather.start_pair()
    copies = [
        pltpu.make_async_copy(g.src, g.dst.at[g.axis.me], local.at[i]) for i, g in enumerate(gathers)
    ]
    for copy in copies:
        copy.start()
    for gather in gathers:
        gather.pass_on()
    for gather in gathers:
        gather.finish()
    for copy in copies:
        copy.wait()


def gather_all(arrays, names, sizes):
    shapes = [jax.ShapeDtypeStruct((sizes[n],) + a.shape, a.dtype) for a, n in zip(arrays, names)]
    sems = [pltpu.SemaphoreType.DMA((sizes[n],)) for n in names]
    return pl.pallas_call(
        functools.partial(gather_kernel, sizes, names),
        out_shape=shapes,
        in_specs=[INVMEM] * len(arrays),
        out_specs=[ANY] * len(arrays),
        scratch_shapes=sems + sems + [pltpu.SemaphoreType.DMA((len(arrays),))],
        compiler_params=pltpu.CompilerParams(collective_id=0, has_side_effects=True),
        name="gather_inputs",
    )(*arrays)


class Reduce:
    def __init__(self, axis, part, out, held, summed, last, send, recv):
        self.axis, self.part, self.out = axis, part, out
        self.held, self.summed, self.last, self.send, self.recv = held, summed, last, send, recv

    def first(self, row):
        block = self.part.at[2 * row + 1 - self.axis.par]
        return remote(block, self.held.at[row], self.send.at[row], self.recv.at[row], self.axis, self.axis.pair)

    def second(self, step):
        row, index = lax.rem(self.axis.row + step, self.axis.half), self.axis.half + step
        return remote(
            self.summed.at[row], self.last.at[step - 1], self.send.at[index], self.recv.at[index],
            self.axis, self.axis.line(step),
        )

    def start(self):
        for row in range(self.axis.half):
            self.first(row).start()

    def add(self, row, target, own):
        rows = self.part.shape[1]
        chunk = 64 if rows % 64 == 0 and rows > 96 else rows

        @pl.loop(0, rows // chunk)
        def _(index):
            at = pl.ds(index * chunk, chunk)
            total = self.part[2 * row + self.axis.par, at].astype(jnp.float32) + self.held[row, at].astype(jnp.float32)
            if own:
                target[at] = total.astype(target.dtype)
            else:
                target[row, at] = total.astype(target.dtype)

    def middle(self):
        for row in range(self.axis.half):
            self.first(row).wait()
        for step in range(1, self.axis.half):
            self.add(lax.rem(self.axis.row + step, self.axis.half), self.summed, False)
            self.second(step).start()
        self.add(self.axis.row, self.out, True)

    def end(self):
        rows = self.part.shape[1]
        chunk = 64 if rows % 64 == 0 and rows > 96 else rows
        for step in range(1, self.axis.half):
            self.second(step).wait()

        @pl.loop(0, rows // chunk)
        def _(index):
            at = pl.ds(index * chunk, chunk)
            total = self.out[at]
            for step in range(1, self.axis.half):
                total = total + self.last[step - 1, at].astype(jnp.float32)
            self.out[at] = total


def reduce_kernel(sizes, names, shared, *refs):
    count, n_shared = len(names), len(shared)
    parts, refs = refs[:count], refs[count:]
    outs, refs = refs[:count], refs[count:]
    held, refs = refs[:count], refs[count:]
    summed, refs = refs[:count], refs[count:]
    last, refs = refs[:count], refs[count:]
    sends, refs = refs[:count], refs[count:]
    recvs, refs = refs[:count], refs[count:]
    slots, refs = refs[:n_shared], refs[n_shared:]
    s_sends, refs = refs[:n_shared], refs[n_shared:]
    s_recvs = refs[:n_shared]
    axes = {name: Axis(name, size) for name, size in sizes.items()}
    barrier = pltpu.get_barrier_semaphore()
    pl.semaphore_wait(barrier, sum(axis.greet(barrier) for axis in axes.values()))
    reduces = [
        Reduce(axes[n], *seven) for n, *seven in zip(names, parts, outs, held, summed, last, sends, recvs)
    ]
    for item in reduces:
        item.start()
    for item in reduces:
        item.middle()
    for item in reduces:
        item.end()
    axis = axes["tensor"]
    copies = []
    for i, k in enumerate(shared):
        slots[i][axis.me] = outs[k][...]
        for step in range(1, axis.size):
            peer = lax.rem(axis.me + step, axis.size)
            copies.append(
                remote(slots[i].at[axis.me], slots[i].at[axis.me], s_sends[i].at[step], s_recvs[i].at[step], axis, peer)
            )
            copies[-1].start()
    for copy in copies:
        copy.wait()
    for i, k in enumerate(shared):
        total = slots[i][0]
        for t in range(1, axis.size):
            total = total + slots[i][t]
        outs[k][...] = total


def reduce_all(arrays, names, shared, sizes):
    halves = [sizes[n] // 2 for n in names]
    tails = [a.shape[1:] for a in arrays]
    sems = [pltpu.SemaphoreType.DMA((sizes[n],)) for n in names]
    nt = sizes["tensor"]
    s_sems = [pltpu.SemaphoreType.DMA((nt,)) for _ in shared]
    return pl.pallas_call(
        functools.partial(reduce_kernel, sizes, names, shared),
        out_shape=[jax.ShapeDtypeStruct(tail, jnp.float32) for tail in tails],
        in_specs=[INVMEM] * len(arrays),
        out_specs=[INVMEM] * len(arrays),
        scratch_shapes=[pltpu.VMEM((h,) + tail, a.dtype) for h, tail, a in zip(halves, tails, arrays)] * 2
        + [pltpu.VMEM((h - 1,) + tail, a.dtype) for h, tail, a in zip(halves, tails, arrays)]
        + sems
        + sems
        + [pltpu.VMEM((nt,) + tails[k], jnp.float32) for k in shared]
        + s_sems
        + s_sems,
        compiler_params=pltpu.CompilerParams(
            collective_id=1, has_side_effects=True, vmem_limit_bytes=60 << 20
        ),
        name="reduce_outputs",
    )(*arrays)


def shards(
    tokens,
    cotangent,
    seq_lengths,
    w_query,
    w_keyvalue,
    w_out,
    w_up,
    w_down,
    norm1_gain,
    norm1_bias,
    norm2_gain,
    norm2_bias,
):
    own_rows = tokens.shape[0]
    pack_rows = own_rows * lax.axis_size("tensor")
    row_start = lax.axis_index("tensor") * own_rows
    segment, position, valid = slot_tables(seq_lengths, pack_rows)
    own_valid = lax.dynamic_slice_in_dim(valid, row_start, own_rows)
    sizes = {"dp": lax.axis_size("dp"), "tensor": lax.axis_size("tensor")}
    norms = jnp.stack([norm1_gain, norm1_bias, norm2_gain, norm2_bias], axis=1)
    pad = jnp.zeros((norms.shape[0], 124), norms.dtype)
    mixed_in = jnp.concatenate([w_keyvalue, norms, pad], axis=1)
    names = ("tensor", "dp", "dp", "dp", "dp", "dp", "tensor")
    gathered = gather_all((tokens, w_query, mixed_in, w_up, w_out, w_down, cotangent), names, sizes)
    gathered = [g.reshape((-1,) + g.shape[2:]) for g in gathered]
    all_tokens, wq_all, kvn_all, wup_all, wo_all, wdown_all, all_cot = gathered
    wkv_all = kvn_all[:, : w_keyvalue.shape[1]]
    vectors = kvn_all[:, w_keyvalue.shape[1] : w_keyvalue.shape[1] + 4].astype(jnp.float32)
    gain1, bias1, gain2, bias2 = (vectors[:, i] for i in range(4))
    token_f = tokens.astype(jnp.float32)
    scaled_all, inv_all = norm_stats(all_tokens.astype(jnp.float32))
    scaled_own = lax.dynamic_slice_in_dim(scaled_all, row_start, own_rows)
    inv_own = lax.dynamic_slice_in_dim(inv_all, row_start, own_rows)
    normed1 = (scaled_all * gain1 + bias1).astype(jnp.bfloat16)
    normed2 = (scaled_all * gain2 + bias2).astype(jnp.bfloat16)
    head = wkv_all.shape[1] // 2
    heads_dev = wq_all.shape[1] // head
    scale = head ** (-0.5)
    cosine, sine = rotary_tables(position, ROT)
    query_pre = jnp.dot(normed1, wq_all, preferred_element_type=jnp.float32)
    kv_pre = jnp.dot(normed1, wkv_all, preferred_element_type=jnp.float32)
    queries = rotate(query_pre.reshape(pack_rows, heads_dev, head), cosine, sine, ROT).astype(
        jnp.bfloat16
    )
    keys = rotate(kv_pre[:, None, :head], cosine, sine, ROT)[:, 0].astype(jnp.bfloat16)
    values = kv_pre[:, head:].astype(jnp.bfloat16)
    attended_f, totals = attend_forward(queries, keys, values, segment, BLOCK, scale)
    attended = attended_f.reshape(pack_rows, heads_dev * head).astype(jnp.bfloat16)
    up_pre = jnp.dot(normed2, wup_all, preferred_element_type=jnp.float32)
    hidden = jax.nn.gelu(up_pre, approximate=False).astype(jnp.bfloat16)
    partial_mixed = contract_cols(attended, wo_all) + contract_cols(hidden, wdown_all)
    grad_all = all_cot.astype(jnp.float32) * valid[:, None]
    grad_low = grad_all.astype(jnp.bfloat16)
    d_out_weight = contract_rows(grad_low, attended)
    d_down = contract_rows(grad_low, hidden)
    d_attended = jnp.dot(grad_low, wo_all, preferred_element_type=jnp.float32).astype(jnp.bfloat16)
    d_hidden = jnp.dot(grad_low, wdown_all, preferred_element_type=jnp.float32)
    slope = 0.5 * (1.0 + lax.erf(up_pre * (1.0 / math.sqrt(2.0)))) + up_pre * jnp.exp(
        -0.5 * up_pre * up_pre
    ) * (1.0 / math.sqrt(2.0 * math.pi))
    d_up_pre = (d_hidden * slope).astype(jnp.bfloat16)
    d_up = contract_rows(normed2, d_up_pre)
    d_queries, d_keys, d_values = attend_backward(
        queries,
        keys,
        values,
        d_attended.reshape(pack_rows, heads_dev, head),
        segment,
        totals,
        BLOCK,
        scale,
    )
    d_query_pre = (
        rotate_back(d_queries, cosine, sine, ROT)
        .reshape(pack_rows, heads_dev * head)
        .astype(jnp.bfloat16)
    )
    d_keys_pre = rotate_back(d_keys[:, None, :], cosine, sine, ROT)[:, 0]
    d_kv_pre = jnp.concatenate([d_keys_pre, d_values], axis=1).astype(jnp.bfloat16)
    d_query = contract_rows(normed1, d_query_pre)
    d_keyvalue = contract_rows(normed1, d_kv_pre)
    d_normed1 = contract_cols(d_query_pre, wq_all) + contract_cols(d_kv_pre, wkv_all)
    d_normed2 = contract_cols(d_up_pre, wup_all)
    own_grad = cotangent.astype(jnp.float32) * own_valid[:, None]
    d_scaled = d_normed1 * gain1 + d_normed2 * gain2
    d_norms = jnp.stack(
        [
            jnp.sum(d_normed1 * scaled_all, axis=0),
            jnp.sum(d_normed1, axis=0),
            jnp.sum(d_normed2 * scaled_all, axis=0),
            jnp.sum(d_normed2, axis=0),
        ]
    )
    nd, nt = sizes["dp"], sizes["tensor"]
    parts = [partial_mixed, d_scaled, d_out_weight, d_up, d_down, d_query, d_keyvalue]
    names = ("tensor", "tensor") + ("dp",) * 6
    parts = [p.astype(jnp.bfloat16).reshape(sizes[n], -1, p.shape[-1]) for p, n in zip(parts, names)]
    parts.append(jnp.swapaxes(d_norms.reshape(4, nd, -1), 0, 1))
    sums = reduce_all(parts, names, (6, 7), sizes)
    mixed, d_scaled_own = sums[:2]
    out_tokens = (token_f + mixed).astype(jnp.bfloat16)
    d_tokens = own_grad + norm_back(d_scaled_own, scaled_own, inv_own)
    return (out_tokens, d_tokens, sums[5], sums[6], sums[2], sums[3], sums[4]) + tuple(sums[7][i] for i in range(4))


def solution(mesh):
    return jax.shard_map(
        shards,
        mesh=mesh,
        in_specs=(
            P(("dp", "tensor"), None),
            P(("dp", "tensor"), None),
            P("dp", None),
            P("dp", "tensor"),
            P("dp", None),
            P("dp", "tensor"),
            P("dp", "tensor"),
            P("dp", "tensor"),
            P("dp"),
            P("dp"),
            P("dp"),
            P("dp"),
        ),
        out_specs=(
            P(("dp", "tensor"), None),
            P(("dp", "tensor"), None),
            P("dp", "tensor"),
            P("dp", None),
            P("dp", "tensor"),
            P("dp", "tensor"),
            P("dp", "tensor"),
            P("dp"),
            P("dp"),
            P("dp"),
            P("dp"),
        ),
        check_vma=False,
    )
```

```python
import functools
import math

import jax
import jax.numpy as jnp
from jax import lax
from jax.experimental import pallas as pl
from jax.experimental.pallas import tpu as pltpu
from jax.sharding import PartitionSpec as P

ROT = 16
SEQ_LEAST = 1024
SEQ_MOST = 1792
BLOCK = 256
EPS = 1e-05
NEG = -1e30
F32 = jnp.float32
BF16 = jnp.bfloat16


def dot(left, right):
    return jnp.dot(left, right, preferred_element_type=F32)


def dot_rows(left, right):
    return lax.dot_general(left, right, (((0,), (0,)), ((), ())), preferred_element_type=F32)


def dot_cols(left, right):
    return lax.dot_general(left, right, (((1,), (1,)), ((), ())), preferred_element_type=F32)


def lanes_of(rows):
    return lax.broadcasted_iota(jnp.int32, (rows, 128), 1)


def swap_halves(x, lane):
    return jnp.where(lane < ROT // 2, pltpu.roll(x, 128 - ROT // 2, 1), pltpu.roll(x, ROT // 2, 1))


def three_parts(x):
    high = x.astype(BF16).astype(F32)
    middle = (x - high).astype(BF16).astype(F32)
    return high, middle, x - high - middle


def unit_heads(wide, heads):
    pieces = []
    for h in range(heads):
        piece = wide[:, h // 2 * 128 : h // 2 * 128 + 128]
        pieces.append(piece if h % 2 == 0 else pltpu.roll(piece, 64, 1))
    return pieces


def join_heads(pieces, lane):
    wide = []
    for h in range(0, len(pieces), 2):
        second = pltpu.roll(pieces[h + 1], 64, 1) if h + 1 < len(pieces) else jnp.zeros_like(pieces[h])
        wide.append(jnp.where(lane < 64, pieces[h], second))
    return jnp.concatenate(wide, axis=1)


class Core:
    def __init__(self, heads, length, **refs):
        self.heads, self.length = heads, length
        self.__dict__.update(refs)

    def past(self, first, shape, axis):
        return lax.broadcasted_iota(jnp.int32, shape, axis) + first >= self.length

    def tables(self):
        rows = self.cosine.shape[0]

        @pl.loop(0, rows // BLOCK)
        def _(index):
            at = pl.ds(pl.multiple_of(index * BLOCK, BLOCK), BLOCK)
            lane = lanes_of(BLOCK)
            row = lax.broadcasted_iota(jnp.int32, (BLOCK, 128), 0) + index * BLOCK
            position = jnp.where(row >= self.length, row - self.length, row).astype(F32)
            exponent = jnp.where(lane < ROT // 2, lane, lane - ROT // 2).astype(F32) * (-2.0 / ROT)
            angle = position * jnp.exp(exponent * math.log(10000.0))
            sine = jnp.sin(angle)
            self.cosine[at] = jnp.where(lane < ROT, jnp.cos(angle), 1.0)
            self.sine[at] = jnp.where(lane < ROT // 2, -sine, jnp.where(lane < ROT, sine, 0.0))

    def unpack_params(self):
        start = self.heads * 64
        turned = self.w_query[:, start // 128 * 128 : start // 128 * 128 + 128].T.astype(F32)
        self.params[0:4] = turned[start % 128 : start % 128 + 4]

    def normalize(self, block):
        at = pl.ds(pl.multiple_of(block * BLOCK, BLOCK), BLOCK)
        x = self.tokens[at].astype(F32)
        centered = x - jnp.mean(x, axis=1, keepdims=True)
        scaled = centered * lax.rsqrt(jnp.mean(centered * centered, axis=1, keepdims=True) + EPS)
        gain1, bias1, gain2, bias2 = (self.params[i : i + 1] for i in range(4))
        self.scaled[at] = scaled.astype(BF16)
        self.normed1[at] = (scaled * gain1 + bias1).astype(BF16)
        self.normed2[at] = (scaled * gain2 + bias2).astype(BF16)

    def project(self, block):
        first = pl.multiple_of(block * BLOCK, BLOCK)
        at = pl.ds(first, BLOCK)
        lane = lanes_of(BLOCK)
        cosine, sine = self.cosine[at], self.sine[at]
        past = self.past(first, (BLOCK, 128), 0)
        normed = self.normed1[at]
        key_value = dot(normed, self.w_keyvalue[...])
        keys = key_value * cosine + swap_halves(key_value, lane) * sine
        hidden_key = jnp.where(past, 0.0, NEG)
        extra = jnp.where(lane == 64, hidden_key, jnp.where(lane < 68, -1.0, 0.0))
        self.keys[at] = jnp.where(lane < 64, keys, extra).astype(BF16)
        ones = jnp.where(lane < 67, 1.0, 0.0)
        self.values[at] = jnp.where(lane < 64, pltpu.roll(key_value, 64, 1), ones).astype(BF16)
        query = dot(normed, self.w_query[...])
        flag = jnp.where((lane == 64) & past, 1.0, 0.0)
        for h, piece in enumerate(unit_heads(query, self.heads)):
            turned = (piece * cosine + swap_halves(piece, lane) * sine).astype(BF16).astype(F32)
            turned = turned * (64 ** (-0.5))
            self.queries[block, h * BLOCK : (h + 1) * BLOCK] = jnp.where(lane < 64, turned, flag).astype(BF16)

    def key_blocks(self, block):
        first = SEQ_LEAST // BLOCK if block * BLOCK >= SEQ_MOST else 0
        return range(first, block + 1)

    def attend(self, block):
        rows = self.heads * BLOCK
        query = self.queries[block]
        lane = lanes_of(rows)
        top = jnp.full((rows, BLOCK), -3e38, F32)
        for j in self.key_blocks(block):
            span = slice(j * BLOCK, (j + 1) * BLOCK)
            scores = dot_cols(query, self.keys[span])
            if j == block:
                row = lax.rem(lax.broadcasted_iota(jnp.int32, (rows, BLOCK), 0), BLOCK)
                column = lax.broadcasted_iota(jnp.int32, (rows, BLOCK), 1)
                scores = jnp.where(column <= row, scores, NEG)
            self.scores[:, span] = scores
            top = jnp.maximum(top, scores)
        top = jnp.max(top, axis=1, keepdims=True)
        total = jnp.zeros((rows, 128), F32)
        for j in self.key_blocks(block):
            span = slice(j * BLOCK, (j + 1) * BLOCK)
            probs = jnp.exp(self.scores[:, span] - top).astype(BF16)
            total = total + dot(probs, self.values[span])
        weight = jnp.sum(jnp.where(lane == 64, total, 0.0), axis=1, keepdims=True)
        output = total / weight
        pieces = [output[h * BLOCK : (h + 1) * BLOCK] for h in range(self.heads)]
        self.attended[block * BLOCK : (block + 1) * BLOCK] = join_heads(pieces, lanes_of(BLOCK)).astype(BF16)
        high, middle, low = three_parts(top + jnp.log(weight))
        parts = jnp.where(lane == 65, high, jnp.where(lane == 66, middle, low))
        self.queries[block] = jnp.where((lane >= 65) & (lane < 68), parts, query.astype(F32)).astype(BF16)

    def feed(self, at):
        up = dot(self.normed2[at], self.w_up[...])
        normal = 0.5 * (1.0 + lax.erf(up * (1.0 / math.sqrt(2.0))))
        self.hidden[at] = (up * normal).astype(BF16)
        density = jnp.exp(-0.5 * up * up) * (1.0 / math.sqrt(2.0 * math.pi))
        self.slope[at] = (normal + up * density).astype(BF16)

    def mix(self, at):
        return dot_cols(self.attended[at], self.w_out[...]) + dot_cols(self.hidden[at], self.w_down[...])

    def feed_back(self, at, first, rows):
        past = self.past(first, (rows, 1), 0)
        grad = jnp.where(past, 0.0, self.cotangent[at].astype(F32)).astype(BF16)
        self.grad[at] = grad
        d_hidden = dot(grad, self.w_down[...])
        self.slope[at] = (d_hidden * self.slope[at].astype(F32)).astype(BF16)

    def attend_grad(self, block):
        first = pl.multiple_of(block * BLOCK, BLOCK)
        at = pl.ds(first, BLOCK)
        lane = lanes_of(BLOCK)
        grads = unit_heads(dot(self.grad[at], self.w_out[...]), self.heads)
        outputs = unit_heads(self.attended[at].astype(F32), self.heads)
        for h in range(self.heads):
            grad = grads[h].astype(BF16).astype(F32)
            delta = jnp.sum(jnp.where(lane < 64, grad * outputs[h], 0.0), axis=1, keepdims=True)
            high, middle, low = three_parts(-delta)
            parts = jnp.where(lane == 64, high, jnp.where(lane == 65, middle, jnp.where(lane == 66, low, 0.0)))
            self.d_attended[block, h * BLOCK : (h + 1) * BLOCK] = jnp.where(lane < 64, grad, parts).astype(BF16)

    def attend_back(self, block):
        rows = self.heads * BLOCK
        query, grad = self.queries[block], self.d_attended[block]
        total = jnp.zeros((rows, 128), F32)
        for j in self.key_blocks(block):
            span = slice(j * BLOCK, (j + 1) * BLOCK)
            keys, values = self.keys[span], self.values[span]
            scores, d_probs = dot_cols(keys, query), dot_cols(values, grad)
            if j == block:
                key = lax.broadcasted_iota(jnp.int32, (BLOCK, rows), 0)
                row = lax.rem(lax.broadcasted_iota(jnp.int32, (BLOCK, rows), 1), BLOCK)
                scores = jnp.where(key <= row, scores, NEG)
            probs = jnp.exp(scores)
            d_scores = (probs * d_probs).astype(BF16)
            self.d_values[span] += dot(probs.astype(BF16), grad)
            self.d_keys[span] += dot(d_scores, query)
            total = total + dot_rows(d_scores, keys)
        at = slice(block * BLOCK, (block + 1) * BLOCK)
        lane = lanes_of(BLOCK)
        cosine, sine = self.cosine[at], self.sine[at]

        def turn_back(x):
            return x * cosine - swap_halves(x, lane) * sine

        pieces = [turn_back(total[h * BLOCK : (h + 1) * BLOCK]) * (64 ** (-0.5)) for h in range(self.heads)]
        self.d_query[at] = join_heads(pieces, lane).astype(BF16)
        self.d_keyvalue[at] = jnp.where(
            lane < 64, turn_back(self.d_keys[at]), pltpu.roll(self.d_values[at], 64, 1)
        ).astype(BF16)

    def input_grad(self, block):
        at = slice(block * BLOCK, (block + 1) * BLOCK)
        d_normed1 = dot_cols(self.d_query[at], self.w_query[...]) + dot_cols(self.d_keyvalue[at], self.w_keyvalue[...])
        d_normed2 = dot_cols(self.slope[at], self.w_up[...])
        scaled = self.scaled[at].astype(F32)
        for i, value in enumerate((d_normed1 * scaled, d_normed1, d_normed2 * scaled, d_normed2)):
            self.d_norms[i] += jnp.sum(value.reshape(BLOCK // 8, 8, -1), axis=0)
        return d_normed1 * self.params[0:1] + d_normed2 * self.params[2:3]


MESH = pl.DeviceIdType.MESH
ANY = pl.BlockSpec(memory_space=pl.ANY)
INVMEM = pl.BlockSpec(memory_space=pltpu.VMEM)


class Axis:
    def __init__(self, name, size):
        self.name, self.size, self.half = name, size, size // 2
        self.me = lax.axis_index(name)
        self.row, self.par = self.me // 2, self.me % 2
        self.pair = self.me + 1 - 2 * self.par

    def line(self, step):
        return lax.rem(self.row + step + self.half, self.half) * 2 + self.par

    def pair_line(self, step):
        return lax.rem(self.row + step + self.half, self.half) * 2 + 1 - self.par

    def greet(self, barrier):
        for step in range(1, self.size):
            peer = lax.rem(self.me + step, self.size)
            pl.semaphore_signal(barrier, inc=1, device_id={self.name: peer}, device_id_type=MESH)
        return self.size - 1


def remote(src, dst, send, recv, axis, peer):
    return pltpu.make_async_remote_copy(
        src_ref=src, dst_ref=dst, send_sem=send, recv_sem=recv, device_id={axis.name: peer}, device_id_type=MESH
    )


class Gather:
    def __init__(self, axis, src, dst, send, recv):
        self.axis, self.src, self.dst, self.send, self.recv = axis, src, dst, send, recv

    def own(self, index):
        peer = self.axis.pair if index == 0 else self.axis.line(index)
        return remote(self.src, self.dst.at[self.axis.me], self.send.at[index], self.recv.at[index], self.axis, peer)

    def forward(self, step):
        slot, index = self.dst.at[self.axis.line(-step)], self.axis.half + step
        return remote(slot, slot, self.send.at[index], self.recv.at[index], self.axis, self.axis.pair)

    def start_line(self):
        for step in range(1, self.axis.half):
            self.own(step).start()

    def start_pair(self):
        self.own(0).start()

    def pass_on(self):
        for step in range(1, self.axis.half):
            self.own(step).wait_recv()
            self.forward(step).start()

    def finish(self):
        self.own(0).wait_recv()
        for step in range(1, self.axis.half):
            self.forward(step).wait_recv()
        for step in range(self.axis.half):
            self.own(step).wait_send()
        for step in range(1, self.axis.half):
            self.forward(step).wait_send()


def gather_kernel(sizes, names, *refs):
    count = len(names)
    srcs, dsts = refs[:count], refs[count : 2 * count]
    sends, recvs = refs[2 * count : 3 * count], refs[3 * count : 4 * count]
    local = refs[4 * count]
    axes = {name: Axis(name, size) for name, size in sizes.items()}
    barrier = pltpu.get_barrier_semaphore()
    pl.semaphore_wait(barrier, sum(axis.greet(barrier) for axis in axes.values()))
    gathers = [Gather(axes[n], *four) for n, *four in zip(names, srcs, dsts, sends, recvs)]
    for gather in gathers:
        gather.start_line()
        gather.start_pair()
    copies = [
        pltpu.make_async_copy(g.src, g.dst.at[g.axis.me], local.at[i]) for i, g in enumerate(gathers)
    ]
    for copy in copies:
        copy.start()
    for gather in gathers[2:] + gathers[:2]:
        gather.pass_on()
    for gather in gathers:
        gather.finish()
    for copy in copies:
        copy.wait()


def gather_all(arrays, names, sizes):
    shapes = [jax.ShapeDtypeStruct((sizes[n],) + a.shape, a.dtype) for a, n in zip(arrays, names)]
    sems = [pltpu.SemaphoreType.DMA((sizes[n],)) for n in names]
    return pl.pallas_call(
        functools.partial(gather_kernel, sizes, names),
        out_shape=shapes,
        in_specs=[INVMEM] * len(arrays),
        out_specs=[ANY] * len(arrays),
        scratch_shapes=sems + sems + [pltpu.SemaphoreType.DMA((len(arrays),))],
        compiler_params=pltpu.CompilerParams(collective_id=0, has_side_effects=True),
        name="gather_inputs",
    )(*arrays)


class Reduce:
    def __init__(self, axis, part, out, held, summed, last, send, recv):
        self.axis, self.part, self.out = axis, part, out
        self.held, self.summed, self.last, self.send, self.recv = held, summed, last, send, recv

    def first(self, row):
        block = self.part.at[2 * row + 1 - self.axis.par]
        return remote(block, self.held.at[row], self.send.at[row], self.recv.at[row], self.axis, self.axis.pair)

    def second(self, step):
        row, index = lax.rem(self.axis.row + step, self.axis.half), self.axis.half + step
        return remote(
            self.summed.at[row], self.last.at[step - 1], self.send.at[index], self.recv.at[index],
            self.axis, self.axis.line(step),
        )

    def start(self):
        for row in range(self.axis.half):
            self.first(row).start()

    def add(self, row, target, own):
        rows = self.part.shape[1]
        chunk = 64 if rows % 64 == 0 and rows > 96 else rows

        @pl.loop(0, rows // chunk)
        def _(index):
            at = pl.ds(index * chunk, chunk)
            total = self.part[2 * row + self.axis.par, at].astype(jnp.float32) + self.held[row, at].astype(jnp.float32)
            if own:
                target[at] = total.astype(target.dtype)
            else:
                target[row, at] = total.astype(target.dtype)

    def middle(self):
        for row in range(self.axis.half):
            self.first(row).wait()
        for step in range(1, self.axis.half):
            self.add(lax.rem(self.axis.row + step, self.axis.half), self.summed, False)
            self.second(step).start()
        self.add(self.axis.row, self.out, True)

    def end(self):
        rows = self.part.shape[1]
        chunk = 64 if rows % 64 == 0 and rows > 96 else rows
        for step in range(1, self.axis.half):
            self.second(step).wait()

        @pl.loop(0, rows // chunk)
        def _(index):
            at = pl.ds(index * chunk, chunk)
            total = self.out[at]
            for step in range(1, self.axis.half):
                total = total + self.last[step - 1, at].astype(jnp.float32)
            self.out[at] = total


def reduce_kernel(sizes, names, shared, *refs):
    count, n_shared = len(names), len(shared)
    parts, refs = refs[:count], refs[count:]
    outs, refs = refs[:count], refs[count:]
    held, refs = refs[:count], refs[count:]
    summed, refs = refs[:count], refs[count:]
    last, refs = refs[:count], refs[count:]
    sends, refs = refs[:count], refs[count:]
    recvs, refs = refs[:count], refs[count:]
    slots, refs = refs[:n_shared], refs[n_shared:]
    s_sends, refs = refs[:n_shared], refs[n_shared:]
    s_recvs = refs[:n_shared]
    axes = {name: Axis(name, size) for name, size in sizes.items()}
    barrier = pltpu.get_barrier_semaphore()
    pl.semaphore_wait(barrier, sum(axis.greet(barrier) for axis in axes.values()))
    reduces = [
        Reduce(axes[n], *seven) for n, *seven in zip(names, parts, outs, held, summed, last, sends, recvs)
    ]
    for item in reduces:
        item.start()
    for item in reduces:
        item.middle()
    for item in reduces:
        item.end()
    axis = axes["tensor"]
    copies = []
    for i, k in enumerate(shared):
        slots[i][axis.me] = outs[k][...]
        for step in range(1, axis.size):
            peer = lax.rem(axis.me + step, axis.size)
            copies.append(
                remote(slots[i].at[axis.me], slots[i].at[axis.me], s_sends[i].at[step], s_recvs[i].at[step], axis, peer)
            )
            copies[-1].start()
    for copy in copies:
        copy.wait()
    for i, k in enumerate(shared):
        total = slots[i][0]
        for t in range(1, axis.size):
            total = total + slots[i][t]
        outs[k][...] = total


def reduce_all(arrays, names, shared, sizes):
    halves = [sizes[n] // 2 for n in names]
    tails = [a.shape[1:] for a in arrays]
    sems = [pltpu.SemaphoreType.DMA((sizes[n],)) for n in names]
    nt = sizes["tensor"]
    s_sems = [pltpu.SemaphoreType.DMA((nt,)) for _ in shared]
    return pl.pallas_call(
        functools.partial(reduce_kernel, sizes, names, shared),
        out_shape=[jax.ShapeDtypeStruct(tail, jnp.float32) for tail in tails],
        in_specs=[INVMEM] * len(arrays),
        out_specs=[INVMEM] * len(arrays),
        scratch_shapes=[pltpu.VMEM((h,) + tail, a.dtype) for h, tail, a in zip(halves, tails, arrays)] * 2
        + [pltpu.VMEM((h - 1,) + tail, a.dtype) for h, tail, a in zip(halves, tails, arrays)]
        + sems
        + sems
        + [pltpu.VMEM((nt,) + tails[k], jnp.float32) for k in shared]
        + s_sems
        + s_sems,
        compiler_params=pltpu.CompilerParams(
            collective_id=1, has_side_effects=True, vmem_limit_bytes=60 << 20
        ),
        name="reduce_outputs",
    )(*arrays)


SCRATCH = {
    "grad": ("rows", "model", BF16), "params": (8, "model", F32), "cosine": ("rows", 128, F32), "sine": ("rows", 128, F32),
    "scaled": ("rows", "model", BF16), "normed1": ("rows", "model", BF16), "normed2": ("rows", "model", BF16),
    "queries": ("blocks", "stack", 128, BF16), "keys": ("rows", 128, BF16), "values": ("rows", 128, BF16),
    "scores": ("stack", "rows", F32), "attended": ("rows", "wide", BF16), "hidden": ("rows", "units", BF16),
    "slope": ("rows", "units", BF16), "d_attended": ("blocks", "stack", 128, BF16), "d_query": ("rows", "wide", BF16),
    "d_keyvalue": ("rows", 128, BF16), "d_keys": ("rows", 128, F32), "d_values": ("rows", 128, F32),
    "d_norms": (4, 8, "model", F32),
}
INPUTS = ("tokens", "cotangent", "w_query", "w_keyvalue", "w_up", "w_down", "w_out")


def core_kernel(heads, seq, *refs):
    named = dict(zip(INPUTS, refs))
    mixed, scaled_grad, g_query, g_keyvalue, g_out, g_up, g_down, g_norms = refs[len(INPUTS) : len(INPUTS) + 8]
    named.update(zip(SCRATCH, refs[len(INPUTS) + 8 :]))
    core = Core(heads, seq[0, 0], **named)
    rows, model = core.tokens.shape
    used = SEQ_MOST
    core.tables()
    core.unpack_params()

    @pl.loop(0, rows // BLOCK)
    def _(block):
        core.normalize(block)
        core.project(block)

    for block in range(rows // BLOCK):
        core.attend(block)

    @pl.loop(0, rows // 512)
    def _(index):
        at = pl.ds(pl.multiple_of(index * 512, 512), 512)
        core.feed(at)
        mixed[at] = core.mix(at).astype(BF16)

    @pl.loop(0, 4)
    def _(index):
        first = pl.multiple_of(index * (used // 4), used // 4)
        core.feed_back(pl.ds(first, used // 4), first, used // 4)

    @pl.loop(0, used // BLOCK)
    def _(block):
        core.attend_grad(block)

    @pl.loop(0, model // BLOCK)
    def _(index):
        at = pl.ds(pl.multiple_of(index * BLOCK, BLOCK), BLOCK)
        grad = core.grad[:used, at]
        g_down[at] = dot_rows(grad, core.hidden[:used]).astype(BF16)
        g_out[at] = dot_rows(grad, core.attended[:used]).astype(BF16)
        g_up[at] = dot_rows(core.normed2[:used, at], core.slope[:used]).astype(BF16)

    for ref in (core.d_keys, core.d_values, core.d_norms):
        ref[...] = jnp.zeros_like(ref)
    for block in range(used // BLOCK - 1, -1, -1):
        core.attend_back(block)
        scaled_grad[block * BLOCK : (block + 1) * BLOCK] = core.input_grad(block).astype(BF16)
    scaled_grad[used:] = jnp.zeros((rows - used, model), BF16)

    @pl.loop(0, model // BLOCK)
    def _(index):
        at = pl.ds(pl.multiple_of(index * BLOCK, BLOCK), BLOCK)
        normed = core.normed1[:used, at]
        g_query[at] = dot_rows(normed, core.d_query[:used]).astype(BF16)
        g_keyvalue[at] = dot_rows(normed, core.d_keyvalue[:used]).astype(BF16)

    for i in range(4):
        g_norms[i : i + 1] = jnp.sum(core.d_norms[i], axis=0, keepdims=True)


def run_core(seq_lengths, arrays):
    tokens, _, w_query, w_keyvalue, w_up, _, w_out = arrays
    rows, model = tokens.shape
    heads, wide, units = w_out.shape[1] // 64, w_query.shape[1], w_up.shape[1]
    heads = (w_query.shape[1] - 4) // 64
    sizes = {
        "rows": rows, "model": model, "blocks": rows // BLOCK, "stack": heads * BLOCK, "wide": wide, "units": units,
    }
    shape = jax.ShapeDtypeStruct
    return pl.pallas_call(
        functools.partial(core_kernel, heads),
        out_shape=[shape((rows, model), BF16)] * 2
        + [shape((model, n), BF16) for n in (wide, 128, wide, units, units)]
        + [shape((4, model), F32)],
        in_specs=[pl.BlockSpec(memory_space=pltpu.SMEM)] + [INVMEM] * len(arrays),
        out_specs=[INVMEM] * 8,
        scratch_shapes=[
            pltpu.VMEM(tuple(sizes.get(n, n) for n in entry[:-1]), entry[-1]) for entry in SCRATCH.values()
        ],
        compiler_params=pltpu.CompilerParams(vmem_limit_bytes=67043328),
        name="layer",
    )(seq_lengths, *arrays)


def shards(
    tokens,
    cotangent,
    seq_lengths,
    w_query,
    w_keyvalue,
    w_out,
    w_up,
    w_down,
    norm1_gain,
    norm1_bias,
    norm2_gain,
    norm2_bias,
):
    sizes = {"dp": lax.axis_size("dp"), "tensor": lax.axis_size("tensor")}
    width = w_query.shape[1]
    wide = (width + 4 + 127) // 128 * 128
    norms = jnp.stack([norm1_gain, norm1_bias, norm2_gain, norm2_bias], axis=1)
    query_in = jnp.concatenate([w_query, jnp.pad(norms, ((0, 0), (0, wide - width - 4)))], axis=1)
    out_in = jnp.pad(w_out, ((0, 0), (0, wide - width)))
    names = ("tensor", "tensor", "dp", "dp", "dp", "dp", "dp")
    gathered = gather_all((tokens, cotangent, query_in, w_keyvalue, w_up, w_down, out_in), names, sizes)
    gathered = [g.reshape((-1,) + g.shape[2:]) for g in gathered]
    results = run_core(seq_lengths, gathered)
    nd = sizes["dp"]
    names = ("tensor", "tensor") + ("dp",) * 6
    parts = [p.reshape(sizes[n], -1, p.shape[-1]) for p, n in zip(results[:7], names)]
    parts.append(jnp.swapaxes(results[7].reshape(4, nd, -1), 0, 1))
    mixed, d_scaled, d_query, d_keyvalue, d_out, d_up, d_down, d_norms = reduce_all(parts, names, (3, 7), sizes)
    token_f = tokens.astype(F32)
    out_tokens = (token_f + mixed).astype(BF16)
    centered = token_f - jnp.mean(token_f, axis=-1, keepdims=True)
    inv_std = lax.rsqrt(jnp.mean(centered * centered, axis=-1, keepdims=True) + EPS)
    scaled = centered * inv_std
    row = lax.axis_index("tensor") * tokens.shape[0] + lax.iota(jnp.int32, tokens.shape[0])
    own_grad = jnp.where((row < seq_lengths[0, 0])[:, None], cotangent.astype(F32), 0.0)
    d_tokens = own_grad + inv_std * (
        d_scaled
        - jnp.mean(d_scaled, axis=-1, keepdims=True)
        - scaled * jnp.mean(d_scaled * scaled, axis=-1, keepdims=True)
    )
    return (out_tokens, d_tokens, d_query[:, :width], d_keyvalue, d_out[:, :width], d_up, d_down) + tuple(
        d_norms[i] for i in range(4)
    )


def solution(mesh):
    return jax.shard_map(
        shards,
        mesh=mesh,
        in_specs=(
            P(("dp", "tensor"), None),
            P(("dp", "tensor"), None),
            P("dp", None),
            P("dp", "tensor"),
            P("dp", None),
            P("dp", "tensor"),
            P("dp", "tensor"),
            P("dp", "tensor"),
            P("dp"),
            P("dp"),
            P("dp"),
            P("dp"),
        ),
        out_specs=(
            P(("dp", "tensor"), None),
            P(("dp", "tensor"), None),
            P("dp", "tensor"),
            P("dp", None),
            P("dp", "tensor"),
            P("dp", "tensor"),
            P("dp", "tensor"),
            P("dp"),
            P("dp"),
            P("dp"),
            P("dp"),
        ),
        check_vma=False,
    )
```

```python
import functools
import math
import types

import jax
import jax.numpy as jnp
from jax import lax
from jax.experimental import pallas as pl
from jax.experimental.pallas import tpu as pltpu
from jax.sharding import PartitionSpec as P

ROT = 16
SEQ_LEAST = 1024
SEQ_MOST = 1792
BLOCK = 256
EPS = 1e-05
NEG = -1e30
F32 = jnp.float32
BF16 = jnp.bfloat16


def dot(left, right):
    return jnp.dot(left, right, preferred_element_type=F32)


def dot_rows(left, right):
    return lax.dot_general(left, right, (((0,), (0,)), ((), ())), preferred_element_type=F32)


def dot_cols(left, right):
    return lax.dot_general(left, right, (((1,), (1,)), ((), ())), preferred_element_type=F32)


def lanes_of(rows):
    return lax.broadcasted_iota(jnp.int32, (rows, 128), 1)


def swap_halves(x, lane):
    return jnp.where(lane < ROT // 2, pltpu.roll(x, 128 - ROT // 2, 1), pltpu.roll(x, ROT // 2, 1))


def three_parts(x):
    high = x.astype(BF16).astype(F32)
    middle = (x - high).astype(BF16).astype(F32)
    return high, middle, x - high - middle


def unit_heads(wide, heads):
    pieces = []
    for h in range(heads):
        piece = wide[:, h // 2 * 128 : h // 2 * 128 + 128]
        pieces.append(piece if h % 2 == 0 else pltpu.roll(piece, 64, 1))
    return pieces


def join_heads(pieces, lane):
    wide = []
    for h in range(0, len(pieces), 2):
        second = pltpu.roll(pieces[h + 1], 64, 1) if h + 1 < len(pieces) else jnp.zeros_like(pieces[h])
        wide.append(jnp.where(lane < 64, pieces[h], second))
    return jnp.concatenate(wide, axis=1)


class Core:
    def __init__(self, heads, length, **refs):
        self.heads, self.length = heads, length
        self.__dict__.update(refs)

    def past(self, first, shape, axis):
        return lax.broadcasted_iota(jnp.int32, shape, axis) + first >= self.length

    def tables(self):
        rows = self.cosine.shape[0]

        @pl.loop(0, rows // BLOCK)
        def _(index):
            at = pl.ds(pl.multiple_of(index * BLOCK, BLOCK), BLOCK)
            lane = lanes_of(BLOCK)
            row = lax.broadcasted_iota(jnp.int32, (BLOCK, 128), 0) + index * BLOCK
            position = jnp.where(row >= self.length, row - self.length, row).astype(F32)
            exponent = jnp.where(lane < ROT // 2, lane, lane - ROT // 2).astype(F32) * (-2.0 / ROT)
            angle = position * jnp.exp(exponent * math.log(10000.0))
            sine = jnp.sin(angle)
            self.cosine[at] = jnp.where(lane < ROT, jnp.cos(angle), 1.0)
            self.sine[at] = jnp.where(lane < ROT // 2, -sine, jnp.where(lane < ROT, sine, 0.0))

    def unpack_params(self):
        start = self.heads * 64
        turned = self.w_query[:, start // 128 * 128 : start // 128 * 128 + 128].T.astype(F32)
        self.params[0:4] = turned[start % 128 : start % 128 + 4]

    def normalize(self, block):
        at = pl.ds(pl.multiple_of(block * BLOCK, BLOCK), BLOCK)
        x = self.tokens[at].astype(F32)
        centered = x - jnp.mean(x, axis=1, keepdims=True)
        scaled = centered * lax.rsqrt(jnp.mean(centered * centered, axis=1, keepdims=True) + EPS)
        gain1, bias1, gain2, bias2 = (self.params[i : i + 1] for i in range(4))
        self.scaled[at] = scaled.astype(BF16)
        self.normed1[at] = (scaled * gain1 + bias1).astype(BF16)
        self.normed2[at] = (scaled * gain2 + bias2).astype(BF16)

    def project(self, block):
        first = pl.multiple_of(block * BLOCK, BLOCK)
        at = pl.ds(first, BLOCK)
        lane = lanes_of(BLOCK)
        cosine, sine = self.cosine[at], self.sine[at]
        past = self.past(first, (BLOCK, 128), 0)
        normed = self.normed1[at]
        key_value = dot(normed, self.w_keyvalue[...])
        keys = key_value * cosine + swap_halves(key_value, lane) * sine
        hidden_key = jnp.where(past, 0.0, NEG)
        extra = jnp.where(lane == 64, hidden_key, jnp.where(lane < 68, -1.0, 0.0))
        self.keys[at] = jnp.where(lane < 64, keys, extra).astype(BF16)
        ones = jnp.where(lane < 67, 1.0, 0.0)
        self.values[at] = jnp.where(lane < 64, pltpu.roll(key_value, 64, 1), ones).astype(BF16)
        query = dot(normed, self.w_query[...])
        flag = jnp.where((lane == 64) & past, 1.0, 0.0)
        for h, piece in enumerate(unit_heads(query, self.heads)):
            turned = (piece * cosine + swap_halves(piece, lane) * sine).astype(BF16).astype(F32)
            turned = turned * (64 ** (-0.5))
            self.queries[block, h * BLOCK : (h + 1) * BLOCK] = jnp.where(lane < 64, turned, flag).astype(BF16)

    def key_blocks(self, block):
        first = SEQ_LEAST // BLOCK if block * BLOCK >= SEQ_MOST else 0
        return range(first, block + 1)

    def attend(self, block):
        rows = self.heads * BLOCK
        query = self.queries[block]
        lane = lanes_of(rows)
        top = jnp.full((rows, BLOCK), -3e38, F32)
        for index, j in enumerate(self.key_blocks(block)):
            scores = dot_cols(query, self.keys[j * BLOCK : (j + 1) * BLOCK])
            if j == block:
                row = lax.rem(lax.broadcasted_iota(jnp.int32, (rows, BLOCK), 0), BLOCK)
                column = lax.broadcasted_iota(jnp.int32, (rows, BLOCK), 1)
                scores = jnp.where(column <= row, scores, NEG)
            self.scores[:, index * BLOCK : (index + 1) * BLOCK] = scores
            top = jnp.maximum(top, scores)
        top = jnp.max(top, axis=1, keepdims=True)
        total = jnp.zeros((rows, 128), F32)
        for index, j in enumerate(self.key_blocks(block)):
            probs = jnp.exp(self.scores[:, index * BLOCK : (index + 1) * BLOCK] - top).astype(BF16)
            total = total + dot(probs, self.values[j * BLOCK : (j + 1) * BLOCK])
        weight = jnp.sum(jnp.where(lane == 64, total, 0.0), axis=1, keepdims=True)
        output = total / weight
        pieces = [output[h * BLOCK : (h + 1) * BLOCK] for h in range(self.heads)]
        self.attended[block * BLOCK : (block + 1) * BLOCK] = join_heads(pieces, lanes_of(BLOCK)).astype(BF16)
        high, middle, low = three_parts(top + jnp.log(weight))
        parts = jnp.where(lane == 65, high, jnp.where(lane == 66, middle, low))
        self.queries[block] = jnp.where((lane >= 65) & (lane < 68), parts, query.astype(F32)).astype(BF16)

    def feed(self, at):
        up = dot(self.normed2[at], self.w_up[...])
        normal = 0.5 * (1.0 + lax.erf(up * (1.0 / math.sqrt(2.0))))
        self.hidden[at] = (up * normal).astype(BF16)
        density = jnp.exp(-0.5 * up * up) * (1.0 / math.sqrt(2.0 * math.pi))
        self.slope[at] = (normal + up * density).astype(BF16)

    def mix(self, at):
        return dot_cols(self.attended[at], self.w_out[...]) + dot_cols(self.hidden[at], self.w_down[...])

    def mask(self, at, first, rows):
        past = self.past(first, (rows, 1), 0)
        self.grad[at] = jnp.where(past, 0.0, self.cotangent[at].astype(F32)).astype(BF16)

    def feed_back(self, at):
        d_hidden = dot(self.grad[at], self.w_down[...])
        self.slope[at] = (d_hidden * self.slope[at].astype(F32)).astype(BF16)

    def attend_grad(self, block):
        first = pl.multiple_of(block * BLOCK, BLOCK)
        at = pl.ds(first, BLOCK)
        lane = lanes_of(BLOCK)
        grads = unit_heads(dot(self.grad[at], self.w_out[...]), self.heads)
        outputs = unit_heads(self.attended[at].astype(F32), self.heads)
        for h in range(self.heads):
            grad = grads[h].astype(BF16).astype(F32)
            delta = jnp.sum(jnp.where(lane < 64, grad * outputs[h], 0.0), axis=1, keepdims=True)
            high, middle, low = three_parts(-delta)
            parts = jnp.where(lane == 64, high, jnp.where(lane == 65, middle, jnp.where(lane == 66, low, 0.0)))
            self.d_attended[block, h * BLOCK : (h + 1) * BLOCK] = jnp.where(lane < 64, grad, parts).astype(BF16)

    def attend_back(self, block):
        rows = self.heads * BLOCK
        query, grad = self.queries[block], self.d_attended[block]
        total = jnp.zeros((rows, 128), F32)
        for j in self.key_blocks(block):
            span = slice(j * BLOCK, (j + 1) * BLOCK)
            keys, values = self.keys[span], self.values[span]
            scores, d_probs = dot_cols(keys, query), dot_cols(values, grad)
            if j == block:
                key = lax.broadcasted_iota(jnp.int32, (BLOCK, rows), 0)
                row = lax.rem(lax.broadcasted_iota(jnp.int32, (BLOCK, rows), 1), BLOCK)
                scores = jnp.where(key <= row, scores, NEG)
            probs = jnp.exp(scores)
            d_scores = (probs * d_probs).astype(BF16)
            self.d_values[span] += dot(probs.astype(BF16), grad)
            self.d_keys[span] += dot(d_scores, query)
            total = total + dot_rows(d_scores, keys)
        at = slice(block * BLOCK, (block + 1) * BLOCK)
        lane = lanes_of(BLOCK)
        cosine, sine = self.cosine[at], self.sine[at]

        def turn_back(x):
            return x * cosine - swap_halves(x, lane) * sine

        pieces = [turn_back(total[h * BLOCK : (h + 1) * BLOCK]) * (64 ** (-0.5)) for h in range(self.heads)]
        self.d_query[at] = join_heads(pieces, lane).astype(BF16)
        self.d_keyvalue[at] = jnp.where(
            lane < 64, turn_back(self.d_keys[at]), pltpu.roll(self.d_values[at], 64, 1)
        ).astype(BF16)

    def input_grad(self, block):
        at = slice(block * BLOCK, (block + 1) * BLOCK)
        d_normed1 = dot_cols(self.d_query[at], self.w_query[...]) + dot_cols(self.d_keyvalue[at], self.w_keyvalue[...])
        d_normed2 = dot_cols(self.slope[at], self.w_up[...])
        scaled = self.scaled[at].astype(F32)
        for i, value in enumerate((d_normed1 * scaled, d_normed1, d_normed2 * scaled, d_normed2)):
            self.d_norms[i] += jnp.sum(value.reshape(BLOCK // 8, 8, -1), axis=0)
        return d_normed1 * self.params[0:1] + d_normed2 * self.params[2:3]


MESH = pl.DeviceIdType.MESH
INVMEM = pl.BlockSpec(memory_space=pltpu.VMEM)


class Axis:
    def __init__(self, name, size):
        self.name, self.size, self.half = name, size, size // 2
        self.me = lax.axis_index(name)
        self.row, self.par = self.me // 2, self.me % 2
        self.pair = self.me + 1 - 2 * self.par

    def other_row(self, step):
        return lax.rem(self.row + step + self.half, self.half)

    def line(self, step):
        return self.other_row(step) * 2 + self.par

    def greet(self, barrier):
        for step in range(1, self.size):
            peer = lax.rem(self.me + step, self.size)
            pl.semaphore_signal(barrier, inc=1, device_id={self.name: peer}, device_id_type=MESH)
        return self.size - 1


def remote(src, dst, send, recv, axis, peer):
    return pltpu.make_async_remote_copy(
        src_ref=src, dst_ref=dst, send_sem=send, recv_sem=recv, device_id={axis.name: peer}, device_id_type=MESH
    )


def part_of(ref, index, rows):
    return ref.at[pl.ds(pl.multiple_of(index * rows, rows), rows)]


class Gather:
    def __init__(self, axis, src, dst, send, recv, local):
        self.axis, self.src, self.dst, self.send, self.recv = axis, src, dst, send, recv
        self.copy = pltpu.make_async_copy(src, self.slot(axis.me), local)

    def slot(self, index):
        return part_of(self.dst, index, self.src.shape[0])

    def own(self, index):
        peer = self.axis.pair if index == 0 else self.axis.line(index)
        return remote(self.src, self.slot(self.axis.me), self.send.at[index], self.recv.at[index], self.axis, peer)

    def forward(self, step):
        slot, index = self.slot(self.axis.line(-step)), self.axis.half + step
        return remote(slot, slot, self.send.at[index], self.recv.at[index], self.axis, self.axis.pair)

    def start_line(self):
        for step in range(1, self.axis.half):
            self.own(step).start()

    def start_pair(self):
        self.own(0).start()

    def pass_on(self):
        for step in range(1, self.axis.half):
            self.own(step).wait_recv()
            self.forward(step).start()

    def arrive(self):
        self.copy.wait()
        self.own(0).wait_recv()
        for step in range(1, self.axis.half):
            self.forward(step).wait_recv()

    def leave(self):
        for step in range(self.axis.half):
            self.own(step).wait_send()
        for step in range(1, self.axis.half):
            self.forward(step).wait_send()


class Reduce:
    def __init__(self, axis, part, out, held, last, send, recv):
        self.axis, self.part, self.out, self.held, self.last = axis, part, out, held, last
        self.send, self.recv, self.rows = send, recv, out.shape[0]
        self.chunk = 32 if self.rows % 32 == 0 else self.rows

    def first(self, row):
        block = part_of(self.part, 2 * row + 1 - self.axis.par, self.rows)
        held = part_of(self.held, row, self.rows)
        return remote(block, held, self.send.at[row], self.recv.at[row], self.axis, self.axis.pair)

    def second(self, step):
        index = self.axis.half + step
        block = part_of(self.held, self.axis.other_row(step), self.rows)
        last = part_of(self.last, step - 1, self.rows)
        return remote(block, last, self.send.at[index], self.recv.at[index], self.axis, self.axis.line(step))

    def start(self):
        for row in range(self.axis.half):
            self.first(row).start()

    def chunks(self, body):
        @pl.loop(0, self.rows // self.chunk)
        def _(index):
            body(pl.multiple_of(index * self.chunk, self.chunk))

    def total(self, row, at):
        part = self.part[pl.ds((2 * row + self.axis.par) * self.rows + at, self.chunk)].astype(F32)
        return part + self.held[pl.ds(row * self.rows + at, self.chunk)].astype(F32)

    def middle(self):
        for row in range(self.axis.half):
            self.first(row).wait()
        for step in range(1, self.axis.half):
            row = self.axis.other_row(step)

            def add(at, row=row):
                self.held[pl.ds(row * self.rows + at, self.chunk)] = self.total(row, at).astype(self.held.dtype)

            self.chunks(add)
            self.second(step).start()

        def keep(at):
            self.out[pl.ds(at, self.chunk)] = self.total(self.axis.row, at)

        self.chunks(keep)

    def end(self):
        for step in range(1, self.axis.half):
            self.second(step).wait()

        def add(at):
            total = self.out[pl.ds(at, self.chunk)]
            for step in range(1, self.axis.half):
                total = total + self.last[pl.ds((step - 1) * self.rows + at, self.chunk)].astype(F32)
            self.out[pl.ds(at, self.chunk)] = total

        self.chunks(add)


class Stream:
    def __init__(self, axis, part, out, held, last, pair_send, pair_recv, line_send, line_recv):
        self.axis, self.part, self.out, self.held, self.last = axis, part, out, held, last
        self.pair_sems, self.line_sems = (pair_send, pair_recv), (line_send, line_recv)

    def split(self, chunk):
        return chunk // 4, chunk // 2 % 2, chunk % 2

    def pair_copy(self, chunk):
        row, _, half = self.split(chunk)
        index = 2 * row + half
        send, recv = (sems.at[index] for sems in self.pair_sems)
        held = part_of(self.held, index, BLOCK)
        return remote(part_of(self.part, chunk, BLOCK), held, send, recv, self.axis, self.axis.pair)

    def line_copy(self, chunk):
        row, _, half = self.split(chunk)
        send, recv = (sems.at[half] for sems in self.line_sems)
        held = part_of(self.held, 2 * row + half, BLOCK)
        return remote(held, part_of(self.last, half, BLOCK), send, recv, self.axis, self.axis.line(1))

    def give(self, chunk):
        @pl.when(self.axis.par != self.split(chunk)[1])
        def _():
            self.pair_copy(chunk).start()

    def take(self, chunk):
        row, par, half = self.split(chunk)

        @pl.when(self.axis.par == par)
        def _():
            self.pair_copy(chunk).wait_recv()

            def total(at):
                part = self.part[pl.ds(chunk * BLOCK + at, 32)].astype(F32)
                return part + self.held[pl.ds((2 * row + half) * BLOCK + at, 32)].astype(F32)

            @pl.when(self.axis.row == row)
            def _():
                @pl.loop(0, BLOCK // 32)
                def _(index):
                    at = pl.multiple_of(index * 32, 32)
                    self.out[pl.ds(half * BLOCK + at, 32)] = total(at)

            @pl.when(self.axis.row != row)
            def _():
                @pl.loop(0, BLOCK // 32)
                def _(index):
                    at = pl.multiple_of(index * 32, 32)
                    self.held[pl.ds((2 * row + half) * BLOCK + at, 32)] = total(at).astype(BF16)

                self.line_copy(chunk).start()

    def end(self, chunk):
        row, par, half = self.split(chunk)

        @pl.when(self.axis.par != par)
        def _():
            self.pair_copy(chunk).wait_send()

        @pl.when((self.axis.par == par) & (self.axis.row != row))
        def _():
            self.line_copy(chunk).wait_send()

        @pl.when((self.axis.par == par) & (self.axis.row == row))
        def _():
            self.line_copy(chunk).wait_recv()

            @pl.loop(0, BLOCK // 32)
            def _(index):
                at = pl.multiple_of(index * 32, 32)
                rows = pl.ds(half * BLOCK + at, 32)
                self.out[rows] += self.last[rows].astype(F32)

WEIGHTS = ("w_query", "w_keyvalue", "w_up", "w_down", "w_out")
INPUTS = ("tokens", "cotangent") + WEIGHTS


def own_shapes(z):
    wide_rows = (z.rows, z.model)
    return dict(
        params=((8, z.model), F32), cosine=((z.rows, 128), F32), sine=((z.rows, 128), F32),
        scaled=(wide_rows, BF16), normed1=(wide_rows, BF16), normed2=(wide_rows, BF16),
        queries=((z.rows // BLOCK, z.stack, 128), BF16), keys=((z.rows, 128), BF16), values=((z.rows, 128), BF16),
        scores=((z.stack, z.used), F32), attended=((z.rows, z.wide), BF16), hidden=((z.rows, z.units), BF16),
        slope=((z.rows, z.units), BF16), d_attended=((z.used // BLOCK, z.stack, 128), BF16),
        d_query=((z.used, z.wide), BF16), d_keyvalue=((z.used, 128), BF16), d_keys=((z.used, 128), F32),
        d_values=((z.used, 128), F32), d_norms=((4, 8, z.model), F32),
    )


class Names:
    def __init__(self, names, refs):
        self.__dict__.update(zip(names, refs, strict=True))


def fused_specs(z):
    half, model = z.nd // 2, z.model
    columns = dict(zip(WEIGHTS, (z.wide, 128, z.units, z.units, z.wide)))
    arrays = own_shapes(z)
    arrays.update(pack_query=((z.own, z.wide), BF16), pack_out=((z.own, z.wide), BF16))
    arrays.update(tokens=((z.rows, model), BF16), cotangent=((z.rows, model), BF16))
    arrays.update({name: ((model, columns[name]), BF16) for name in WEIGHTS})
    arrays.update(mixed=((z.rows, model), BF16), held_mixed=((z.rows // 2, model), BF16))
    arrays.update(last_mixed=((z.slots, model), BF16), held_scaled=((z.rows // 2, model), BF16))
    arrays.update(last_scaled=((z.slots, model), BF16))
    for name in WEIGHTS:
        arrays["g_" + name] = ((model, columns[name]), BF16)
        arrays["held_" + name] = ((half * z.own, columns[name]), BF16)
        arrays["last_" + name] = ((max(half - 1, 1) * z.own, columns[name]), BF16)
    arrays.update(g_norms=((z.nd * 8, z.own), F32), held_norms=((half * 8, z.own), F32))
    arrays.update(last_norms=((max(half - 1, 1) * 8, z.own), F32))
    semaphores = dict(send_mixed=z.nt, recv_mixed=z.nt, send_norms=z.nd, recv_norms=z.nd)
    for name in INPUTS:
        count = z.nd if name in WEIGHTS else z.nt
        semaphores.update({"send_" + name: count, "recv_" + name: count})
    for name in WEIGHTS:
        semaphores.update({"out_" + name: z.nd, "in_" + name: z.nd})
    semaphores.update(pair_send=4, pair_recv=4, line_send=2, line_recv=2, local=len(INPUTS))
    semaphores.update(share_send=2 * z.nt, share_recv=2 * z.nt)
    return arrays, semaphores


OUTPUTS = ("mixed_sum", "scaled_sum", "s_w_query", "s_w_out", "s_w_up", "s_w_down", "shared_kv", "shared_norms")


def fused_kernel(z, names, *refs):
    it = Names(("seq", "norms") + tuple("i_" + n for n in INPUTS) + OUTPUTS + names, refs)
    dp, tensor = Axis("dp", z.nd), Axis("tensor", z.nt)
    rows, model, used, slots = z.rows, z.model, z.used, z.slots
    core = Core(z.heads, it.seq[0, 0], **{n: getattr(it, n) for n in tuple(own_shapes(z)) + INPUTS}, grad=it.cotangent)
    barrier = pltpu.get_barrier_semaphore()
    expected = dp.greet(barrier) + tensor.greet(barrier)

    width = z.heads * 64
    pad = jnp.zeros((z.own, z.wide - width), BF16)
    lane = lanes_of(z.own)
    first = width // 128 * 128
    tail = jnp.concatenate([it.i_w_query[:, first:].astype(F32), pad.astype(F32)], axis=1)
    it.pack_query[:, :first] = it.i_w_query[:, :first]
    it.pack_query[:, first:] = jnp.where(lane < width - first, tail, it.norms[...].astype(F32)).astype(BF16)
    it.pack_out[:, :first] = it.i_w_out[:, :first]
    it.pack_out[:, first:] = jnp.concatenate([it.i_w_out[:, first:], pad], axis=1)
    sources = dict(w_query=it.pack_query, w_out=it.pack_out)
    g = {}
    for i, name in enumerate(INPUTS):
        axis = tensor if name in ("tokens", "cotangent") else dp
        source = sources.get(name, getattr(it, "i_" + name))
        sems = getattr(it, "send_" + name), getattr(it, "recv_" + name)
        g[name] = Gather(axis, source, getattr(it, name), *sems, it.local.at[i])
    pl.semaphore_wait(barrier, expected)

    for name in ("tokens", "cotangent"):
        g[name].start_line()
        g[name].start_pair()
    for name in WEIGHTS:
        g[name].start_line()
    g["w_query"].start_pair()
    g["w_keyvalue"].start_pair()
    for name in INPUTS:
        g[name].copy.start()
    core.tables()
    for name in ("w_query", "w_keyvalue"):
        g[name].pass_on()
    g["w_up"].start_pair()
    for name in ("w_query", "w_keyvalue"):
        g[name].arrive()
    core.unpack_params()

    def enter(slot):
        for part in range(slots // BLOCK):
            core.normalize(slot * (slots // BLOCK) + part)
            core.project(slot * (slots // BLOCK) + part)

    g["tokens"].copy.wait()

    @pl.loop(0, 2)
    def _(index):
        @pl.when(index == 1)
        def _():
            g["tokens"].own(0).wait_recv()

        enter(tensor.me + index * (tensor.pair - tensor.me))

    g["w_up"].pass_on()
    g["w_down"].start_pair()
    g["tokens"].pass_on()

    @pl.loop(0, 2)
    def _(index):
        @pl.when(index == 1)
        def _():
            g["tokens"].forward(1).wait_recv()

        enter(tensor.line(1) + index * (tensor.pair - tensor.me))

    for block in range(rows // BLOCK):
        core.attend(block)
        if block == 4:
            g["w_down"].pass_on()
            g["w_out"].start_pair()
    g["w_up"].arrive()

    @pl.loop(0, rows // slots)
    def _(index):
        core.feed(pl.ds(pl.multiple_of(index * slots, slots), slots))

    g["w_out"].pass_on()
    g["cotangent"].pass_on()
    g["w_down"].arrive()
    g["cotangent"].arrive()
    g["cotangent"].leave()

    quarter = used // 4

    @pl.loop(0, 4)
    def _(index):
        first = pl.multiple_of(index * quarter, quarter)
        core.mask(pl.ds(first, quarter), first, quarter)

    r = {}
    for name in WEIGHTS:
        out = getattr(it, "s_" + name) if name != "w_keyvalue" else it.shared_kv.at[tensor.me]
        some = [getattr(it, kind + name) for kind in ("g_", "held_", "last_", "out_", "in_")]
        r[name] = Reduce(dp, some[0], out, *some[1:])
    r["norms"] = Reduce(
        dp, it.g_norms, it.shared_norms.at[tensor.me], it.held_norms, it.last_norms, it.send_norms, it.recv_norms
    )
    r["mixed"] = Reduce(tensor, it.mixed, it.mixed_sum, it.held_mixed, it.last_mixed, it.send_mixed, it.recv_mixed)
    scaled = Stream(
        tensor, it.mixed, it.scaled_sum, it.held_scaled, it.last_scaled,
        it.pair_send, it.pair_recv, it.line_send, it.line_recv,
    )

    def weight_grad(name, left, right):
        @pl.loop(0, model // BLOCK)
        def _(index):
            at = pl.ds(pl.multiple_of(index * BLOCK, BLOCK), BLOCK)
            r[name].part[at] = dot_rows(left[:used, at], right[:used]).astype(BF16)

    weight_grad("w_down", core.grad, core.hidden)
    r["w_down"].start()
    weight_grad("w_out", core.grad, core.attended)
    r["w_out"].start()
    g["w_out"].arrive()

    @pl.loop(0, tensor.size)
    def _(index):
        row = lax.rem(index, tensor.half)
        par = jnp.where(index < tensor.half, 1 - tensor.par, tensor.par)
        at = pl.ds(pl.multiple_of((2 * row + par) * slots, slots), slots)
        it.mixed[at] = core.mix(at).astype(BF16)

        @pl.when(index < tensor.half)
        def _():
            r["mixed"].first(row).start()

    @pl.loop(0, 4)
    def _(index):
        core.feed_back(pl.ds(pl.multiple_of(index * quarter, quarter), quarter))

    weight_grad("w_up", core.normed2, core.slope)
    r["w_up"].start()
    r["mixed"].middle()

    @pl.loop(0, used // BLOCK)
    def _(block):
        core.attend_grad(block)

    r["w_down"].middle()
    for ref in (core.d_keys, core.d_values, core.d_norms, it.scaled_sum):
        ref[...] = jnp.zeros_like(ref)
    chunks = range(used // BLOCK - 1, -1, -1)
    for block in chunks:
        core.attend_back(block)
        it.mixed[block * BLOCK : (block + 1) * BLOCK] = core.input_grad(block).astype(BF16)
        scaled.give(block)
        if block + 1 in chunks:
            scaled.take(block + 1)
        if block == 5:
            r["w_out"].middle()
        if block == 3:
            r["w_up"].middle()

    weight_grad("w_query", core.normed1, core.d_query)
    r["w_query"].start()
    weight_grad("w_keyvalue", core.normed1, core.d_keyvalue)
    r["w_keyvalue"].start()
    part = model // dp.size
    sums = jnp.concatenate([jnp.sum(core.d_norms[i], axis=0, keepdims=True) for i in range(4)] + [jnp.zeros((4, model), F32)])
    for i in range(dp.size):
        it.g_norms[i * 8 : (i + 1) * 8] = sums[:, i * part : (i + 1) * part]
    r["norms"].start()
    scaled.take(0)
    for name in ("w_query", "w_keyvalue", "norms"):
        r[name].middle()
    for name in ("w_keyvalue", "norms"):
        r[name].end()
    copies = []
    for i, ref in enumerate((it.shared_kv, it.shared_norms)):
        for step in range(1, tensor.size):
            peer = lax.rem(tensor.me + step, tensor.size)
            sems = [s.at[i * tensor.size + step] for s in (it.share_send, it.share_recv)]
            copies.append(remote(ref.at[tensor.me], ref.at[tensor.me], *sems, tensor, peer))
            copies[-1].start()
    for name in ("w_down", "w_out", "w_up", "mixed", "w_query"):
        r[name].end()
    for block in chunks:
        scaled.end(block)
    for copy in copies:
        copy.wait()
    for name in INPUTS:
        if name != "cotangent":
            g[name].leave()


def finish_kernel(heads, seq, tokens, cotangent, *refs):
    sums = Names(OUTPUTS, refs[: len(OUTPUTS)])
    out_tokens, d_tokens, d_query, d_keyvalue, d_out, d_up, d_down, d_norms = refs[len(OUTPUTS) :]
    rows, chunk = tokens.shape[0], 128
    first_row = lax.axis_index("tensor") * rows

    @pl.loop(0, rows // chunk)
    def _(index):
        first = pl.multiple_of(index * chunk, chunk)
        at = pl.ds(first, chunk)
        token = tokens[at].astype(F32)
        out_tokens[at] = (token + sums.mixed_sum[at]).astype(BF16)
        centered = token - jnp.mean(token, axis=1, keepdims=True)
        inv_std = lax.rsqrt(jnp.mean(centered * centered, axis=1, keepdims=True) + EPS)
        scaled = centered * inv_std
        grad = sums.scaled_sum[at]
        row = lax.broadcasted_iota(jnp.int32, (chunk, 1), 0) + first + first_row
        own = jnp.where(row < seq[0, 0], cotangent[at].astype(F32), 0.0)
        inner = jnp.mean(grad * scaled, axis=1, keepdims=True)
        d_tokens[at] = own + inv_std * (grad - jnp.mean(grad, axis=1, keepdims=True) - scaled * inner)

    d_query[...] = sums.s_w_query[:, : heads * 64]
    d_out[...] = sums.s_w_out[:, : heads * 64]
    d_up[...] = sums.s_w_up[...]
    d_down[...] = sums.s_w_down[...]
    kv, norms = sums.shared_kv[0], sums.shared_norms[0]
    for t in range(1, sums.shared_kv.shape[0]):
        kv, norms = kv + sums.shared_kv[t], norms + sums.shared_norms[t]
    d_keyvalue[...] = kv
    d_norms[...] = norms


def plain_kernel(z, seq, *refs):
    named = dict(zip(INPUTS, refs))
    mixed, scaled_grad, g_query, g_keyvalue, g_out, g_up, g_down, g_norms = refs[len(INPUTS) : len(INPUTS) + 8]
    *own, grad = refs[len(INPUTS) + 8 :]
    named.update(zip(own_shapes(z), own), grad=grad)
    core = Core(z.heads, seq[0, 0], **named)
    rows, model, used = z.rows, z.model, z.used
    core.tables()
    core.unpack_params()

    @pl.loop(0, rows // BLOCK)
    def _(block):
        core.normalize(block)
        core.project(block)

    for block in range(rows // BLOCK):
        core.attend(block)

    @pl.loop(0, rows // 512)
    def _(index):
        at = pl.ds(pl.multiple_of(index * 512, 512), 512)
        core.feed(at)
        mixed[at] = core.mix(at).astype(BF16)

    @pl.loop(0, 4)
    def _(index):
        first = pl.multiple_of(index * (used // 4), used // 4)
        core.mask(pl.ds(first, used // 4), first, used // 4)
        core.feed_back(pl.ds(first, used // 4))

    @pl.loop(0, used // BLOCK)
    def _(block):
        core.attend_grad(block)

    @pl.loop(0, model // BLOCK)
    def _(index):
        at = pl.ds(pl.multiple_of(index * BLOCK, BLOCK), BLOCK)
        grad = core.grad[:used, at]
        g_down[at] = dot_rows(grad, core.hidden[:used]).astype(BF16)
        g_out[at] = dot_rows(grad, core.attended[:used]).astype(BF16)
        g_up[at] = dot_rows(core.normed2[:used, at], core.slope[:used]).astype(BF16)

    for ref in (core.d_keys, core.d_values, core.d_norms):
        ref[...] = jnp.zeros_like(ref)
    for block in range(used // BLOCK - 1, -1, -1):
        core.attend_back(block)
        scaled_grad[block * BLOCK : (block + 1) * BLOCK] = core.input_grad(block).astype(BF16)
    scaled_grad[used:] = jnp.zeros((rows - used, model), BF16)

    @pl.loop(0, model // BLOCK)
    def _(index):
        at = pl.ds(pl.multiple_of(index * BLOCK, BLOCK), BLOCK)
        normed = core.normed1[:used, at]
        g_query[at] = dot_rows(normed, core.d_query[:used]).astype(BF16)
        g_keyvalue[at] = dot_rows(normed, core.d_keyvalue[:used]).astype(BF16)

    for i in range(4):
        g_norms[i : i + 1] = jnp.sum(core.d_norms[i], axis=0, keepdims=True)


def run_plain(seq_lengths, norms, arrays, z):
    tokens, cotangent, w_query, w_keyvalue, w_up, w_down, w_out = arrays
    width, model = w_query.shape[1], tokens.shape[1]
    wide = z.wide
    pad = jnp.pad(w_query[:, width // 128 * 128 :], ((0, 0), (0, wide - width)))
    lane = lax.iota(jnp.int32, 128)[None]
    tail = jnp.where(lane < width % 128, pad, norms)
    query = jnp.concatenate([w_query[:, : width // 128 * 128], tail], axis=1)
    out = jnp.pad(w_out, ((0, 0), (0, wide - width)))
    gathered = [lax.all_gather(a, "tensor", axis=0, tiled=True) for a in (tokens, cotangent)]
    gathered += [lax.all_gather(a, "dp", axis=0, tiled=True) for a in (query, w_keyvalue, w_up, w_down, out)]
    shape = jax.ShapeDtypeStruct
    results = pl.pallas_call(
        functools.partial(plain_kernel, z),
        out_shape=[shape((z.rows, model), BF16)] * 2
        + [shape((model, n), BF16) for n in (wide, 128, wide, z.units, z.units)]
        + [shape((4, model), F32)],
        in_specs=[pl.BlockSpec(memory_space=pltpu.SMEM)] + [INVMEM] * len(gathered),
        out_specs=[INVMEM] * 8,
        scratch_shapes=[pltpu.VMEM(*entry) for entry in own_shapes(z).values()] + [pltpu.VMEM((z.used, model), BF16)],
        compiler_params=pltpu.CompilerParams(vmem_limit_bytes=67043328),
        name="plain_layer",
    )(seq_lengths, *gathered)
    names = ("tensor", "tensor") + ("dp",) * 5
    sums = [
        lax.psum_scatter(p.astype(F32), n, scatter_dimension=0, tiled=True) for p, n in zip(results[:7], names)
    ]
    norm_sums = lax.psum_scatter(results[7], "dp", scatter_dimension=1, tiled=True)
    shared_kv = lax.all_gather(sums[3], "tensor")
    shared_norms = lax.all_gather(jnp.pad(norm_sums, ((0, 4), (0, 0))), "tensor")
    return sums[0], sums[1], sums[2], sums[4], sums[5], sums[6], shared_kv, shared_norms


def run_whole(seq_lengths, norms, arrays, z):
    arrays_of, semaphores = fused_specs(z)
    shapes = [
        (z.slots, z.model), (z.slots, z.model), (z.own, z.wide), (z.own, z.wide), (z.own, z.units), (z.own, z.units),
        (z.nt, z.own, 128), (z.nt, 8, z.own),
    ]
    scratch = [pltpu.VMEM(*entry) for entry in arrays_of.values()]
    scratch += [pltpu.SemaphoreType.DMA((count,)) for count in semaphores.values()]
    return pl.pallas_call(
        functools.partial(fused_kernel, z, tuple(arrays_of) + tuple(semaphores)),
        out_shape=[jax.ShapeDtypeStruct(shape, F32) for shape in shapes],
        in_specs=[pl.BlockSpec(memory_space=pltpu.SMEM)] + [INVMEM] * (1 + len(arrays)),
        out_specs=[INVMEM] * len(shapes),
        scratch_shapes=scratch,
        compiler_params=pltpu.CompilerParams(collective_id=0, has_side_effects=True, vmem_limit_bytes=67043328),
        name="layer",
    )(seq_lengths, norms, *arrays)


def run_layer(seq_lengths, norms, arrays, nd, nt):
    tokens, _, w_query, w_keyvalue, w_up, _, _ = arrays
    heads, own, units = w_query.shape[1] // 64, w_query.shape[0], w_up.shape[1]
    slots, model = tokens.shape
    z = types.SimpleNamespace(
        nd=nd, nt=nt, heads=heads, rows=slots * nt, model=model, stack=heads * BLOCK, units=units, used=SEQ_MOST,
        wide=(heads * 64 + 4 + 127) // 128 * 128, own=own, slots=slots,
    )
    run = run_whole if own % 32 == 0 and slots == 2 * BLOCK and nt == 4 else run_plain
    sums = run(seq_lengths, norms, arrays, z)
    shape = jax.ShapeDtypeStruct
    results = pl.pallas_call(
        functools.partial(finish_kernel, heads),
        out_shape=[
            shape((slots, model), BF16), shape((slots, model), F32), shape((own, heads * 64), F32), shape((own, 128), F32),
            shape((own, heads * 64), F32), shape((own, units), F32), shape((own, units), F32), shape((8, own), F32),
        ],
        in_specs=[pl.BlockSpec(memory_space=pltpu.SMEM)] + [INVMEM] * (2 + len(sums)),
        out_specs=[INVMEM] * 8,
        compiler_params=pltpu.CompilerParams(vmem_limit_bytes=48 << 20),
        name="finish",
    )(seq_lengths, *arrays[:2], *sums)
    return tuple(results[:7]) + tuple(results[7][i] for i in range(4))


def shards(
    tokens,
    cotangent,
    seq_lengths,
    w_query,
    w_keyvalue,
    w_out,
    w_up,
    w_down,
    norm1_gain,
    norm1_bias,
    norm2_gain,
    norm2_bias,
):
    start = w_query.shape[1] % 128
    norms = jnp.stack([norm1_gain, norm1_bias, norm2_gain, norm2_bias], axis=1)
    norms = jnp.pad(norms, ((0, 0), (start, 124 - start)))
    arrays = (tokens, cotangent, w_query, w_keyvalue, w_up, w_down, w_out)
    return run_layer(seq_lengths, norms, arrays, lax.axis_size("dp"), lax.axis_size("tensor"))


def solution(mesh):
    return jax.shard_map(
        shards,
        mesh=mesh,
        in_specs=(
            P(("dp", "tensor"), None),
            P(("dp", "tensor"), None),
            P("dp", None),
            P("dp", "tensor"),
            P("dp", None),
            P("dp", "tensor"),
            P("dp", "tensor"),
            P("dp", "tensor"),
            P("dp"),
            P("dp"),
            P("dp"),
            P("dp"),
        ),
        out_specs=(
            P(("dp", "tensor"), None),
            P(("dp", "tensor"), None),
            P("dp", "tensor"),
            P("dp", None),
            P("dp", "tensor"),
            P("dp", "tensor"),
            P("dp", "tensor"),
            P("dp"),
            P("dp"),
            P("dp"),
            P("dp"),
        ),
        check_vma=False,
    )
```

```python
import functools
import math
import types

import jax
import jax.numpy as jnp
from jax import lax
from jax.experimental import pallas as pl
from jax.experimental.pallas import tpu as pltpu
from jax.sharding import PartitionSpec as P

ROT = 16
SEQ_LEAST = 1024
SEQ_MOST = 1792
BLOCK = 256
EPS = 1e-05
NEG = -1e30
F32 = jnp.float32
BF16 = jnp.bfloat16


def dot(left, right):
    return jnp.dot(left, right, preferred_element_type=F32)


def dot_rows(left, right):
    return lax.dot_general(left, right, (((0,), (0,)), ((), ())), preferred_element_type=F32)


def dot_cols(left, right):
    return lax.dot_general(left, right, (((1,), (1,)), ((), ())), preferred_element_type=F32)


def lanes_of(rows):
    return lax.broadcasted_iota(jnp.int32, (rows, 128), 1)


def swap_halves(x, lane):
    return jnp.where(lane < ROT // 2, pltpu.roll(x, 128 - ROT // 2, 1), pltpu.roll(x, ROT // 2, 1))


def three_parts(x):
    high = x.astype(BF16).astype(F32)
    middle = (x - high).astype(BF16).astype(F32)
    return high, middle, x - high - middle


def unit_heads(wide, heads):
    pieces = []
    for h in range(heads):
        piece = wide[:, h // 2 * 128 : h // 2 * 128 + 128]
        pieces.append(piece if h % 2 == 0 else pltpu.roll(piece, 64, 1))
    return pieces


def join_heads(pieces, lane):
    wide = []
    for h in range(0, len(pieces), 2):
        second = pltpu.roll(pieces[h + 1], 64, 1) if h + 1 < len(pieces) else jnp.zeros_like(pieces[h])
        wide.append(jnp.where(lane < 64, pieces[h], second))
    return jnp.concatenate(wide, axis=1)


class Core:
    def __init__(self, heads, length, **refs):
        self.heads, self.length = heads, length
        self.__dict__.update(refs)
        stack, used = heads * BLOCK, self.d_query.shape[0]
        self.d_stack = self.scores.at[0:stack, 0:128]
        self.d_keys = self.scores.at[stack : stack + used, 0:128]
        self.d_values = self.scores.at[stack : stack + used, 128:256]

    def past(self, first, shape, axis):
        return lax.broadcasted_iota(jnp.int32, shape, axis) + first >= self.length

    def tables(self, part):
        count = self.cosine.shape[0] // BLOCK // 2

        @pl.loop(part * count, part * count + count)
        def _(index):
            at = pl.ds(pl.multiple_of(index * BLOCK, BLOCK), BLOCK)
            lane = lanes_of(BLOCK)
            row = lax.broadcasted_iota(jnp.int32, (BLOCK, 128), 0) + index * BLOCK
            position = jnp.where(row >= self.length, row - self.length, row).astype(F32)
            exponent = jnp.where(lane < ROT // 2, lane, lane - ROT // 2).astype(F32) * (-2.0 / ROT)
            angle = position * jnp.exp(exponent * math.log(10000.0))
            sine = jnp.sin(angle)
            self.cosine[at] = jnp.where(lane < ROT, jnp.cos(angle), 1.0)
            self.sine[at] = jnp.where(lane < ROT // 2, -sine, jnp.where(lane < ROT, sine, 0.0))

    def unpack_params(self):
        start = self.heads * 64
        turned = self.w_query[:, start // 128 * 128 : start // 128 * 128 + 128].T.astype(F32)
        self.params[0:4] = turned[start % 128 : start % 128 + 4]

    def normalize(self, block):
        at = pl.ds(pl.multiple_of(block * BLOCK, BLOCK), BLOCK)
        x = self.tokens[at].astype(F32)
        centered = x - jnp.mean(x, axis=1, keepdims=True)
        scaled = centered * lax.rsqrt(jnp.mean(centered * centered, axis=1, keepdims=True) + EPS)
        gain1, bias1, gain2, bias2 = (self.params[i : i + 1] for i in range(4))
        self.scaled[at] = scaled.astype(BF16)
        self.normed1[at] = (scaled * gain1 + bias1).astype(BF16)
        self.normed2[at] = (scaled * gain2 + bias2).astype(BF16)

    def project(self, block):
        first = pl.multiple_of(block * BLOCK, BLOCK)
        at = pl.ds(first, BLOCK)
        lane = lanes_of(BLOCK)
        cosine, sine = self.cosine[at], self.sine[at]
        past = self.past(first, (BLOCK, 128), 0)
        normed = self.normed1[at]
        key_value = dot(normed, self.w_keyvalue[...])
        keys = key_value * cosine + swap_halves(key_value, lane) * sine
        hidden_key = jnp.where(past, 0.0, NEG)
        extra = jnp.where(lane == 64, hidden_key, jnp.where(lane < 68, -1.0, 0.0))
        self.keys[at] = jnp.where(lane < 64, keys, extra).astype(BF16)
        ones = jnp.where(lane < 67, 1.0, 0.0)
        self.values[at] = jnp.where(lane < 64, pltpu.roll(key_value, 64, 1), ones).astype(BF16)
        query = dot(normed, self.w_query[...])
        flag = jnp.where((lane == 64) & past, 1.0, 0.0)
        for h, piece in enumerate(unit_heads(query, self.heads)):
            turned = (piece * cosine + swap_halves(piece, lane) * sine).astype(BF16).astype(F32)
            turned = turned * (64 ** (-0.5))
            self.queries[block, h * BLOCK : (h + 1) * BLOCK] = jnp.where(lane < 64, turned, flag).astype(BF16)

    def key_blocks(self, block):
        first = SEQ_LEAST // BLOCK if block * BLOCK >= SEQ_MOST else 0
        return range(first, block + 1)

    def attend(self, block):
        rows = self.heads * BLOCK
        query = self.queries[block]
        lane = lanes_of(rows)
        top = jnp.full((rows, BLOCK), -3e38, F32)
        for index, j in enumerate(self.key_blocks(block)):
            scores = dot_cols(query, self.keys[j * BLOCK : (j + 1) * BLOCK])
            if j == block:
                row = lax.rem(lax.broadcasted_iota(jnp.int32, (rows, BLOCK), 0), BLOCK)
                column = lax.broadcasted_iota(jnp.int32, (rows, BLOCK), 1)
                scores = jnp.where(column <= row, scores, NEG)
            self.scores[index * rows : (index + 1) * rows] = scores
            top = jnp.maximum(top, scores)
        top = jnp.max(top, axis=1, keepdims=True)
        total = jnp.zeros((rows, 128), F32)
        for index, j in enumerate(self.key_blocks(block)):
            probs = jnp.exp(self.scores[index * rows : (index + 1) * rows] - top).astype(BF16)
            total = total + dot(probs, self.values[j * BLOCK : (j + 1) * BLOCK])
        weight = jnp.sum(jnp.where(lane == 64, total, 0.0), axis=1, keepdims=True)
        output = total / weight
        pieces = [output[h * BLOCK : (h + 1) * BLOCK] for h in range(self.heads)]
        self.attended[block * BLOCK : (block + 1) * BLOCK] = join_heads(pieces, lanes_of(BLOCK)).astype(BF16)
        high, middle, low = three_parts(top + jnp.log(weight))
        parts = jnp.where(lane == 65, high, jnp.where(lane == 66, middle, low))
        self.queries[block] = jnp.where((lane >= 65) & (lane < 68), parts, query.astype(F32)).astype(BF16)

    def feed(self, at):
        up = dot(self.normed2[at], self.w_up[...])
        normal = 0.5 * (1.0 + lax.erf(up * (1.0 / math.sqrt(2.0))))
        self.hidden[at] = (up * normal).astype(BF16)
        density = jnp.exp(-0.5 * up * up) * (1.0 / math.sqrt(2.0 * math.pi))
        self.slope[at] = (normal + up * density).astype(BF16)

    def mix(self, at):
        return dot_cols(self.attended[at], self.w_out[...]) + dot_cols(self.hidden[at], self.w_down[...])

    def mask(self, at, first, rows):
        past = self.past(first, (rows, 1), 0)
        self.grad[at] = jnp.where(past, 0.0, self.cotangent[at].astype(F32)).astype(BF16)

    def feed_back(self, at):
        d_hidden = dot(self.grad[at], self.w_down[...])
        self.slope[at] = (d_hidden * self.slope[at].astype(F32)).astype(BF16)

    def attend_grad(self, block):
        first = pl.multiple_of(block * BLOCK, BLOCK)
        at = pl.ds(first, BLOCK)
        lane = lanes_of(BLOCK)
        grads = unit_heads(dot(self.grad[at], self.w_out[...]), self.heads)
        outputs = unit_heads(self.attended[at].astype(F32), self.heads)
        for h in range(self.heads):
            grad = grads[h].astype(BF16).astype(F32)
            delta = jnp.sum(jnp.where(lane < 64, grad * outputs[h], 0.0), axis=1, keepdims=True)
            high, middle, low = three_parts(-delta)
            parts = jnp.where(lane == 64, high, jnp.where(lane == 65, middle, jnp.where(lane == 66, low, 0.0)))
            self.d_attended[block, h * BLOCK : (h + 1) * BLOCK] = jnp.where(lane < 64, grad, parts).astype(BF16)

    def attend_back(self, block):
        rows = self.heads * BLOCK
        query, grad = self.queries[block], self.d_attended[block]

        def span(first, size, diagonal):
            at = pl.ds(pl.multiple_of(first, BLOCK), size)
            keys, values = self.keys[at], self.values[at]
            scores, d_probs = dot_cols(keys, query), dot_cols(values, grad)
            if diagonal:
                key = lax.broadcasted_iota(jnp.int32, (size, rows), 0)
                row = lax.rem(lax.broadcasted_iota(jnp.int32, (size, rows), 1), BLOCK) + (size - BLOCK)
                scores = jnp.where(key <= row, scores, NEG)
            probs = jnp.exp(scores)
            d_scores = (probs * d_probs).astype(BF16)
            self.d_values[at] += dot(probs.astype(BF16), grad)
            self.d_keys[at] += dot(d_scores, query)
            d_query = dot_rows(d_scores, keys)
            if diagonal:
                self.d_stack[...] = d_query
            else:
                self.d_stack[...] += d_query

        @pl.when(block % 2 == 1)
        def _():
            span((block - 1) * BLOCK, 2 * BLOCK, True)

        @pl.when(block % 2 == 0)
        def _():
            span(block * BLOCK, BLOCK, True)

        @pl.loop(0, block // 2)
        def _(index):
            span(index * 2 * BLOCK, 2 * BLOCK, False)

        at = pl.ds(pl.multiple_of(block * BLOCK, BLOCK), BLOCK)
        lane = lanes_of(BLOCK)
        cosine, sine = self.cosine[at], self.sine[at]

        def turn_back(x):
            return x * cosine - swap_halves(x, lane) * sine

        pieces = [
            turn_back(self.d_stack[h * BLOCK : (h + 1) * BLOCK]) * (64 ** (-0.5)) for h in range(self.heads)
        ]
        self.d_query[at] = join_heads(pieces, lane).astype(BF16)
        self.d_keyvalue[at] = jnp.where(
            lane < 64, turn_back(self.d_keys[at]), pltpu.roll(self.d_values[at], 64, 1)
        ).astype(BF16)

    def input_grad(self, block):
        at = pl.ds(pl.multiple_of(block * BLOCK, BLOCK), BLOCK)
        d_normed1 = dot_cols(self.d_query[at], self.w_query[...]) + dot_cols(self.d_keyvalue[at], self.w_keyvalue[...])
        d_normed2 = dot_cols(self.slope[at], self.w_up[...])
        scaled = self.scaled[at].astype(F32)
        for i, value in enumerate((d_normed1 * scaled, d_normed1, d_normed2 * scaled, d_normed2)):
            self.d_norms[i] += jnp.sum(value.reshape(BLOCK // 8, 8, -1), axis=0)
        return d_normed1 * self.params[0:1] + d_normed2 * self.params[2:3]


MESH = pl.DeviceIdType.MESH
INVMEM = pl.BlockSpec(memory_space=pltpu.VMEM)


class Axis:
    def __init__(self, name, size):
        self.name, self.size, self.half = name, size, size // 2
        self.me = lax.axis_index(name)
        self.row, self.par = self.me // 2, self.me % 2
        self.pair = self.me + 1 - 2 * self.par

    def other_row(self, step):
        return lax.rem(self.row + step + self.half, self.half)

    def line(self, step):
        return self.other_row(step) * 2 + self.par

    def greet(self, barrier):
        for step in range(1, self.size):
            peer = lax.rem(self.me + step, self.size)
            pl.semaphore_signal(barrier, inc=1, device_id={self.name: peer}, device_id_type=MESH)
        return self.size - 1


def remote(src, dst, send, recv, axis, peer):
    return pltpu.make_async_remote_copy(
        src_ref=src, dst_ref=dst, send_sem=send, recv_sem=recv, device_id={axis.name: peer}, device_id_type=MESH
    )


def part_of(ref, index, rows):
    return ref.at[pl.ds(pl.multiple_of(index * rows, rows), rows)]


class Gather:
    def __init__(self, axis, src, dst, send, recv, local):
        self.axis, self.src, self.dst, self.send, self.recv = axis, src, dst, send, recv
        self.half = axis.half
        self.copy = pltpu.make_async_copy(src, self.slot(axis.me), local)

    def slot(self, index):
        return part_of(self.dst, index, self.src.shape[0])

    def along(self, row, way, own=False):
        slot = self.slot(2 * row + self.axis.par)
        send = self.send.at[row if way > 0 else self.half + row]
        peer = self.axis.me + 2 * way
        return remote(self.src if own else slot, slot, send, self.recv.at[row], self.axis, peer)

    def across(self, row, own=False):
        slot = self.slot(2 * row + self.axis.par)
        sems = self.send.at[2 * self.half + row], self.recv.at[self.half + row]
        return remote(self.src if own else slot, slot, *sems, self.axis, self.axis.pair)

    def start_line(self):
        @pl.when(self.axis.row + 1 < self.half)
        def _():
            self.along(self.axis.row, 1, own=True).start()

        @pl.when(self.axis.row > 0)
        def _():
            self.along(self.axis.row, -1, own=True).start()

    def start_pair(self):
        self.across(self.axis.row, own=True).start()

    def pass_on(self, distance):
        if distance >= self.half:
            return
        me = self.axis.row

        @pl.when(me >= distance)
        def _():
            row = me - distance
            self.along(row, 1).wait_recv()

            @pl.when(me + 1 < self.half)
            def _():
                self.along(row, 1).start()

            self.across(row).start()

        @pl.when(me + distance < self.half)
        def _():
            row = me + distance
            self.along(row, -1).wait_recv()

            @pl.when(me > 0)
            def _():
                self.along(row, -1).start()

            self.across(row).start()

    def pair_arrived(self, row):
        slot = self.slot(2 * row + 1 - self.axis.par)
        sems = self.send.at[2 * self.half + row], self.recv.at[self.half + row]
        remote(slot, slot, *sems, self.axis, self.axis.pair).wait_recv()

    def arrive(self):
        self.copy.wait()
        for row in range(self.half):
            self.pair_arrived(row)

    def leave(self):
        for row in range(self.half):
            self.across(row).wait_send()

            @pl.when((self.axis.row >= row) & (self.axis.row + 1 < self.half))
            def _():
                self.along(row, 1).wait_send()

            @pl.when((self.axis.row <= row) & (self.axis.row > 0))
            def _():
                self.along(row, -1).wait_send()


class Reduce:
    def __init__(self, axis, part, out, held, last, send, recv):
        self.axis, self.part, self.out, self.held, self.last = axis, part, out, held, last
        self.send, self.recv, self.rows = send, recv, out.shape[0]
        self.chunk = 32 if self.rows % 32 == 0 else self.rows

    def first(self, row):
        block = part_of(self.part, 2 * row + 1 - self.axis.par, self.rows)
        held = part_of(self.held, row, self.rows)
        return remote(block, held, self.send.at[row], self.recv.at[row], self.axis, self.axis.pair)

    def second(self, step):
        index = self.axis.half + step
        block = part_of(self.held, self.axis.other_row(step), self.rows)
        last = part_of(self.last, step - 1, self.rows)
        return remote(block, last, self.send.at[index], self.recv.at[index], self.axis, self.axis.line(step))

    def start(self):
        for step in range(self.axis.half):
            self.first(self.axis.other_row(step + 1)).start()

    def chunks(self, body):
        @pl.loop(0, self.rows // self.chunk)
        def _(index):
            body(pl.multiple_of(index * self.chunk, self.chunk))

    def total(self, row, at):
        part = self.part[pl.ds((2 * row + self.axis.par) * self.rows + at, self.chunk)].astype(F32)
        return part + self.held[pl.ds(row * self.rows + at, self.chunk)].astype(F32)

    def middle(self):
        for step in range(1, self.axis.half):
            row = self.axis.other_row(step)
            self.first(row).wait()

            def add(at, row=row):
                self.held[pl.ds(row * self.rows + at, self.chunk)] = self.total(row, at).astype(self.held.dtype)

            self.chunks(add)
            self.second(step).start()

        self.first(self.axis.row).wait()

        def keep(at):
            self.out[pl.ds(at, self.chunk)] = self.total(self.axis.row, at)

        self.chunks(keep)

    def end(self):
        for step in range(1, self.axis.half):
            self.second(step).wait()

        def add(at):
            total = self.out[pl.ds(at, self.chunk)]
            for step in range(1, self.axis.half):
                total = total + self.last[pl.ds((step - 1) * self.rows + at, self.chunk)].astype(F32)
            self.out[pl.ds(at, self.chunk)] = total

        self.chunks(add)


class Stream:
    def __init__(self, axis, part, out, held, last, pair_send, pair_recv, line_send, line_recv):
        self.axis, self.part, self.out, self.held, self.last = axis, part, out, held, last
        self.pair_sems, self.line_sems = (pair_send, pair_recv), (line_send, line_recv)

    def split(self, chunk):
        return chunk // 4, chunk // 2 % 2, chunk % 2

    def pair_copy(self, chunk):
        row, _, half = self.split(chunk)
        index = 2 * row + half
        send, recv = (sems.at[index] for sems in self.pair_sems)
        held = part_of(self.held, index, BLOCK)
        return remote(part_of(self.part, chunk, BLOCK), held, send, recv, self.axis, self.axis.pair)

    def line_copy(self, chunk):
        row, _, half = self.split(chunk)
        send, recv = (sems.at[half] for sems in self.line_sems)
        held = part_of(self.held, 2 * row + half, BLOCK)
        return remote(held, part_of(self.last, half, BLOCK), send, recv, self.axis, self.axis.line(1))

    def give(self, chunk):
        @pl.when(self.axis.par != self.split(chunk)[1])
        def _():
            self.pair_copy(chunk).start()

    def take(self, chunk):
        row, par, half = self.split(chunk)

        @pl.when(self.axis.par == par)
        def _():
            self.pair_copy(chunk).wait_recv()

            def total(at):
                part = self.part[pl.ds(chunk * BLOCK + at, 32)].astype(F32)
                return part + self.held[pl.ds((2 * row + half) * BLOCK + at, 32)].astype(F32)

            @pl.when(self.axis.row == row)
            def _():
                @pl.loop(0, BLOCK // 32)
                def _(index):
                    at = pl.multiple_of(index * 32, 32)
                    self.out[pl.ds(half * BLOCK + at, 32)] = total(at)

            @pl.when(self.axis.row != row)
            def _():
                @pl.loop(0, BLOCK // 32)
                def _(index):
                    at = pl.multiple_of(index * 32, 32)
                    self.held[pl.ds((2 * row + half) * BLOCK + at, 32)] = total(at).astype(BF16)

                self.line_copy(chunk).start()

    def end(self, chunk):
        row, par, half = self.split(chunk)

        @pl.when(self.axis.par != par)
        def _():
            self.pair_copy(chunk).wait_send()

        @pl.when((self.axis.par == par) & (self.axis.row != row))
        def _():
            self.line_copy(chunk).wait_send()

        @pl.when((self.axis.par == par) & (self.axis.row == row))
        def _():
            self.line_copy(chunk).wait_recv()

            @pl.loop(0, BLOCK // 32)
            def _(index):
                at = pl.multiple_of(index * 32, 32)
                rows = pl.ds(half * BLOCK + at, 32)
                self.out[rows] += self.last[rows].astype(F32)

WEIGHTS = ("w_query", "w_keyvalue", "w_up", "w_down", "w_out")
INPUTS = ("tokens", "cotangent") + WEIGHTS


def own_shapes(z):
    wide_rows = (z.rows, z.model)
    return dict(
        params=((8, z.model), F32), cosine=((z.rows, 128), F32), sine=((z.rows, 128), F32),
        normed1=(wide_rows, BF16), normed2=(wide_rows, BF16),
        queries=((z.rows // BLOCK, z.stack, 128), BF16), keys=((z.rows, 128), BF16), values=((z.rows, 128), BF16),
        scores=((z.used // BLOCK * z.stack, BLOCK), F32), attended=((z.rows, z.wide), BF16), hidden=((z.rows, z.units), BF16),
        slope=((z.rows, z.units), BF16), d_attended=((z.used // BLOCK, z.stack, 128), BF16),
        d_query=((z.used, z.wide), BF16), d_keyvalue=((z.used, 128), BF16), d_norms=((4, 8, z.model), F32),
    )


class Names:
    def __init__(self, names, refs):
        self.__dict__.update(zip(names, refs, strict=True))


def fused_specs(z):
    half, model = z.nd // 2, z.model
    columns = dict(zip(WEIGHTS, (z.wide, 128, z.units, z.units, z.wide)))
    arrays = own_shapes(z)
    arrays.update(pack_query=((z.own, z.wide), BF16), pack_out=((z.own, z.wide), BF16))
    arrays.update(tokens=((z.rows, model), BF16), cotangent=((z.rows, model), BF16))
    arrays.update({name: ((model, columns[name]), BF16) for name in WEIGHTS})
    arrays.update(mixed=((z.rows, model), BF16), held_mixed=((z.rows // 2, model), BF16))
    arrays.update(last_mixed=((z.slots, model), BF16), held_scaled=((z.rows // 2, model), BF16))
    arrays.update(last_scaled=((z.slots, model), BF16))
    for name in WEIGHTS:
        arrays["g_" + name] = ((model, columns[name]), BF16)
        arrays["held_" + name] = ((half * z.own, columns[name]), BF16)
        arrays["last_" + name] = ((max(half - 1, 1) * z.own, columns[name]), BF16)
    arrays.update(g_norms=((z.nd * 8, z.own), F32), held_norms=((half * 8, z.own), F32))
    arrays.update(last_norms=((max(half - 1, 1) * 8, z.own), F32))
    semaphores = dict(send_mixed=z.nt, recv_mixed=z.nt, send_norms=z.nd, recv_norms=z.nd)
    for name in INPUTS:
        count = z.nd if name in WEIGHTS else z.nt
        semaphores.update({"send_" + name: count // 2 * 3, "recv_" + name: count})
    for name in WEIGHTS:
        semaphores.update({"out_" + name: z.nd, "in_" + name: z.nd})
    semaphores.update(pair_send=4, pair_recv=4, line_send=2, line_recv=2, local=len(INPUTS))
    semaphores.update(share_send=2 * z.nt, share_recv=2 * z.nt)
    return arrays, semaphores


OUTPUTS = ("mixed_sum", "scaled_sum", "s_w_query", "s_w_out", "s_w_up", "s_w_down", "shared_kv", "shared_norms")


def fused_kernel(z, names, *refs):
    it = Names(("seq", "norms") + tuple("i_" + n for n in INPUTS) + OUTPUTS + names, refs)
    dp, tensor = Axis("dp", z.nd), Axis("tensor", z.nt)
    rows, model, used, slots = z.rows, z.model, z.used, z.slots
    core = Core(z.heads, it.seq[0, 0], **{n: getattr(it, n) for n in tuple(own_shapes(z)) + INPUTS}, grad=it.cotangent, scaled=it.tokens)
    barrier = pltpu.get_barrier_semaphore()
    expected = dp.greet(barrier) + tensor.greet(barrier)

    width = z.heads * 64
    pad = jnp.zeros((z.own, z.wide - width), BF16)
    lane = lanes_of(z.own)
    first = width // 128 * 128
    tail = jnp.concatenate([it.i_w_query[:, first:].astype(F32), pad.astype(F32)], axis=1)
    it.pack_query[:, :first] = it.i_w_query[:, :first]
    it.pack_query[:, first:] = jnp.where(lane < width - first, tail, it.norms[...].astype(F32)).astype(BF16)
    it.pack_out[:, :first] = it.i_w_out[:, :first]
    it.pack_out[:, first:] = jnp.concatenate([it.i_w_out[:, first:], pad], axis=1)
    sources = dict(w_query=it.pack_query, w_out=it.pack_out)
    g = {}
    for i, name in enumerate(INPUTS):
        axis = tensor if name in ("tokens", "cotangent") else dp
        source = sources.get(name, getattr(it, "i_" + name))
        sems = getattr(it, "send_" + name), getattr(it, "recv_" + name)
        g[name] = Gather(axis, source, getattr(it, name), *sems, it.local.at[i])
    pl.semaphore_wait(barrier, expected)

    def hand_on(names, distance):
        for name in names:
            g[name].pass_on(distance)

    small = ("w_query", "w_keyvalue")
    for name in ("tokens", "cotangent"):
        g[name].start_line()
        g[name].start_pair()
    for name in small:
        g[name].start_line()
        g[name].start_pair()
    g["w_up"].start_pair()
    for name in INPUTS:
        g[name].copy.start()
    core.tables(0)
    hand_on(small, 1)
    g["w_up"].start_line()
    core.tables(1)
    hand_on(small, 2)
    g["w_down"].start_pair()
    hand_on(small, 3)
    hand_on(("w_up",), 1)
    g["w_down"].start_line()
    for name in small:
        g[name].arrive()
    core.unpack_params()

    def enter(slot):
        for part in range(slots // BLOCK):
            core.normalize(slot * (slots // BLOCK) + part)
            core.project(slot * (slots // BLOCK) + part)

    g["tokens"].copy.wait()

    @pl.loop(0, 4)
    def _(index):
        @pl.when(index == 1)
        def _():
            g["tokens"].pair_arrived(tensor.row)
            hand_on(("w_up",), 2)
            g["w_out"].start_pair()

        @pl.when(index == 2)
        def _():
            hand_on(("w_up",), 3)
            hand_on(("w_down",), 1)
            g["w_out"].start_line()
            g["tokens"].pass_on(1)
            g["tokens"].leave()

        @pl.when(index == 3)
        def _():
            g["tokens"].pair_arrived(1 - tensor.row)
            hand_on(("w_down",), 2)

        enter(tensor.me + lax.rem(index, 2) * (tensor.pair - tensor.me) + index // 2 * (tensor.line(1) - tensor.me))

    for block in range(rows // BLOCK):
        core.attend(block)
        if block == 3:
            hand_on(("w_down",), 3)
            hand_on(("w_out",), 1)
        if block == 5:
            hand_on(("w_out",), 2)
    hand_on(("w_out",), 3)
    g["w_up"].arrive()

    @pl.loop(0, rows // slots)
    def _(index):
        core.feed(pl.ds(pl.multiple_of(index * slots, slots), slots))

    g["cotangent"].pass_on(1)
    g["w_down"].arrive()
    g["cotangent"].arrive()
    g["cotangent"].leave()

    quarter = used // 4

    @pl.loop(0, 4)
    def _(index):
        first = pl.multiple_of(index * quarter, quarter)
        core.mask(pl.ds(first, quarter), first, quarter)

    r = {}
    for name in WEIGHTS:
        out = getattr(it, "s_" + name) if name != "w_keyvalue" else it.shared_kv.at[tensor.me]
        some = [getattr(it, kind + name) for kind in ("g_", "held_", "last_", "out_", "in_")]
        r[name] = Reduce(dp, some[0], out, *some[1:])
    r["norms"] = Reduce(
        dp, it.g_norms, it.shared_norms.at[tensor.me], it.held_norms, it.last_norms, it.send_norms, it.recv_norms
    )
    r["mixed"] = Reduce(tensor, it.mixed, it.mixed_sum, it.held_mixed, it.last_mixed, it.send_mixed, it.recv_mixed)
    scaled = Stream(
        tensor, it.mixed, it.scaled_sum, it.held_scaled, it.last_scaled,
        it.pair_send, it.pair_recv, it.line_send, it.line_recv,
    )

    def weight_grad(name, left, right):
        @pl.loop(0, model // BLOCK)
        def _(index):
            at = pl.ds(pl.multiple_of(index * BLOCK, BLOCK), BLOCK)
            r[name].part[at] = dot_rows(left[:used, at], right[:used]).astype(BF16)

    weight_grad("w_down", core.grad, core.hidden)
    r["w_down"].start()
    weight_grad("w_out", core.grad, core.attended)
    r["w_out"].start()
    g["w_out"].arrive()

    @pl.loop(0, tensor.size)
    def _(index):
        row = lax.rem(index, tensor.half)
        par = jnp.where(index < tensor.half, 1 - tensor.par, tensor.par)
        at = pl.ds(pl.multiple_of((2 * row + par) * slots, slots), slots)
        it.mixed[at] = core.mix(at).astype(BF16)

        @pl.when(index < tensor.half)
        def _():
            r["mixed"].first(row).start()

    @pl.loop(0, 4)
    def _(index):
        core.feed_back(pl.ds(pl.multiple_of(index * quarter, quarter), quarter))

    weight_grad("w_up", core.normed2, core.slope)
    r["w_up"].start()
    r["mixed"].middle()

    @pl.loop(0, used // BLOCK)
    def _(block):
        core.attend_grad(block)

    r["w_down"].middle()
    for ref in (core.d_keys, core.d_values, core.d_norms, it.scaled_sum):
        ref[...] = jnp.zeros_like(ref)
    chunks = used // BLOCK

    @pl.loop(0, chunks)
    def _(index):
        block = chunks - 1 - index
        core.attend_back(block)
        part_of(it.mixed, block, BLOCK)[...] = core.input_grad(block).astype(BF16)
        scaled.give(block)

        @pl.when(index > 0)
        def _():
            scaled.take(block + 1)

        @pl.when(index == 1)
        def _():
            r["w_out"].middle()

        @pl.when(index == 3)
        def _():
            r["w_up"].middle()

    weight_grad("w_query", core.normed1, core.d_query)
    r["w_query"].start()
    weight_grad("w_keyvalue", core.normed1, core.d_keyvalue)
    r["w_keyvalue"].start()
    part = model // dp.size
    sums = jnp.concatenate([jnp.sum(core.d_norms[i], axis=0, keepdims=True) for i in range(4)] + [jnp.zeros((4, model), F32)])
    for i in range(dp.size):
        it.g_norms[i * 8 : (i + 1) * 8] = sums[:, i * part : (i + 1) * part]
    r["norms"].start()
    scaled.take(0)
    for name in ("w_query", "w_keyvalue", "norms"):
        r[name].middle()
    for name in ("w_keyvalue", "norms"):
        r[name].end()
    copies = []
    for i, ref in enumerate((it.shared_kv, it.shared_norms)):
        for step in range(1, tensor.size):
            peer = lax.rem(tensor.me + step, tensor.size)
            sems = [s.at[i * tensor.size + step] for s in (it.share_send, it.share_recv)]
            copies.append(remote(ref.at[tensor.me], ref.at[tensor.me], *sems, tensor, peer))
            copies[-1].start()
    for name in ("w_down", "w_out", "w_up", "mixed", "w_query"):
        r[name].end()
    @pl.loop(0, chunks)
    def _(index):
        scaled.end(chunks - 1 - index)

    for copy in copies:
        copy.wait()
    for name in INPUTS:
        if name in WEIGHTS:
            g[name].leave()


def finish_kernel(heads, seq, tokens, cotangent, *refs):
    sums = Names(OUTPUTS, refs[: len(OUTPUTS)])
    out_tokens, d_tokens, d_query, d_keyvalue, d_out, d_up, d_down, d_norms = refs[len(OUTPUTS) :]
    rows, chunk = tokens.shape[0], 128
    first_row = lax.axis_index("tensor") * rows

    @pl.loop(0, rows // chunk)
    def _(index):
        first = pl.multiple_of(index * chunk, chunk)
        at = pl.ds(first, chunk)
        token = tokens[at].astype(F32)
        out_tokens[at] = (token + sums.mixed_sum[at]).astype(BF16)
        centered = token - jnp.mean(token, axis=1, keepdims=True)
        inv_std = lax.rsqrt(jnp.mean(centered * centered, axis=1, keepdims=True) + EPS)
        scaled = centered * inv_std
        grad = sums.scaled_sum[at]
        row = lax.broadcasted_iota(jnp.int32, (chunk, 1), 0) + first + first_row
        own = jnp.where(row < seq[0, 0], cotangent[at].astype(F32), 0.0)
        inner = jnp.mean(grad * scaled, axis=1, keepdims=True)
        d_tokens[at] = own + inv_std * (grad - jnp.mean(grad, axis=1, keepdims=True) - scaled * inner)

    d_query[...] = sums.s_w_query[:, : heads * 64]
    d_out[...] = sums.s_w_out[:, : heads * 64]
    d_up[...] = sums.s_w_up[...]
    d_down[...] = sums.s_w_down[...]
    kv, norms = sums.shared_kv[0], sums.shared_norms[0]
    for t in range(1, sums.shared_kv.shape[0]):
        kv, norms = kv + sums.shared_kv[t], norms + sums.shared_norms[t]
    d_keyvalue[...] = kv
    d_norms[...] = norms


def plain_kernel(z, seq, *refs):
    named = dict(zip(INPUTS, refs))
    mixed, scaled_grad, g_query, g_keyvalue, g_out, g_up, g_down, g_norms = refs[len(INPUTS) : len(INPUTS) + 8]
    *own, grad, scaled = refs[len(INPUTS) + 8 :]
    named.update(zip(own_shapes(z), own), grad=grad, scaled=scaled)
    core = Core(z.heads, seq[0, 0], **named)
    rows, model, used = z.rows, z.model, z.used
    core.tables(0)
    core.tables(1)
    core.unpack_params()

    @pl.loop(0, rows // BLOCK)
    def _(block):
        core.normalize(block)
        core.project(block)

    for block in range(rows // BLOCK):
        core.attend(block)

    @pl.loop(0, rows // 512)
    def _(index):
        at = pl.ds(pl.multiple_of(index * 512, 512), 512)
        core.feed(at)
        mixed[at] = core.mix(at).astype(BF16)

    @pl.loop(0, 4)
    def _(index):
        first = pl.multiple_of(index * (used // 4), used // 4)
        core.mask(pl.ds(first, used // 4), first, used // 4)
        core.feed_back(pl.ds(first, used // 4))

    @pl.loop(0, used // BLOCK)
    def _(block):
        core.attend_grad(block)

    @pl.loop(0, model // BLOCK)
    def _(index):
        at = pl.ds(pl.multiple_of(index * BLOCK, BLOCK), BLOCK)
        grad = core.grad[:used, at]
        g_down[at] = dot_rows(grad, core.hidden[:used]).astype(BF16)
        g_out[at] = dot_rows(grad, core.attended[:used]).astype(BF16)
        g_up[at] = dot_rows(core.normed2[:used, at], core.slope[:used]).astype(BF16)

    for ref in (core.d_keys, core.d_values, core.d_norms):
        ref[...] = jnp.zeros_like(ref)
    @pl.loop(0, used // BLOCK)
    def _(index):
        block = used // BLOCK - 1 - index
        core.attend_back(block)
        part_of(scaled_grad, block, BLOCK)[...] = core.input_grad(block).astype(BF16)

    scaled_grad[used:] = jnp.zeros((rows - used, model), BF16)

    @pl.loop(0, model // BLOCK)
    def _(index):
        at = pl.ds(pl.multiple_of(index * BLOCK, BLOCK), BLOCK)
        normed = core.normed1[:used, at]
        g_query[at] = dot_rows(normed, core.d_query[:used]).astype(BF16)
        g_keyvalue[at] = dot_rows(normed, core.d_keyvalue[:used]).astype(BF16)

    for i in range(4):
        g_norms[i : i + 1] = jnp.sum(core.d_norms[i], axis=0, keepdims=True)


def run_plain(seq_lengths, norms, arrays, z):
    tokens, cotangent, w_query, w_keyvalue, w_up, w_down, w_out = arrays
    width, model = w_query.shape[1], tokens.shape[1]
    wide = z.wide
    pad = jnp.pad(w_query[:, width // 128 * 128 :], ((0, 0), (0, wide - width)))
    lane = lax.iota(jnp.int32, 128)[None]
    tail = jnp.where(lane < width % 128, pad, norms)
    query = jnp.concatenate([w_query[:, : width // 128 * 128], tail], axis=1)
    out = jnp.pad(w_out, ((0, 0), (0, wide - width)))
    gathered = [lax.all_gather(a, "tensor", axis=0, tiled=True) for a in (tokens, cotangent)]
    gathered += [lax.all_gather(a, "dp", axis=0, tiled=True) for a in (query, w_keyvalue, w_up, w_down, out)]
    shape = jax.ShapeDtypeStruct
    results = pl.pallas_call(
        functools.partial(plain_kernel, z),
        out_shape=[shape((z.rows, model), BF16)] * 2
        + [shape((model, n), BF16) for n in (wide, 128, wide, z.units, z.units)]
        + [shape((4, model), F32)],
        in_specs=[pl.BlockSpec(memory_space=pltpu.SMEM)] + [INVMEM] * len(gathered),
        out_specs=[INVMEM] * 8,
        scratch_shapes=[pltpu.VMEM(*entry) for entry in own_shapes(z).values()] + [pltpu.VMEM((n, model), BF16) for n in (z.used, z.rows)],
        compiler_params=pltpu.CompilerParams(vmem_limit_bytes=67043328),
        name="plain_layer",
    )(seq_lengths, *gathered)
    names = ("tensor", "tensor") + ("dp",) * 5
    sums = [
        lax.psum_scatter(p.astype(F32), n, scatter_dimension=0, tiled=True) for p, n in zip(results[:7], names)
    ]
    norm_sums = lax.psum_scatter(results[7], "dp", scatter_dimension=1, tiled=True)
    shared_kv = lax.all_gather(sums[3], "tensor")
    shared_norms = lax.all_gather(jnp.pad(norm_sums, ((0, 4), (0, 0))), "tensor")
    return sums[0], sums[1], sums[2], sums[4], sums[5], sums[6], shared_kv, shared_norms


def run_whole(seq_lengths, norms, arrays, z):
    arrays_of, semaphores = fused_specs(z)
    shapes = [
        (z.slots, z.model), (z.slots, z.model), (z.own, z.wide), (z.own, z.wide), (z.own, z.units), (z.own, z.units),
        (z.nt, z.own, 128), (z.nt, 8, z.own),
    ]
    scratch = [pltpu.VMEM(*entry) for entry in arrays_of.values()]
    scratch += [pltpu.SemaphoreType.DMA((count,)) for count in semaphores.values()]
    return pl.pallas_call(
        functools.partial(fused_kernel, z, tuple(arrays_of) + tuple(semaphores)),
        out_shape=[jax.ShapeDtypeStruct(shape, F32) for shape in shapes],
        in_specs=[pl.BlockSpec(memory_space=pltpu.SMEM)] + [INVMEM] * (1 + len(arrays)),
        out_specs=[INVMEM] * len(shapes),
        scratch_shapes=scratch,
        compiler_params=pltpu.CompilerParams(collective_id=0, has_side_effects=True, vmem_limit_bytes=67043328),
        name="layer",
    )(seq_lengths, norms, *arrays)


def run_layer(seq_lengths, norms, arrays, nd, nt):
    tokens, _, w_query, w_keyvalue, w_up, _, _ = arrays
    heads, own, units = w_query.shape[1] // 64, w_query.shape[0], w_up.shape[1]
    slots, model = tokens.shape
    z = types.SimpleNamespace(
        nd=nd, nt=nt, heads=heads, rows=slots * nt, model=model, stack=heads * BLOCK, units=units, used=SEQ_MOST,
        wide=(heads * 64 + 4 + 127) // 128 * 128, own=own, slots=slots,
    )
    run = run_whole if own % 32 == 0 and slots == 2 * BLOCK and nt == 4 else run_plain
    sums = run(seq_lengths, norms, arrays, z)
    shape = jax.ShapeDtypeStruct
    results = pl.pallas_call(
        functools.partial(finish_kernel, heads),
        out_shape=[
            shape((slots, model), BF16), shape((slots, model), F32), shape((own, heads * 64), F32), shape((own, 128), F32),
            shape((own, heads * 64), F32), shape((own, units), F32), shape((own, units), F32), shape((8, own), F32),
        ],
        in_specs=[pl.BlockSpec(memory_space=pltpu.SMEM)] + [INVMEM] * (2 + len(sums)),
        out_specs=[INVMEM] * 8,
        compiler_params=pltpu.CompilerParams(vmem_limit_bytes=67043328),
        name="finish",
    )(seq_lengths, *arrays[:2], *sums)
    return tuple(results[:7]) + tuple(results[7][i] for i in range(4))


def shards(
    tokens,
    cotangent,
    seq_lengths,
    w_query,
    w_keyvalue,
    w_out,
    w_up,
    w_down,
    norm1_gain,
    norm1_bias,
    norm2_gain,
    norm2_bias,
):
    start = w_query.shape[1] % 128
    norms = jnp.stack([norm1_gain, norm1_bias, norm2_gain, norm2_bias], axis=1)
    norms = jnp.pad(norms, ((0, 0), (start, 124 - start)))
    arrays = (tokens, cotangent, w_query, w_keyvalue, w_up, w_down, w_out)
    return run_layer(seq_lengths, norms, arrays, lax.axis_size("dp"), lax.axis_size("tensor"))


def solution(mesh):
    return jax.shard_map(
        shards,
        mesh=mesh,
        in_specs=(
            P(("dp", "tensor"), None),
            P(("dp", "tensor"), None),
            P("dp", None),
            P("dp", "tensor"),
            P("dp", None),
            P("dp", "tensor"),
            P("dp", "tensor"),
            P("dp", "tensor"),
            P("dp"),
            P("dp"),
            P("dp"),
            P("dp"),
        ),
        out_specs=(
            P(("dp", "tensor"), None),
            P(("dp", "tensor"), None),
            P("dp", "tensor"),
            P("dp", None),
            P("dp", "tensor"),
            P("dp", "tensor"),
            P("dp", "tensor"),
            P("dp"),
            P("dp"),
            P("dp"),
            P("dp"),
        ),
        check_vma=False,
    )
```

```python
import functools
import math
import types

import jax
import jax.numpy as jnp
from jax import lax
from jax.experimental import pallas as pl
from jax.experimental.pallas import tpu as pltpu
from jax.sharding import PartitionSpec as P

ROT = 16
SEQ_LEAST = 1024
SEQ_MOST = 1792
BLOCK = 256
EPS = 1e-05
NEG = -1e30
F32 = jnp.float32
BF16 = jnp.bfloat16


def dot(left, right):
    return jnp.dot(left, right, preferred_element_type=F32)


def dot_rows(left, right):
    return lax.dot_general(left, right, (((0,), (0,)), ((), ())), preferred_element_type=F32)


def dot_cols(left, right):
    return lax.dot_general(left, right, (((1,), (1,)), ((), ())), preferred_element_type=F32)


def lanes_of(rows):
    return lax.broadcasted_iota(jnp.int32, (rows, 128), 1)


def swap_halves(x, lane):
    return jnp.where(lane < ROT // 2, pltpu.roll(x, 128 - ROT // 2, 1), pltpu.roll(x, ROT // 2, 1))


def three_parts(x):
    high = x.astype(BF16).astype(F32)
    middle = (x - high).astype(BF16).astype(F32)
    return high, middle, x - high - middle


def unit_heads(wide, heads):
    pieces = []
    for h in range(heads):
        piece = wide[:, h // 2 * 128 : h // 2 * 128 + 128]
        pieces.append(piece if h % 2 == 0 else pltpu.roll(piece, 64, 1))
    return pieces


def join_heads(pieces, lane):
    wide = []
    for h in range(0, len(pieces), 2):
        second = pltpu.roll(pieces[h + 1], 64, 1) if h + 1 < len(pieces) else jnp.zeros_like(pieces[h])
        wide.append(jnp.where(lane < 64, pieces[h], second))
    return jnp.concatenate(wide, axis=1)


class Core:
    def __init__(self, heads, length, **refs):
        self.heads, self.length = heads, length
        self.__dict__.update(refs)
        stack, used = heads * BLOCK, self.d_keyvalue.shape[0]
        self.d_query = self.attended
        self.d_stack = self.scores.at[0:stack, 0:128]
        self.d_keys = self.scores.at[stack : stack + used, 0:128]
        self.d_values = self.scores.at[stack : stack + used, 128:256]

    def past(self, first, shape, axis):
        return lax.broadcasted_iota(jnp.int32, shape, axis) + first >= self.length

    def tables(self, part):
        count = self.cosine.shape[0] // BLOCK // 2

        @pl.loop(part * count, part * count + count)
        def _(index):
            at = pl.ds(pl.multiple_of(index * BLOCK, BLOCK), BLOCK)
            lane = lanes_of(BLOCK)
            row = lax.broadcasted_iota(jnp.int32, (BLOCK, 128), 0) + index * BLOCK
            position = jnp.where(row >= self.length, row - self.length, row).astype(F32)
            exponent = jnp.where(lane < ROT // 2, lane, lane - ROT // 2).astype(F32) * (-2.0 / ROT)
            angle = position * jnp.exp(exponent * math.log(10000.0))
            sine = jnp.sin(angle)
            self.cosine[at] = jnp.where(lane < ROT, jnp.cos(angle), 1.0)
            self.sine[at] = jnp.where(lane < ROT // 2, -sine, jnp.where(lane < ROT, sine, 0.0))

    def unpack_params(self):
        start = self.heads * 64
        turned = self.w_query[:, start // 128 * 128 : start // 128 * 128 + 128].T.astype(F32)
        self.params[0:4] = turned[start % 128 : start % 128 + 4]

    def normalize(self, block):
        at = pl.ds(pl.multiple_of(block * BLOCK, BLOCK), BLOCK)
        x = self.tokens[at].astype(F32)
        centered = x - jnp.mean(x, axis=1, keepdims=True)
        scaled = centered * lax.rsqrt(jnp.mean(centered * centered, axis=1, keepdims=True) + EPS)
        gain1, bias1, gain2, bias2 = (self.params[i : i + 1] for i in range(4))
        self.scaled[at] = scaled.astype(BF16)
        self.normed1[at] = (scaled * gain1 + bias1).astype(BF16)
        self.normed2[at] = (scaled * gain2 + bias2).astype(BF16)

    def project(self, block):
        first = pl.multiple_of(block * BLOCK, BLOCK)
        at = pl.ds(first, BLOCK)
        lane = lanes_of(BLOCK)
        cosine, sine = self.cosine[at], self.sine[at]
        past = self.past(first, (BLOCK, 128), 0)
        normed = self.normed1[at]
        key_value = dot(normed, self.w_keyvalue[...])
        keys = key_value * cosine + swap_halves(key_value, lane) * sine
        hidden_key = jnp.where(past, 0.0, NEG)
        extra = jnp.where(lane == 64, hidden_key, jnp.where(lane < 68, -1.0, 0.0))
        self.keys[at] = jnp.where(lane < 64, keys, extra).astype(BF16)
        ones = jnp.where(lane < 67, 1.0, 0.0)
        self.values[at] = jnp.where(lane < 64, pltpu.roll(key_value, 64, 1), ones).astype(BF16)
        query = dot(normed, self.w_query[...])
        flag = jnp.where((lane == 64) & past, 1.0, 0.0)
        for h, piece in enumerate(unit_heads(query, self.heads)):
            turned = (piece * cosine + swap_halves(piece, lane) * sine).astype(BF16).astype(F32)
            turned = turned * (64 ** (-0.5))
            self.queries[block, h * BLOCK : (h + 1) * BLOCK] = jnp.where(lane < 64, turned, flag).astype(BF16)

    def key_blocks(self, block):
        first = SEQ_LEAST // BLOCK if block * BLOCK >= SEQ_MOST else 0
        return range(first, block + 1)

    def attend(self, block):
        rows = self.heads * BLOCK
        query = self.queries[block]
        lane = lanes_of(rows)
        top = jnp.full((rows, BLOCK), -3e38, F32)
        for index, j in enumerate(self.key_blocks(block)):
            scores = dot_cols(query, self.keys[j * BLOCK : (j + 1) * BLOCK])
            if j == block:
                row = lax.rem(lax.broadcasted_iota(jnp.int32, (rows, BLOCK), 0), BLOCK)
                column = lax.broadcasted_iota(jnp.int32, (rows, BLOCK), 1)
                scores = jnp.where(column <= row, scores, NEG)
            self.scores[index * rows : (index + 1) * rows] = scores
            top = jnp.maximum(top, scores)
        top = jnp.max(top, axis=1, keepdims=True)
        total = jnp.zeros((rows, 128), F32)
        for index, j in enumerate(self.key_blocks(block)):
            probs = jnp.exp(self.scores[index * rows : (index + 1) * rows] - top).astype(BF16)
            total = total + dot(probs, self.values[j * BLOCK : (j + 1) * BLOCK])
        weight = jnp.sum(jnp.where(lane == 64, total, 0.0), axis=1, keepdims=True)
        output = total / weight
        pieces = [output[h * BLOCK : (h + 1) * BLOCK] for h in range(self.heads)]
        self.attended[block * BLOCK : (block + 1) * BLOCK] = join_heads(pieces, lanes_of(BLOCK)).astype(BF16)
        high, middle, low = three_parts(top + jnp.log(weight))
        parts = jnp.where(lane == 65, high, jnp.where(lane == 66, middle, low))
        self.queries[block] = jnp.where((lane >= 65) & (lane < 68), parts, query.astype(F32)).astype(BF16)

    def feed(self, at):
        up = dot(self.normed2[at], self.w_up[...])
        normal = 0.5 * (1.0 + lax.erf(up * (1.0 / math.sqrt(2.0))))
        self.hidden[at] = (up * normal).astype(BF16)
        density = jnp.exp(-0.5 * up * up) * (1.0 / math.sqrt(2.0 * math.pi))
        self.slope[at] = (normal + up * density).astype(BF16)

    def mix(self, at):
        return dot_cols(self.attended[at], self.w_out[...]) + dot_cols(self.hidden[at], self.w_down[...])

    def mask(self, at, first, rows):
        past = self.past(first, (rows, 1), 0)
        self.grad[at] = jnp.where(past, 0.0, self.cotangent[at].astype(F32)).astype(BF16)

    def feed_back(self, at):
        d_hidden = dot(self.grad[at], self.w_down[...])
        self.slope[at] = (d_hidden * self.slope[at].astype(F32)).astype(BF16)

    def attend_grad(self, block):
        first = pl.multiple_of(block * BLOCK, BLOCK)
        at = pl.ds(first, BLOCK)
        lane = lanes_of(BLOCK)
        grads = unit_heads(dot(self.grad[at], self.w_out[...]), self.heads)
        outputs = unit_heads(self.attended[at].astype(F32), self.heads)
        for h in range(self.heads):
            grad = grads[h].astype(BF16).astype(F32)
            delta = jnp.sum(jnp.where(lane < 64, grad * outputs[h], 0.0), axis=1, keepdims=True)
            high, middle, low = three_parts(-delta)
            parts = jnp.where(lane == 64, high, jnp.where(lane == 65, middle, jnp.where(lane == 66, low, 0.0)))
            self.d_attended[block, h * BLOCK : (h + 1) * BLOCK] = jnp.where(lane < 64, grad, parts).astype(BF16)

    def attend_back(self, block):
        rows = self.heads * BLOCK
        query, grad = self.queries[block], self.d_attended[block]

        def span(first, size, diagonal):
            at = pl.ds(pl.multiple_of(first, BLOCK), size)
            keys, values = self.keys[at], self.values[at]
            scores, d_probs = dot_cols(keys, query), dot_cols(values, grad)
            if diagonal:
                key = lax.broadcasted_iota(jnp.int32, (size, rows), 0)
                row = lax.rem(lax.broadcasted_iota(jnp.int32, (size, rows), 1), BLOCK) + (size - BLOCK)
                scores = jnp.where(key <= row, scores, NEG)
            probs = jnp.exp(scores)
            d_scores = (probs * d_probs).astype(BF16)
            self.d_values[at] += dot(probs.astype(BF16), grad)
            self.d_keys[at] += dot(d_scores, query)
            d_query = dot_rows(d_scores, keys)
            if diagonal:
                self.d_stack[...] = d_query
            else:
                self.d_stack[...] += d_query

        @pl.when(block % 2 == 1)
        def _():
            span((block - 1) * BLOCK, 2 * BLOCK, True)

        @pl.when(block % 2 == 0)
        def _():
            span(block * BLOCK, BLOCK, True)

        @pl.loop(0, block // 2)
        def _(index):
            span(index * 2 * BLOCK, 2 * BLOCK, False)

        at = pl.ds(pl.multiple_of(block * BLOCK, BLOCK), BLOCK)
        lane = lanes_of(BLOCK)
        cosine, sine = self.cosine[at], self.sine[at]

        def turn_back(x):
            return x * cosine - swap_halves(x, lane) * sine

        pieces = [
            turn_back(self.d_stack[h * BLOCK : (h + 1) * BLOCK]) * (64 ** (-0.5)) for h in range(self.heads)
        ]
        self.d_query[at] = join_heads(pieces, lane).astype(BF16)
        self.d_keyvalue[at] = jnp.where(
            lane < 64, turn_back(self.d_keys[at]), pltpu.roll(self.d_values[at], 64, 1)
        ).astype(BF16)

    def input_grad(self, block):
        at = pl.ds(pl.multiple_of(block * BLOCK, BLOCK), BLOCK)
        d_normed1 = dot_cols(self.d_query[at], self.w_query[...]) + dot_cols(self.d_keyvalue[at], self.w_keyvalue[...])
        d_normed2 = dot_cols(self.slope[at], self.w_up[...])
        scaled = self.scaled[at].astype(F32)
        for i, value in enumerate((d_normed1 * scaled, d_normed1, d_normed2 * scaled, d_normed2)):
            self.d_norms[i] += jnp.sum(value.reshape(BLOCK // 8, 8, -1), axis=0)
        return d_normed1 * self.params[0:1] + d_normed2 * self.params[2:3]


MESH = pl.DeviceIdType.MESH
INVMEM = pl.BlockSpec(memory_space=pltpu.VMEM)
ANY = pl.BlockSpec(memory_space=pl.ANY)


class Axis:
    def __init__(self, name, size):
        self.name, self.size, self.half = name, size, size // 2
        self.me = lax.axis_index(name)
        self.row, self.par = self.me // 2, self.me % 2
        self.pair = self.me + 1 - 2 * self.par

    def other_row(self, step):
        return lax.rem(self.row + step + self.half, self.half)

    def line(self, step):
        return self.other_row(step) * 2 + self.par

    def greet(self, barrier):
        for step in range(1, self.size):
            peer = lax.rem(self.me + step, self.size)
            pl.semaphore_signal(barrier, inc=1, device_id={self.name: peer}, device_id_type=MESH)
        return self.size - 1


def remote(src, dst, send, recv, axis, peer):
    return pltpu.make_async_remote_copy(
        src_ref=src, dst_ref=dst, send_sem=send, recv_sem=recv, device_id={axis.name: peer}, device_id_type=MESH
    )


def part_of(ref, index, rows):
    return ref.at[pl.ds(pl.multiple_of(index * rows, rows), rows)]


class Gather:
    def __init__(self, axis, src, dst, send, recv, local, part=0, parts=1):
        self.axis, self.dst, self.send, self.recv = axis, dst, send, recv
        self.half, self.part, self.parts = axis.half, part, parts
        self.src = part_of(src, part, src.shape[0] // parts)
        self.copy = pltpu.make_async_copy(self.src, self.slot(axis.me), local)

    def slot(self, index):
        return part_of(self.dst, index * self.parts + self.part, self.src.shape[0])

    def along(self, row, way, own=False):
        slot = self.slot(2 * row + self.axis.par)
        send = self.send.at[row if way > 0 else self.half + row]
        peer = self.axis.me + 2 * way
        return remote(self.src if own else slot, slot, send, self.recv.at[row], self.axis, peer)

    def across(self, row, own=False):
        slot = self.slot(2 * row + self.axis.par)
        sems = self.send.at[2 * self.half + row], self.recv.at[self.half + row]
        return remote(self.src if own else slot, slot, *sems, self.axis, self.axis.pair)

    def start_line(self):
        @pl.when(self.axis.row + 1 < self.half)
        def _():
            self.along(self.axis.row, 1, own=True).start()

        @pl.when(self.axis.row > 0)
        def _():
            self.along(self.axis.row, -1, own=True).start()

    def start_pair(self):
        self.across(self.axis.row, own=True).start()

    def pass_on(self, distance):
        if distance >= self.half:
            return
        me = self.axis.row

        @pl.when(me >= distance)
        def _():
            row = me - distance
            self.along(row, 1).wait_recv()

            @pl.when(me + 1 < self.half)
            def _():
                self.along(row, 1).start()

            self.across(row).start()

        @pl.when(me + distance < self.half)
        def _():
            row = me + distance
            self.along(row, -1).wait_recv()

            @pl.when(me > 0)
            def _():
                self.along(row, -1).start()

            self.across(row).start()

    def pair_arrived(self, row):
        slot = self.slot(2 * row + 1 - self.axis.par)
        sems = self.send.at[2 * self.half + row], self.recv.at[self.half + row]
        remote(slot, slot, *sems, self.axis, self.axis.pair).wait_recv()

    def arrive(self):
        self.copy.wait()
        for row in range(self.half):
            self.pair_arrived(row)

    def leave(self):
        for row in range(self.half):
            self.across(row).wait_send()

            @pl.when((self.axis.row >= row) & (self.axis.row + 1 < self.half))
            def _():
                self.along(row, 1).wait_send()

            @pl.when((self.axis.row <= row) & (self.axis.row > 0))
            def _():
                self.along(row, -1).wait_send()


class Reduce:
    def __init__(self, axis, part, out, held, last, send, recv):
        self.axis, self.part, self.out, self.held, self.last = axis, part, out, held, last
        self.send, self.recv, self.rows = send, recv, out.shape[0]
        self.chunk = 32 if self.rows % 32 == 0 else self.rows

    def first(self, row):
        block = part_of(self.part, 2 * row + 1 - self.axis.par, self.rows)
        held = part_of(self.held, row, self.rows)
        return remote(block, held, self.send.at[row], self.recv.at[row], self.axis, self.axis.pair)

    def second(self, step):
        index = self.axis.half + step
        block = part_of(self.held, self.axis.other_row(step), self.rows)
        last = part_of(self.last, step - 1, self.rows)
        return remote(block, last, self.send.at[index], self.recv.at[index], self.axis, self.axis.line(step))

    def start(self):
        for step in range(self.axis.half):
            self.first(self.axis.other_row(step + 1)).start()

    def chunks(self, body):
        @pl.loop(0, self.rows // self.chunk)
        def _(index):
            body(pl.multiple_of(index * self.chunk, self.chunk))

    def total(self, row, at):
        part = self.part[pl.ds((2 * row + self.axis.par) * self.rows + at, self.chunk)].astype(F32)
        return part + self.held[pl.ds(row * self.rows + at, self.chunk)].astype(F32)

    def middle(self):
        for step in range(1, self.axis.half):
            row = self.axis.other_row(step)
            self.first(row).wait()

            def add(at, row=row):
                self.held[pl.ds(row * self.rows + at, self.chunk)] = self.total(row, at).astype(self.held.dtype)

            self.chunks(add)
            self.second(step).start()

        self.first(self.axis.row).wait()

        def keep(at):
            self.out[pl.ds(at, self.chunk)] = self.total(self.axis.row, at)

        self.chunks(keep)

    def end(self):
        for step in range(1, self.axis.half):
            self.second(step).wait()

        def add(at):
            total = self.out[pl.ds(at, self.chunk)]
            for step in range(1, self.axis.half):
                total = total + self.last[pl.ds((step - 1) * self.rows + at, self.chunk)].astype(F32)
            self.out[pl.ds(at, self.chunk)] = total

        self.chunks(add)


class Stream:
    def __init__(self, axis, part, out, held, last, pair_send, pair_recv, line_send, line_recv):
        self.axis, self.part, self.out, self.held, self.last = axis, part, out, held, last
        self.pair_sems, self.line_sems = (pair_send, pair_recv), (line_send, line_recv)

    def split(self, chunk):
        return chunk // 4, chunk // 2 % 2, chunk % 2

    def pair_copy(self, chunk):
        row, _, half = self.split(chunk)
        index = 2 * row + half
        send, recv = (sems.at[index] for sems in self.pair_sems)
        held = part_of(self.held, index, BLOCK)
        return remote(part_of(self.part, chunk, BLOCK), held, send, recv, self.axis, self.axis.pair)

    def line_copy(self, chunk):
        row, _, half = self.split(chunk)
        send, recv = (sems.at[half] for sems in self.line_sems)
        held = part_of(self.held, 2 * row + half, BLOCK)
        return remote(held, part_of(self.last, half, BLOCK), send, recv, self.axis, self.axis.line(1))

    def give(self, chunk):
        @pl.when(self.axis.par != self.split(chunk)[1])
        def _():
            self.pair_copy(chunk).start()

    def take(self, chunk):
        row, par, half = self.split(chunk)

        @pl.when(self.axis.par == par)
        def _():
            self.pair_copy(chunk).wait_recv()

            def total(at):
                part = self.part[pl.ds(chunk * BLOCK + at, 32)].astype(F32)
                return part + self.held[pl.ds((2 * row + half) * BLOCK + at, 32)].astype(F32)

            @pl.when(self.axis.row == row)
            def _():
                @pl.loop(0, BLOCK // 32)
                def _(index):
                    at = pl.multiple_of(index * 32, 32)
                    self.out[pl.ds(half * BLOCK + at, 32)] = total(at)

            @pl.when(self.axis.row != row)
            def _():
                @pl.loop(0, BLOCK // 32)
                def _(index):
                    at = pl.multiple_of(index * 32, 32)
                    self.held[pl.ds((2 * row + half) * BLOCK + at, 32)] = total(at).astype(BF16)

                self.line_copy(chunk).start()

    def end(self, chunk):
        row, par, half = self.split(chunk)

        @pl.when(self.axis.par != par)
        def _():
            self.pair_copy(chunk).wait_send()

        @pl.when((self.axis.par == par) & (self.axis.row != row))
        def _():
            self.line_copy(chunk).wait_send()

        @pl.when((self.axis.par == par) & (self.axis.row == row))
        def _():
            self.line_copy(chunk).wait_recv()

            @pl.loop(0, BLOCK // 32)
            def _(index):
                at = pl.multiple_of(index * 32, 32)
                rows = pl.ds(half * BLOCK + at, 32)
                self.out[rows] += self.last[rows].astype(F32)

WEIGHTS = ("w_query", "w_keyvalue", "w_up", "w_down", "w_out")
INPUTS = ("tokens", "cotangent") + WEIGHTS
OUTPUTS = ("mixed_sum", "scaled_sum", "s_w_query", "s_w_out", "s_w_up", "s_w_down", "shared_kv", "shared_norms")


def own_shapes(z):
    wide_rows = (z.rows, z.model)
    return dict(
        params=((8, z.model), F32), cosine=((z.rows, 128), F32), sine=((z.rows, 128), F32),
        normed1=(wide_rows, BF16), normed2=(wide_rows, BF16),
        queries=((z.rows // BLOCK, z.stack, 128), BF16), keys=((z.rows, 128), BF16), values=((z.rows, 128), BF16),
        scores=((z.used // BLOCK * z.stack, BLOCK), F32), attended=((z.rows, z.wide), BF16), hidden=((z.rows, z.units), BF16),
        slope=((z.rows, z.units), BF16), d_attended=((z.used // BLOCK, z.stack, 128), BF16),
        d_keyvalue=((z.used, 128), BF16), d_norms=((4, 8, z.model), F32),
    )


class Names:
    def __init__(self, names, refs):
        self.__dict__.update(zip(names, refs, strict=True))


def output_shapes(z):
    return [
        (z.slots, z.model), (z.slots, z.model), (z.own, z.wide), (z.own, z.wide), (z.own, z.units), (z.own, z.units),
        (z.nt, z.own, 128), (z.nt, 8, z.own),
    ]


def fused_specs(z):
    half, model = z.nd // 2, z.model
    columns = dict(zip(WEIGHTS, (z.wide, 128, z.units, z.units, z.wide)))
    arrays = own_shapes(z)
    arrays.update({name: (shape, F32) for name, shape in zip(OUTPUTS, output_shapes(z))})
    arrays.update(pack_query=((z.own, z.wide), BF16), pack_out=((z.own, z.wide), BF16))
    arrays.update(tokens=((z.rows, model), BF16), cotangent=((z.rows, model), BF16))
    arrays.update({name: ((model, columns[name]), BF16) for name in WEIGHTS})
    arrays.update(mixed=((z.rows, model), BF16), held_mixed=((z.rows // 2, model), BF16))
    arrays.update(last_mixed=((z.slots, model), BF16), held_scaled=((z.rows // 2, model), BF16))
    arrays.update(last_scaled=((z.slots, model), BF16))
    for name in WEIGHTS:
        arrays["g_" + name] = ((model, columns[name]), BF16)
        arrays["held_" + name] = ((half * z.own, columns[name]), BF16)
        arrays["last_" + name] = ((max(half - 1, 1) * z.own, columns[name]), BF16)
    arrays.update(g_norms=((z.nd * 8, z.own), F32), held_norms=((half * 8, z.own), F32))
    arrays.update(last_norms=((max(half - 1, 1) * 8, z.own), F32))
    semaphores = dict(send_mixed=(z.nt,), recv_mixed=(z.nt,), send_norms=(z.nd,), recv_norms=(z.nd,))
    for name in INPUTS:
        count = z.nd if name in WEIGHTS else z.nt
        shape = (2, count) if name == "tokens" else (count,)
        semaphores.update({"send_" + name: shape[:-1] + (count // 2 * 3,), "recv_" + name: shape})
    for name in WEIGHTS:
        semaphores.update({"out_" + name: (z.nd,), "in_" + name: (z.nd,)})
    semaphores.update(pair_send=(4,), pair_recv=(4,), line_send=(2,), line_recv=(2,), local=(len(INPUTS) + 1,))
    semaphores.update(share_send=(2 * z.nt,), share_recv=(2 * z.nt,), store=(len(OUTPUTS),))
    return arrays, semaphores


def fused_kernel(z, names, *refs):
    vectors, refs = refs[1:5], refs[:1] + refs[5:]
    it = Names(("seq",) + tuple("i_" + n for n in INPUTS) + tuple("o_" + n for n in OUTPUTS) + names, refs)
    dp, tensor = Axis("dp", z.nd), Axis("tensor", z.nt)
    rows, model, used, slots = z.rows, z.model, z.used, z.slots
    core = Core(z.heads, it.seq[0, 0], **{n: getattr(it, n) for n in tuple(own_shapes(z)) + INPUTS}, grad=it.cotangent, scaled=it.tokens)
    barrier = pltpu.get_barrier_semaphore()
    expected = dp.greet(barrier) + tensor.greet(barrier)

    width = z.heads * 64
    pad = jnp.zeros((z.own, z.wide - width), BF16)
    lane = lanes_of(z.own)
    first = width // 128 * 128
    tail = jnp.concatenate([it.i_w_query[:, first:].astype(F32), pad.astype(F32)], axis=1)
    it.pack_query[:, :first] = it.i_w_query[:, :first]
    start = width - first
    turned = [v[...].astype(F32).reshape(1, z.own) for v in vectors]
    turned = jnp.concatenate([jnp.zeros((start, z.own), F32)] + turned + [jnp.zeros((124 - start, z.own), F32)])
    turned = jnp.concatenate([turned, jnp.zeros((128, 128 - z.own), F32)], axis=1).T[: z.own]
    it.pack_query[:, first:] = jnp.where(lane < start, tail, turned).astype(BF16)
    it.pack_out[:, :first] = it.i_w_out[:, :first]
    it.pack_out[:, first:] = jnp.concatenate([it.i_w_out[:, first:], pad], axis=1)
    sources = dict(w_query=it.pack_query, w_out=it.pack_out)
    g = {}
    for i, name in enumerate(INPUTS):
        axis = dp if name in WEIGHTS else tensor
        source = sources.get(name, getattr(it, "i_" + name))
        send, recv = getattr(it, "send_" + name), getattr(it, "recv_" + name)
        g[name] = Gather(axis, source, getattr(it, name), send, recv, it.local.at[i])
    tokens = [
        Gather(tensor, it.i_tokens, it.tokens, it.send_tokens.at[h], it.recv_tokens.at[h], it.local.at[len(INPUTS) * h], h, 2)
        for h in range(2)
    ]
    pl.semaphore_wait(barrier, expected)

    def hand_on(names, distance):
        for name in names:
            g[name].pass_on(distance)

    small = ("w_query", "w_keyvalue")
    for gather in tokens + [g["cotangent"]]:
        gather.start_line()
        gather.start_pair()
    for name in small:
        g[name].start_line()
        g[name].start_pair()
    g["w_up"].start_pair()
    for gather in tokens + [g[name] for name in INPUTS[1:]]:
        gather.copy.start()
    core.tables(0)
    hand_on(small, 1)
    g["w_up"].start_line()
    core.tables(1)
    hand_on(small, 2)
    hand_on(small, 3)
    hand_on(("w_up",), 1)
    g["w_down"].start_line()
    for name in small:
        g[name].arrive()
    core.unpack_params()

    for gather in tokens:
        gather.copy.wait()
    other, other_pair = tensor.line(1), tensor.line(1) + tensor.pair - tensor.me

    @pl.loop(0, 4)
    def _(index):
        @pl.when(index == 1)
        def _():
            for gather in tokens:
                gather.pair_arrived(tensor.row)
            hand_on(("w_up",), 2)
            g["w_down"].start_pair()
            g["w_out"].start_line()

        for half in range(2):

            @pl.when(index == 2 + half)
            def _():
                tokens[half].pass_on(1)
                if half == 0:
                    hand_on(("w_up",), 3)
                tokens[half].pair_arrived(1 - tensor.row)
                tokens[half].leave()

        late = index // 2
        first = jnp.where(index == 0, 2 * tensor.me, 2 * tensor.pair)
        blocks = [
            (1 - late) * first + late * (2 * other + index - 2),
            (1 - late) * (first + 1) + late * (2 * other_pair + index - 2),
        ]
        for block in blocks:
            core.normalize(block)
            core.project(block)

        @pl.when(index == 2)
        def _():
            hand_on(("w_down",), 1)
            g["w_out"].start_pair()

    hand_on(("w_down",), 2)
    g["w_up"].arrive()

    @pl.loop(0, rows // slots)
    def _(index):
        core.feed(pl.ds(pl.multiple_of(index * slots, slots), slots))
        for step, (name, distance) in enumerate((("w_down", 3), ("w_out", 1), ("w_out", 2), ("w_out", 3))):

            @pl.when(index == step)
            def _():
                hand_on((name,), distance)

    for block in range(rows // BLOCK):
        core.attend(block)
    g["cotangent"].pass_on(1)
    g["w_down"].arrive()
    g["cotangent"].arrive()
    g["cotangent"].leave()

    quarter = used // 4

    @pl.loop(0, 4)
    def _(index):
        first = pl.multiple_of(index * quarter, quarter)
        core.mask(pl.ds(first, quarter), first, quarter)

    r = {}
    for name in WEIGHTS:
        out = getattr(it, "s_" + name) if name != "w_keyvalue" else it.shared_kv.at[tensor.me]
        some = [getattr(it, kind + name) for kind in ("g_", "held_", "last_", "out_", "in_")]
        r[name] = Reduce(dp, some[0], out, *some[1:])
    r["norms"] = Reduce(
        dp, it.g_norms, it.shared_norms.at[tensor.me], it.held_norms, it.last_norms, it.send_norms, it.recv_norms
    )
    r["mixed"] = Reduce(tensor, it.mixed, it.mixed_sum, it.held_mixed, it.last_mixed, it.send_mixed, it.recv_mixed)
    scaled = Stream(
        tensor, it.mixed, it.scaled_sum, it.held_scaled, it.last_scaled,
        it.pair_send, it.pair_recv, it.line_send, it.line_recv,
    )

    def weight_grad(name, left, right):
        @pl.loop(0, model // BLOCK)
        def _(index):
            at = pl.ds(pl.multiple_of(index * BLOCK, BLOCK), BLOCK)
            r[name].part[at] = dot_rows(left[:used, at], right[:used]).astype(BF16)

    weight_grad("w_down", core.grad, core.hidden)
    r["w_down"].start()
    weight_grad("w_out", core.grad, core.attended)
    r["w_out"].start()
    g["w_out"].arrive()

    @pl.loop(0, tensor.size)
    def _(index):
        row = lax.rem(index, tensor.half)
        par = jnp.where(index < tensor.half, 1 - tensor.par, tensor.par)
        at = pl.ds(pl.multiple_of((2 * row + par) * slots, slots), slots)
        it.mixed[at] = core.mix(at).astype(BF16)

        @pl.when(index < tensor.half)
        def _():
            r["mixed"].first(row).start()

    @pl.loop(0, 4)
    def _(index):
        core.feed_back(pl.ds(pl.multiple_of(index * quarter, quarter), quarter))

    weight_grad("w_up", core.normed2, core.slope)
    r["w_up"].start()
    r["mixed"].middle()

    @pl.loop(0, used // BLOCK)
    def _(block):
        core.attend_grad(block)

    r["w_down"].middle()
    for ref in (core.d_keys, core.d_values, core.d_norms, it.scaled_sum):
        ref[...] = jnp.zeros_like(ref)
    chunks = used // BLOCK

    @pl.loop(0, chunks)
    def _(index):
        block = chunks - 1 - index
        core.attend_back(block)

        @pl.when(index > 0)
        def _():
            scaled.take(block + 1)

        part_of(it.mixed, block, BLOCK)[...] = core.input_grad(block).astype(BF16)
        scaled.give(block)

        @pl.when(index == 1)
        def _():
            r["w_out"].middle()

        @pl.when(index == 3)
        def _():
            r["w_up"].middle()

    weight_grad("w_keyvalue", core.normed1, core.d_keyvalue)
    r["w_keyvalue"].start()
    part = model // dp.size
    sums = jnp.concatenate([jnp.sum(core.d_norms[i], axis=0, keepdims=True) for i in range(4)] + [jnp.zeros((4, model), F32)])
    for i in range(dp.size):
        it.g_norms[i * 8 : (i + 1) * 8] = sums[:, i * part : (i + 1) * part]
    r["norms"].start()
    weight_grad("w_query", core.normed1, core.d_query)
    r["w_query"].start()
    stores = []

    def store(*some):
        for name in some:
            index = OUTPUTS.index(name)
            stores.append(pltpu.make_async_copy(getattr(it, name), getattr(it, "o_" + name), it.store.at[index]))
            stores[-1].start()

    scaled.take(0)
    r["mixed"].end()
    store("mixed_sum")
    for name in ("w_keyvalue", "norms"):
        r[name].middle()
    r["w_down"].end()
    r["w_query"].middle()
    r["w_out"].end()
    r["w_up"].end()
    store("s_w_down", "s_w_out", "s_w_up")
    for name in ("w_keyvalue", "norms"):
        r[name].end()
    copies = []
    for i, ref in enumerate((it.shared_kv, it.shared_norms)):
        for step in range(1, tensor.size):
            peer = lax.rem(tensor.me + step, tensor.size)
            sems = [s.at[i * tensor.size + step] for s in (it.share_send, it.share_recv)]
            copies.append(remote(ref.at[tensor.me], ref.at[tensor.me], *sems, tensor, peer))
            copies[-1].start()
    r["w_query"].end()
    store("s_w_query")

    @pl.loop(0, chunks)
    def _(index):
        scaled.end(chunks - 1 - index)

    store("scaled_sum")
    for copy in copies:
        copy.wait()
    store("shared_kv", "shared_norms")
    for name in WEIGHTS:
        g[name].leave()
    for copy in stores:
        copy.wait()


def finish_kernel(z, seq, tokens, cotangent, *refs):
    sums = Names(OUTPUTS, refs[: len(OUTPUTS)])
    out_tokens, d_tokens, d_query, d_keyvalue, d_out, d_up, d_down, *d_norms = refs[len(OUTPUTS) :]
    rows = tokens.shape[0]
    token = tokens[...].astype(F32)
    out_tokens[...] = (token + sums.mixed_sum[...]).astype(BF16)
    centered = token - jnp.mean(token, axis=1, keepdims=True)
    inv_std = lax.rsqrt(jnp.mean(centered * centered, axis=1, keepdims=True) + EPS)
    scaled = centered * inv_std
    grad = sums.scaled_sum[...]
    first_row = lax.axis_index("tensor") * z.slots + pl.program_id(0) * rows
    row = lax.broadcasted_iota(jnp.int32, (rows, 1), 0) + first_row
    own = jnp.where(row < seq[0, 0], cotangent[...].astype(F32), 0.0)
    inner = jnp.mean(grad * scaled, axis=1, keepdims=True)
    d_tokens[...] = own + inv_std * (grad - jnp.mean(grad, axis=1, keepdims=True) - scaled * inner)
    d_query[...] = sums.s_w_query[:, : z.heads * 64]
    d_out[...] = sums.s_w_out[:, : z.heads * 64]
    d_up[...] = sums.s_w_up[...]
    d_down[...] = sums.s_w_down[...]
    kv, norms = sums.shared_kv[0], sums.shared_norms[0]
    for t in range(1, z.nt):
        kv, norms = kv + sums.shared_kv[t], norms + sums.shared_norms[t]
    d_keyvalue[...] = kv
    for i in range(4):
        d_norms[i][...] = norms[i]


def plain_kernel(z, seq, *refs):
    named = dict(zip(INPUTS, refs))
    mixed, scaled_grad, g_query, g_keyvalue, g_out, g_up, g_down, g_norms = refs[len(INPUTS) : len(INPUTS) + 8]
    *own, grad, scaled = refs[len(INPUTS) + 8 :]
    named.update(zip(own_shapes(z), own), grad=grad, scaled=scaled)
    core = Core(z.heads, seq[0, 0], **named)
    rows, model, used = z.rows, z.model, z.used
    core.tables(0)
    core.tables(1)
    core.unpack_params()

    @pl.loop(0, rows // BLOCK)
    def _(block):
        core.normalize(block)
        core.project(block)

    for block in range(rows // BLOCK):
        core.attend(block)

    @pl.loop(0, rows // 512)
    def _(index):
        at = pl.ds(pl.multiple_of(index * 512, 512), 512)
        core.feed(at)
        mixed[at] = core.mix(at).astype(BF16)

    @pl.loop(0, 4)
    def _(index):
        first = pl.multiple_of(index * (used // 4), used // 4)
        core.mask(pl.ds(first, used // 4), first, used // 4)
        core.feed_back(pl.ds(first, used // 4))

    @pl.loop(0, used // BLOCK)
    def _(block):
        core.attend_grad(block)

    @pl.loop(0, model // BLOCK)
    def _(index):
        at = pl.ds(pl.multiple_of(index * BLOCK, BLOCK), BLOCK)
        grad = core.grad[:used, at]
        g_down[at] = dot_rows(grad, core.hidden[:used]).astype(BF16)
        g_out[at] = dot_rows(grad, core.attended[:used]).astype(BF16)
        g_up[at] = dot_rows(core.normed2[:used, at], core.slope[:used]).astype(BF16)

    for ref in (core.d_keys, core.d_values, core.d_norms):
        ref[...] = jnp.zeros_like(ref)
    @pl.loop(0, used // BLOCK)
    def _(index):
        block = used // BLOCK - 1 - index
        core.attend_back(block)
        part_of(scaled_grad, block, BLOCK)[...] = core.input_grad(block).astype(BF16)

    scaled_grad[used:] = jnp.zeros((rows - used, model), BF16)

    @pl.loop(0, model // BLOCK)
    def _(index):
        at = pl.ds(pl.multiple_of(index * BLOCK, BLOCK), BLOCK)
        normed = core.normed1[:used, at]
        g_query[at] = dot_rows(normed, core.d_query[:used]).astype(BF16)
        g_keyvalue[at] = dot_rows(normed, core.d_keyvalue[:used]).astype(BF16)

    for i in range(4):
        g_norms[i : i + 1] = jnp.sum(core.d_norms[i], axis=0, keepdims=True)


def run_plain(seq_lengths, norms, arrays, z):
    tokens, cotangent, w_query, w_keyvalue, w_up, w_down, w_out = arrays
    width, model = w_query.shape[1], tokens.shape[1]
    wide = z.wide
    pad = jnp.pad(w_query[:, width // 128 * 128 :], ((0, 0), (0, wide - width)))
    lane, start = lax.iota(jnp.int32, 128)[None], width % 128
    vectors = jnp.pad(jnp.stack(norms, axis=1), ((0, 0), (start, 124 - start)))
    tail = jnp.where(lane < start, pad, vectors)
    query = jnp.concatenate([w_query[:, : width // 128 * 128], tail], axis=1)
    out = jnp.pad(w_out, ((0, 0), (0, wide - width)))
    gathered = [lax.all_gather(a, "tensor", axis=0, tiled=True) for a in (tokens, cotangent)]
    gathered += [lax.all_gather(a, "dp", axis=0, tiled=True) for a in (query, w_keyvalue, w_up, w_down, out)]
    shape = jax.ShapeDtypeStruct
    results = pl.pallas_call(
        functools.partial(plain_kernel, z),
        out_shape=[shape((z.rows, model), BF16)] * 2
        + [shape((model, n), BF16) for n in (wide, 128, wide, z.units, z.units)]
        + [shape((4, model), F32)],
        in_specs=[pl.BlockSpec(memory_space=pltpu.SMEM)] + [INVMEM] * len(gathered),
        out_specs=[INVMEM] * 8,
        scratch_shapes=[pltpu.VMEM(*entry) for entry in own_shapes(z).values()] + [pltpu.VMEM((n, model), BF16) for n in (z.used, z.rows)],
        compiler_params=pltpu.CompilerParams(vmem_limit_bytes=67043328),
        name="plain_layer",
    )(seq_lengths, *gathered)
    names = ("tensor", "tensor") + ("dp",) * 5
    sums = [
        lax.psum_scatter(p.astype(F32), n, scatter_dimension=0, tiled=True) for p, n in zip(results[:7], names)
    ]
    norm_sums = lax.psum_scatter(results[7], "dp", scatter_dimension=1, tiled=True)
    shared_kv = lax.all_gather(sums[3], "tensor")
    shared_norms = lax.all_gather(jnp.pad(norm_sums, ((0, 4), (0, 0))), "tensor")
    return sums[0], sums[1], sums[2], sums[4], sums[5], sums[6], shared_kv, shared_norms


def run_whole(seq_lengths, norms, arrays, z):
    arrays_of, semaphores = fused_specs(z)
    scratch = [pltpu.VMEM(*entry) for entry in arrays_of.values()]
    scratch += [pltpu.SemaphoreType.DMA(shape) for shape in semaphores.values()]
    return pl.pallas_call(
        functools.partial(fused_kernel, z, tuple(arrays_of) + tuple(semaphores)),
        out_shape=[jax.ShapeDtypeStruct(shape, F32) for shape in output_shapes(z)],
        in_specs=[pl.BlockSpec(memory_space=pltpu.SMEM)]
        + [INVMEM] * 4
        + [INVMEM if packed else ANY for packed in (False, False, True, False, False, False, True)],
        out_specs=[ANY] * len(OUTPUTS),
        scratch_shapes=scratch,
        compiler_params=pltpu.CompilerParams(collective_id=0, has_side_effects=True, vmem_limit_bytes=67043328),
        name="layer",
    )(seq_lengths, *norms, *arrays)


def run_layer(seq_lengths, norms, arrays, nd, nt):
    tokens, _, w_query, w_keyvalue, w_up, _, _ = arrays
    heads, own, units = w_query.shape[1] // 64, w_query.shape[0], w_up.shape[1]
    slots, model = tokens.shape
    z = types.SimpleNamespace(
        nd=nd, nt=nt, heads=heads, rows=slots * nt, model=model, stack=heads * BLOCK, units=units, used=SEQ_MOST,
        wide=(heads * 64 + 4 + 127) // 128 * 128, own=own, slots=slots,
    )
    run = run_whole if own % 32 == 0 and slots == 2 * BLOCK and nt == 4 else run_plain
    sums = run(seq_lengths, norms, arrays, z)
    steps = 2 if own % 16 == 0 else 1
    shape = jax.ShapeDtypeStruct

    def block(rows, columns):
        return pl.BlockSpec((rows // steps, columns), lambda i: (i, 0))

    width = heads * 64
    token_rows = block(slots, model)
    weights = [block(own, n) for n in (z.wide, z.wide, units, units)]
    shared = [
        pl.BlockSpec((nt, own // steps, 128), lambda i: (0, i, 0)),
        pl.BlockSpec((nt, 8, own), lambda i: (0, 0, 0)),
    ]
    results = pl.pallas_call(
        functools.partial(finish_kernel, z),
        grid=(steps,),
        out_shape=[shape((slots, model), BF16), shape((slots, model), F32)]
        + [shape((own, n), F32) for n in (width, 128, width, units, units)]
        + [shape((own,), F32)] * 4,
        in_specs=[pl.BlockSpec(memory_space=pltpu.SMEM)] + [token_rows] * 4 + weights + shared,
        out_specs=[token_rows] * 2
        + [block(own, n) for n in (width, 128, width, units, units)]
        + [pl.BlockSpec((own,), lambda i: (0,))] * 4,
        compiler_params=pltpu.CompilerParams(vmem_limit_bytes=67043328),
        name="finish",
    )(seq_lengths, *arrays[:2], *sums)
    return tuple(results)


def shards(
    tokens,
    cotangent,
    seq_lengths,
    w_query,
    w_keyvalue,
    w_out,
    w_up,
    w_down,
    norm1_gain,
    norm1_bias,
    norm2_gain,
    norm2_bias,
):
    norms = (norm1_gain, norm1_bias, norm2_gain, norm2_bias)
    arrays = (tokens, cotangent, w_query, w_keyvalue, w_up, w_down, w_out)
    return run_layer(seq_lengths, norms, arrays, lax.axis_size("dp"), lax.axis_size("tensor"))


def solution(mesh):
    return jax.shard_map(
        shards,
        mesh=mesh,
        in_specs=(
            P(("dp", "tensor"), None),
            P(("dp", "tensor"), None),
            P("dp", None),
            P("dp", "tensor"),
            P("dp", None),
            P("dp", "tensor"),
            P("dp", "tensor"),
            P("dp", "tensor"),
            P("dp"),
            P("dp"),
            P("dp"),
            P("dp"),
        ),
        out_specs=(
            P(("dp", "tensor"), None),
            P(("dp", "tensor"), None),
            P("dp", "tensor"),
            P("dp", None),
            P("dp", "tensor"),
            P("dp", "tensor"),
            P("dp", "tensor"),
            P("dp"),
            P("dp"),
            P("dp"),
            P("dp"),
        ),
        check_vma=False,
    )
```

```python
import functools
import math
import types

import jax
import jax.numpy as jnp
from jax import lax
from jax.experimental import pallas as pl
from jax.experimental.pallas import tpu as pltpu
from jax.sharding import PartitionSpec as P

ROT = 16
SEQ_LEAST = 1024
SEQ_MOST = 1792
BLOCK = 256
WIDE = 3
EPS = 1e-05
NEG = -1e30
F32 = jnp.float32
BF16 = jnp.bfloat16


def dot(left, right):
    return jnp.dot(left, right, preferred_element_type=F32)


def dot_rows(left, right):
    return lax.dot_general(left, right, (((0,), (0,)), ((), ())), preferred_element_type=F32)


def dot_cols(left, right):
    return lax.dot_general(left, right, (((1,), (1,)), ((), ())), preferred_element_type=F32)


def lanes_of(rows):
    return lax.broadcasted_iota(jnp.int32, (rows, 128), 1)


def swap_halves(x, lane):
    return jnp.where(lane < ROT // 2, pltpu.roll(x, 128 - ROT // 2, 1), pltpu.roll(x, ROT // 2, 1))


def three_parts(x):
    high = x.astype(BF16).astype(F32)
    middle = (x - high).astype(BF16).astype(F32)
    return high, middle, x - high - middle


def unit_heads(wide, heads):
    pieces = []
    for h in range(heads):
        piece = wide[:, h // 2 * 128 : h // 2 * 128 + 128]
        pieces.append(piece if h % 2 == 0 else pltpu.roll(piece, 64, 1))
    return pieces


def join_heads(pieces, lane):
    wide = []
    for h in range(0, len(pieces), 2):
        second = pltpu.roll(pieces[h + 1], 64, 1) if h + 1 < len(pieces) else jnp.zeros_like(pieces[h])
        wide.append(jnp.where(lane < 64, pieces[h], second))
    return jnp.concatenate(wide, axis=1)


class Core:
    def __init__(self, heads, length, used, **refs):
        self.heads, self.length, self.used = heads, length, used
        self.__dict__.update(refs)
        stack = heads * BLOCK
        self.d_query = self.attended
        self.d_stack = self.scores.at[0:stack, 0:128]
        self.d_keys = self.scores.at[stack : stack + used, 0:128]
        self.d_values = self.scores.at[stack : stack + used, 128:256]

    def past(self, first, shape, axis):
        return lax.broadcasted_iota(jnp.int32, shape, axis) + first >= self.length

    def tables(self, part):
        count = self.cosine.shape[0] // BLOCK // 2

        @pl.loop(part * count, part * count + count)
        def _(index):
            at = pl.ds(pl.multiple_of(index * BLOCK, BLOCK), BLOCK)
            lane = lanes_of(BLOCK)
            row = lax.broadcasted_iota(jnp.int32, (BLOCK, 128), 0) + index * BLOCK
            position = jnp.where(row >= self.length, row - self.length, row).astype(F32)
            exponent = jnp.where(lane < ROT // 2, lane, lane - ROT // 2).astype(F32) * (-2.0 / ROT)
            angle = position * jnp.exp(exponent * math.log(10000.0))
            sine = jnp.sin(angle)
            self.cosine[at] = jnp.where(lane < ROT, jnp.cos(angle), 1.0)
            self.sine[at] = jnp.where(lane < ROT // 2, -sine, jnp.where(lane < ROT, sine, 0.0))

    def unpack_params(self):
        start = self.heads * 64
        turned = self.w_query[:, start // 128 * 128 : start // 128 * 128 + 128].T.astype(F32)
        self.params[0:4] = turned[start % 128 : start % 128 + 4]

    def normalize(self, block):
        at = pl.ds(pl.multiple_of(block * BLOCK, BLOCK), BLOCK)
        x = self.tokens[at].astype(F32)
        centered = x - jnp.mean(x, axis=1, keepdims=True)
        scaled = centered * lax.rsqrt(jnp.mean(centered * centered, axis=1, keepdims=True) + EPS)
        gain1, bias1, gain2, bias2 = (self.params[i : i + 1] for i in range(4))
        self.scaled[at] = scaled.astype(BF16)
        self.normed1[at] = (scaled * gain1 + bias1).astype(BF16)
        self.normed2[at] = (scaled * gain2 + bias2).astype(BF16)

    def project(self, block):
        first = pl.multiple_of(block * BLOCK, BLOCK)
        at = pl.ds(first, BLOCK)
        lane = lanes_of(BLOCK)
        cosine, sine = self.cosine[at], self.sine[at]
        past = self.past(first, (BLOCK, 128), 0)
        normed = self.normed1[at]
        key_value = dot(normed, self.w_keyvalue[...])
        keys = key_value * cosine + swap_halves(key_value, lane) * sine
        hidden_key = jnp.where(past, 0.0, NEG)
        extra = jnp.where(lane == 64, hidden_key, jnp.where(lane < 68, -1.0, 0.0))
        self.keys[at] = jnp.where(lane < 64, keys, extra).astype(BF16)
        ones = jnp.where(lane < 67, 1.0, 0.0)
        self.values[at] = jnp.where(lane < 64, pltpu.roll(key_value, 64, 1), ones).astype(BF16)
        query = dot(normed, self.w_query[...])
        flag = jnp.where((lane == 64) & past, 1.0, 0.0)
        for h, piece in enumerate(unit_heads(query, self.heads)):
            turned = (piece * cosine + swap_halves(piece, lane) * sine).astype(BF16).astype(F32)
            turned = turned * (64 ** (-0.5))
            self.queries[block, h * BLOCK : (h + 1) * BLOCK] = jnp.where(lane < 64, turned, flag).astype(BF16)

    def key_blocks(self, block):
        first = SEQ_LEAST // BLOCK if block * BLOCK >= SEQ_MOST else 0
        return range(first, block + 1)

    def attend(self, block):
        rows = self.heads * BLOCK
        query = self.queries[block]
        lane = lanes_of(rows)
        top = jnp.full((rows, BLOCK), -3e38, F32)
        for index, j in enumerate(self.key_blocks(block)):
            scores = dot_cols(query, self.keys[j * BLOCK : (j + 1) * BLOCK])
            if j == block:
                row = lax.rem(lax.broadcasted_iota(jnp.int32, (rows, BLOCK), 0), BLOCK)
                column = lax.broadcasted_iota(jnp.int32, (rows, BLOCK), 1)
                scores = jnp.where(column <= row, scores, NEG)
            self.scores[index * rows : (index + 1) * rows] = scores
            top = jnp.maximum(top, scores)
        top = jnp.max(top, axis=1, keepdims=True)
        total = jnp.zeros((rows, 128), F32)
        for index, j in enumerate(self.key_blocks(block)):
            probs = jnp.exp(self.scores[index * rows : (index + 1) * rows] - top).astype(BF16)
            total = total + dot(probs, self.values[j * BLOCK : (j + 1) * BLOCK])
        weight = jnp.sum(jnp.where(lane == 64, total, 0.0), axis=1, keepdims=True)
        output = total / weight
        pieces = [output[h * BLOCK : (h + 1) * BLOCK] for h in range(self.heads)]
        self.attended[block * BLOCK : (block + 1) * BLOCK] = join_heads(pieces, lanes_of(BLOCK)).astype(BF16)
        high, middle, low = three_parts(top + jnp.log(weight))
        parts = jnp.where(lane == 65, high, jnp.where(lane == 66, middle, low))
        self.queries[block] = jnp.where((lane >= 65) & (lane < 68), parts, query.astype(F32)).astype(BF16)

    def feed(self, at):
        up = dot(self.normed2[at], self.w_up[...])
        normal = 0.5 * (1.0 + lax.erf(up * (1.0 / math.sqrt(2.0))))
        self.hidden[at] = (up * normal).astype(BF16)
        density = jnp.exp(-0.5 * up * up) * (1.0 / math.sqrt(2.0 * math.pi))
        self.slope[at] = (normal + up * density).astype(BF16)

    def mix(self, at):
        return dot_cols(self.attended[at], self.w_out[...]) + dot_cols(self.hidden[at], self.w_down[...])

    def mask(self, at, first, rows):
        past = self.past(first, (rows, 1), 0)
        self.grad[at] = jnp.where(past, 0.0, self.cotangent[at].astype(F32)).astype(BF16)

    def feed_back(self, at):
        d_hidden = dot(self.grad[at], self.w_down[...])
        self.slope[at] = (d_hidden * self.slope[at].astype(F32)).astype(BF16)

    def d_attended(self, block, first, size):
        across = self.hidden.shape[1] // 128
        row = block // across * (self.heads * BLOCK) + first
        lane = lax.rem(block, across) * 128
        return self.hidden.at[pl.ds(pl.multiple_of(row, BLOCK), size), pl.ds(pl.multiple_of(lane, 128), 128)]

    def attend_grad(self, block):
        first = pl.multiple_of(block * BLOCK, BLOCK)
        at = pl.ds(first, BLOCK)
        lane = lanes_of(BLOCK)
        grads = unit_heads(dot(self.grad[at], self.w_out[...]), self.heads)
        outputs = unit_heads(self.attended[at].astype(F32), self.heads)
        for h in range(self.heads):
            grad = grads[h].astype(BF16).astype(F32)
            delta = jnp.sum(jnp.where(lane < 64, grad * outputs[h], 0.0), axis=1, keepdims=True)
            high, middle, low = three_parts(-delta)
            parts = jnp.where(lane == 64, high, jnp.where(lane == 65, middle, jnp.where(lane == 66, low, 0.0)))
            self.d_attended(block, h * BLOCK, BLOCK)[...] = jnp.where(lane < 64, grad, parts).astype(BF16)

    def attend_back(self, block):
        rows = self.heads * BLOCK
        query, grad = self.queries[block], self.d_attended(block, 0, rows)[...]

        def span(first, size, diagonal):
            at = pl.ds(pl.multiple_of(first, BLOCK), size)
            keys, values = self.keys[at], self.values[at]
            scores, d_probs = dot_cols(keys, query), dot_cols(values, grad)
            if diagonal:
                key = lax.broadcasted_iota(jnp.int32, (size, rows), 0)
                row = lax.rem(lax.broadcasted_iota(jnp.int32, (size, rows), 1), BLOCK) + (size - BLOCK)
                scores = jnp.where(key <= row, scores, NEG)
            probs = jnp.exp(scores)
            d_scores = (probs * d_probs).astype(BF16)
            self.d_values[at] += dot(probs.astype(BF16), grad)
            self.d_keys[at] += dot(d_scores, query)
            d_query = dot_rows(d_scores, keys)
            if diagonal:
                self.d_stack[...] = d_query
            else:
                self.d_stack[...] += d_query

        last = lax.rem(block, WIDE)
        for size in range(WIDE):

            @pl.when(last == size)
            def _():
                span((block - size) * BLOCK, (size + 1) * BLOCK, True)

        @pl.loop(0, block // WIDE)
        def _(index):
            span(index * WIDE * BLOCK, WIDE * BLOCK, False)

        at = pl.ds(pl.multiple_of(block * BLOCK, BLOCK), BLOCK)
        pieces = [
            self.turn_back(self.d_stack[h * BLOCK : (h + 1) * BLOCK], at) * (64 ** (-0.5)) for h in range(self.heads)
        ]
        self.d_query[at] = join_heads(pieces, lanes_of(BLOCK)).astype(BF16)

    def turn_back(self, x, at):
        return x * self.cosine[at] - swap_halves(x, lanes_of(BLOCK)) * self.sine[at]

    def keyvalue_grad(self):
        rows = self.d_keyvalue.shape[0]

        @pl.loop(0, self.used // BLOCK)
        def _(block):
            at = pl.ds(pl.multiple_of(block * BLOCK, BLOCK), BLOCK)
            d_keys = self.turn_back(self.d_keys[at], at)
            d_values = pltpu.roll(self.d_values[at], 64, 1)
            self.d_keyvalue[at] = jnp.where(lanes_of(BLOCK) < 64, d_keys, d_values).astype(BF16)

        self.d_keyvalue[self.used :] = jnp.zeros((rows - self.used, 128), BF16)

    def keyvalue_norms(self):
        weight = self.w_keyvalue[...].astype(F32)
        grad = self.d_keyvalue[: self.used]
        gain = jnp.sum(dot_rows(self.scaled[: self.used], grad) * weight, axis=1, keepdims=True)
        bias = jnp.sum(jnp.sum(grad.astype(F32), axis=0, keepdims=True) * weight, axis=1, keepdims=True)
        lane = lanes_of(weight.shape[0])
        turned = jnp.where(lane == 0, gain, bias).T
        return turned[0:1], turned[1:2]

    def input_grad(self, block):
        at = pl.ds(pl.multiple_of(block * BLOCK, BLOCK), BLOCK)
        d_normed1 = dot_cols(self.d_query[at], self.w_query[...])
        d_normed2 = dot_cols(self.slope[at], self.w_up[...])
        scaled = self.scaled[at].astype(F32)
        for i, value in enumerate((d_normed1 * scaled, d_normed1, d_normed2 * scaled, d_normed2)):
            self.d_norms[i] += jnp.sum(value.reshape(BLOCK // 8, 8, -1), axis=0)
        return d_normed1 * self.params[0:1] + d_normed2 * self.params[2:3]


MESH = pl.DeviceIdType.MESH
INVMEM = pl.BlockSpec(memory_space=pltpu.VMEM)
ANY = pl.BlockSpec(memory_space=pl.ANY)


class Axis:
    def __init__(self, name, size):
        self.name, self.size, self.half = name, size, size // 2
        self.me = lax.axis_index(name)
        self.row, self.par = self.me // 2, self.me % 2
        self.pair = self.me + 1 - 2 * self.par

    def other_row(self, step):
        return lax.rem(self.row + step + self.half, self.half)

    def line(self, step):
        return self.other_row(step) * 2 + self.par

    def greet(self, barrier):
        for step in range(1, self.size):
            peer = lax.rem(self.me + step, self.size)
            pl.semaphore_signal(barrier, inc=1, device_id={self.name: peer}, device_id_type=MESH)
        return self.size - 1


def remote(src, dst, send, recv, axis, peer):
    return pltpu.make_async_remote_copy(
        src_ref=src, dst_ref=dst, send_sem=send, recv_sem=recv, device_id={axis.name: peer}, device_id_type=MESH
    )


def part_of(ref, index, rows):
    return ref.at[pl.ds(pl.multiple_of(index * rows, rows), rows)]


class Gather:
    def __init__(self, axis, src, dst, send, recv, local, part=0, parts=1):
        self.axis, self.dst, self.send, self.recv = axis, dst, send, recv
        self.half, self.part, self.parts = axis.half, part, parts
        self.src = part_of(src, part, src.shape[0] // parts)
        self.copy = pltpu.make_async_copy(self.src, self.slot(axis.me), local)

    def slot(self, index):
        return part_of(self.dst, index * self.parts + self.part, self.src.shape[0])

    def along(self, row, way, own=False):
        slot = self.slot(2 * row + self.axis.par)
        send = self.send.at[row if way > 0 else self.half + row]
        peer = self.axis.me + 2 * way
        return remote(self.src if own else slot, slot, send, self.recv.at[row], self.axis, peer)

    def across(self, row, own=False):
        slot = self.slot(2 * row + self.axis.par)
        sems = self.send.at[2 * self.half + row], self.recv.at[self.half + row]
        return remote(self.src if own else slot, slot, *sems, self.axis, self.axis.pair)

    def start_line(self):
        @pl.when(self.axis.row + 1 < self.half)
        def _():
            self.along(self.axis.row, 1, own=True).start()

        @pl.when(self.axis.row > 0)
        def _():
            self.along(self.axis.row, -1, own=True).start()

    def start_pair(self):
        self.across(self.axis.row, own=True).start()

    def pass_on(self, distance):
        if distance >= self.half:
            return
        me = self.axis.row

        @pl.when(me >= distance)
        def _():
            row = me - distance
            self.along(row, 1).wait_recv()

            @pl.when(me + 1 < self.half)
            def _():
                self.along(row, 1).start()

            self.across(row).start()

        @pl.when(me + distance < self.half)
        def _():
            row = me + distance
            self.along(row, -1).wait_recv()

            @pl.when(me > 0)
            def _():
                self.along(row, -1).start()

            self.across(row).start()

    def pair_arrived(self, row):
        slot = self.slot(2 * row + 1 - self.axis.par)
        sems = self.send.at[2 * self.half + row], self.recv.at[self.half + row]
        remote(slot, slot, *sems, self.axis, self.axis.pair).wait_recv()

    def arrive(self):
        self.copy.wait()
        for row in range(self.half):
            self.pair_arrived(row)

    def leave(self):
        for row in range(self.half):
            self.across(row).wait_send()

            @pl.when((self.axis.row >= row) & (self.axis.row + 1 < self.half))
            def _():
                self.along(row, 1).wait_send()

            @pl.when((self.axis.row <= row) & (self.axis.row > 0))
            def _():
                self.along(row, -1).wait_send()


class Reduce:
    def __init__(self, axis, part, out, held, last, send, recv):
        self.axis, self.part, self.out, self.held, self.last = axis, part, out, held, last
        self.send, self.recv, self.rows = send, recv, out.shape[0]
        self.chunk = 32 if self.rows % 32 == 0 else self.rows

    def first(self, row):
        block = part_of(self.part, 2 * row + 1 - self.axis.par, self.rows)
        held = part_of(self.held, row, self.rows)
        return remote(block, held, self.send.at[row], self.recv.at[row], self.axis, self.axis.pair)

    def second(self, step):
        index = self.axis.half + step
        block = part_of(self.held, self.axis.other_row(step), self.rows)
        last = part_of(self.last, step - 1, self.rows)
        return remote(block, last, self.send.at[index], self.recv.at[index], self.axis, self.axis.line(step))

    def start(self):
        for step in range(self.axis.half):
            self.first(self.axis.other_row(step + 1)).start()

    def chunks(self, body):
        @pl.loop(0, self.rows // self.chunk)
        def _(index):
            body(pl.multiple_of(index * self.chunk, self.chunk))

    def total(self, row, at):
        part = self.part[pl.ds((2 * row + self.axis.par) * self.rows + at, self.chunk)].astype(F32)
        return part + self.held[pl.ds(row * self.rows + at, self.chunk)].astype(F32)

    def middle(self):
        for step in range(1, self.axis.half):
            row = self.axis.other_row(step)
            self.first(row).wait()

            def add(at, row=row):
                self.held[pl.ds(row * self.rows + at, self.chunk)] = self.total(row, at).astype(self.held.dtype)

            self.chunks(add)
            self.second(step).start()

        self.first(self.axis.row).wait()

        def keep(at):
            self.out[pl.ds(at, self.chunk)] = self.total(self.axis.row, at)

        self.chunks(keep)

    def end(self):
        for step in range(1, self.axis.half):
            self.second(step).wait()

        def add(at):
            total = self.out[pl.ds(at, self.chunk)]
            for step in range(1, self.axis.half):
                total = total + self.last[pl.ds((step - 1) * self.rows + at, self.chunk)].astype(F32)
            self.out[pl.ds(at, self.chunk)] = total

        self.chunks(add)


class Stream:
    def __init__(self, axis, part, out, held, last, pair_send, pair_recv, line_send, line_recv):
        self.axis, self.part, self.out, self.held, self.last = axis, part, out, held, last
        self.pair_sems, self.line_sems = (pair_send, pair_recv), (line_send, line_recv)

    def split(self, chunk):
        return chunk // 4, chunk // 2 % 2, chunk % 2

    def pair_copy(self, chunk):
        row, _, half = self.split(chunk)
        index = 2 * row + half
        send, recv = (sems.at[index] for sems in self.pair_sems)
        held = part_of(self.held, index, BLOCK)
        return remote(part_of(self.part, chunk, BLOCK), held, send, recv, self.axis, self.axis.pair)

    def line_copy(self, chunk):
        row, _, half = self.split(chunk)
        send, recv = (sems.at[half] for sems in self.line_sems)
        held = part_of(self.held, 2 * row + half, BLOCK)
        return remote(held, part_of(self.last, half, BLOCK), send, recv, self.axis, self.axis.line(1))

    def give(self, chunk):
        @pl.when(self.axis.par != self.split(chunk)[1])
        def _():
            self.pair_copy(chunk).start()

    def take(self, chunk):
        row, par, half = self.split(chunk)

        @pl.when(self.axis.par == par)
        def _():
            self.pair_copy(chunk).wait_recv()

            def total(at):
                part = self.part[pl.ds(chunk * BLOCK + at, 32)].astype(F32)
                return part + self.held[pl.ds((2 * row + half) * BLOCK + at, 32)].astype(F32)

            @pl.when(self.axis.row == row)
            def _():
                @pl.loop(0, BLOCK // 32)
                def _(index):
                    at = pl.multiple_of(index * 32, 32)
                    self.out[pl.ds(half * BLOCK + at, 32)] = total(at)

            @pl.when(self.axis.row != row)
            def _():
                @pl.loop(0, BLOCK // 32)
                def _(index):
                    at = pl.multiple_of(index * 32, 32)
                    self.held[pl.ds((2 * row + half) * BLOCK + at, 32)] = total(at).astype(BF16)

                self.line_copy(chunk).start()

    def end(self, chunk):
        row, par, half = self.split(chunk)

        @pl.when(self.axis.par != par)
        def _():
            self.pair_copy(chunk).wait_send()

        @pl.when((self.axis.par == par) & (self.axis.row != row))
        def _():
            self.line_copy(chunk).wait_send()

        @pl.when((self.axis.par == par) & (self.axis.row == row))
        def _():
            self.line_copy(chunk).wait_recv()

            @pl.loop(0, BLOCK // 32)
            def _(index):
                at = pl.multiple_of(index * 32, 32)
                rows = pl.ds(half * BLOCK + at, 32)
                self.out[rows] += self.last[rows].astype(F32)

WEIGHTS = ("w_query", "w_keyvalue", "w_up", "w_down", "w_out")
INPUTS = ("tokens", "cotangent") + WEIGHTS
OUTPUTS = ("mixed_sum", "scaled_sum", "s_w_query", "s_w_out", "s_w_up", "s_w_down", "shared_kv", "shared_norms")


def own_shapes(z):
    wide_rows = (z.rows, z.model)
    return dict(
        params=((8, z.model), F32), cosine=((z.rows, 128), F32), sine=((z.rows, 128), F32),
        normed1=(wide_rows, BF16), normed2=(wide_rows, BF16),
        queries=((z.rows // BLOCK, z.stack, 128), BF16), keys=((z.rows, 128), BF16), values=((z.rows, 128), BF16),
        scores=((z.used // BLOCK * z.stack, BLOCK), F32), attended=((z.rows, z.wide), BF16), hidden=((z.rows, z.units), BF16),
        slope=((z.rows, z.units), BF16), d_keyvalue=((z.rows, 128), BF16), d_norms=((4, 8, z.model), F32),
    )


class Names:
    def __init__(self, names, refs):
        self.__dict__.update(zip(names, refs, strict=True))


def output_shapes(z):
    return [
        (z.slots, z.model), (z.slots, z.model), (z.own, z.wide), (z.own, z.wide), (z.own, z.units), (z.own, z.units),
        (z.nt, z.own, 128), (z.nt, 8, z.own),
    ]


def fused_specs(z):
    half, model = z.nd // 2, z.model
    columns = dict(zip(WEIGHTS, (z.wide, 128, z.units, z.units, z.wide)))
    arrays = own_shapes(z)
    arrays.update({name: (shape, F32) for name, shape in zip(OUTPUTS, output_shapes(z))})
    arrays.update(pack_query=((z.own, z.wide), BF16), pack_out=((z.own, z.wide), BF16))
    arrays.update(tokens=((z.rows, model), BF16), cotangent=((z.rows, model), BF16))
    arrays.update({name: ((model, columns[name]), BF16) for name in WEIGHTS})
    arrays.update(mixed=((z.rows, model), BF16), held_mixed=((z.rows // 2, model), BF16))
    arrays.update(last_mixed=((z.slots, model), BF16), held_scaled=((z.rows // 2, model), BF16))
    arrays.update(last_scaled=((z.slots, model), BF16))
    for name in WEIGHTS:
        arrays["g_" + name] = ((model, columns[name]), BF16)
        arrays["held_" + name] = ((half * z.own, columns[name]), BF16)
        arrays["last_" + name] = ((max(half - 1, 1) * z.own, columns[name]), BF16)
    arrays.update(held_pack=((z.rows // 2, 128), BF16), last_pack=((z.slots, 128), BF16), pack_sum=((z.slots, 128), F32))
    arrays.update(g_norms=((z.nd * 8, z.own), F32), held_norms=((half * 8, z.own), F32))
    arrays.update(last_norms=((max(half - 1, 1) * 8, z.own), F32))
    semaphores = dict(send_mixed=(z.nt,), recv_mixed=(z.nt,), send_pack=(z.nt,), recv_pack=(z.nt,), send_norms=(z.nd,), recv_norms=(z.nd,))
    for name in INPUTS:
        count = z.nd if name in WEIGHTS else z.nt
        shape = (2, count) if name == "tokens" else (count,)
        semaphores.update({"send_" + name: shape[:-1] + (count // 2 * 3,), "recv_" + name: shape})
    for name in WEIGHTS:
        semaphores.update({"out_" + name: (z.nd,), "in_" + name: (z.nd,)})
    semaphores.update(pair_send=(4,), pair_recv=(4,), line_send=(2,), line_recv=(2,), local=(len(INPUTS) + 1,))
    semaphores.update(share_send=(2 * z.nt,), share_recv=(2 * z.nt,), store=(len(OUTPUTS),))
    return arrays, semaphores


def fused_kernel(z, names, *refs):
    vectors, refs = refs[1:5], refs[:1] + refs[5:]
    it = Names(("seq",) + tuple("i_" + n for n in INPUTS) + tuple("o_" + n for n in OUTPUTS) + names, refs)
    dp, tensor = Axis("dp", z.nd), Axis("tensor", z.nt)
    rows, model, used, slots = z.rows, z.model, z.used, z.slots
    core = Core(z.heads, it.seq[0, 0], z.used, **{n: getattr(it, n) for n in tuple(own_shapes(z)) + INPUTS}, grad=it.cotangent, scaled=it.tokens)
    barrier = pltpu.get_barrier_semaphore()
    expected = dp.greet(barrier) + tensor.greet(barrier)

    width = z.heads * 64
    pad = jnp.zeros((z.own, z.wide - width), BF16)
    lane = lanes_of(z.own)
    first = width // 128 * 128
    tail = jnp.concatenate([it.i_w_query[:, first:].astype(F32), pad.astype(F32)], axis=1)
    it.pack_query[:, :first] = it.i_w_query[:, :first]
    start = width - first
    turned = [v[...].astype(F32).reshape(1, z.own) for v in vectors]
    turned = jnp.concatenate([jnp.zeros((start, z.own), F32)] + turned + [jnp.zeros((124 - start, z.own), F32)])
    turned = jnp.concatenate([turned, jnp.zeros((128, 128 - z.own), F32)], axis=1).T[: z.own]
    it.pack_query[:, first:] = jnp.where(lane < start, tail, turned).astype(BF16)
    it.pack_out[:, :first] = it.i_w_out[:, :first]
    it.pack_out[:, first:] = jnp.concatenate([it.i_w_out[:, first:], pad], axis=1)
    sources = dict(w_query=it.pack_query, w_out=it.pack_out)
    g = {}
    for i, name in enumerate(INPUTS):
        axis = dp if name in WEIGHTS else tensor
        source = sources.get(name, getattr(it, "i_" + name))
        send, recv = getattr(it, "send_" + name), getattr(it, "recv_" + name)
        g[name] = Gather(axis, source, getattr(it, name), send, recv, it.local.at[i])
    tokens = [
        Gather(tensor, it.i_tokens, it.tokens, it.send_tokens.at[h], it.recv_tokens.at[h], it.local.at[len(INPUTS) * h], h, 2)
        for h in range(2)
    ]
    pl.semaphore_wait(barrier, expected)

    def hand_on(names, distance):
        for name in names:
            g[name].pass_on(distance)

    small = ("w_query", "w_keyvalue")
    for gather in tokens + [g["cotangent"]]:
        gather.start_line()
        gather.start_pair()
    for name in small:
        g[name].start_line()
        g[name].start_pair()
    g["w_up"].start_pair()
    for gather in tokens + [g[name] for name in INPUTS[1:]]:
        gather.copy.start()
    core.tables(0)
    hand_on(small, 1)
    g["w_up"].start_line()
    core.tables(1)
    hand_on(small, 2)
    hand_on(small, 3)
    hand_on(("w_up",), 1)
    g["w_down"].start_line()
    for name in small:
        g[name].arrive()
    core.unpack_params()

    for gather in tokens:
        gather.copy.wait()
    other, other_pair = tensor.line(1), tensor.line(1) + tensor.pair - tensor.me

    @pl.loop(0, 4)
    def _(index):
        @pl.when(index == 1)
        def _():
            for gather in tokens:
                gather.pair_arrived(tensor.row)
            hand_on(("w_up",), 2)
            g["w_down"].start_pair()
            g["w_out"].start_line()

        for half in range(2):

            @pl.when(index == 2 + half)
            def _():
                tokens[half].pass_on(1)
                if half == 0:
                    hand_on(("w_up",), 3)
                tokens[half].pair_arrived(1 - tensor.row)
                tokens[half].leave()

        late = index // 2
        first = jnp.where(index == 0, 2 * tensor.me, 2 * tensor.pair)
        blocks = [
            (1 - late) * first + late * (2 * other + index - 2),
            (1 - late) * (first + 1) + late * (2 * other_pair + index - 2),
        ]
        for block in blocks:
            core.normalize(block)
            core.project(block)

        @pl.when(index == 2)
        def _():
            hand_on(("w_down",), 1)
            g["w_out"].start_pair()

    hand_on(("w_down",), 2)
    g["w_up"].arrive()

    @pl.loop(0, rows // slots)
    def _(index):
        core.feed(pl.ds(pl.multiple_of(index * slots, slots), slots))
        for step, (name, distance) in enumerate((("w_down", 3), ("w_out", 1), ("w_out", 2), ("w_out", 3))):

            @pl.when(index == step)
            def _():
                hand_on((name,), distance)

    for block in range(rows // BLOCK):
        core.attend(block)
    g["cotangent"].pass_on(1)
    g["w_down"].arrive()
    g["cotangent"].arrive()
    g["cotangent"].leave()

    quarter = used // 4

    @pl.loop(0, 4)
    def _(index):
        first = pl.multiple_of(index * quarter, quarter)
        core.mask(pl.ds(first, quarter), first, quarter)

    r = {}
    for name in WEIGHTS:
        out = getattr(it, "s_" + name) if name != "w_keyvalue" else it.shared_kv.at[tensor.me]
        some = [getattr(it, kind + name) for kind in ("g_", "held_", "last_", "out_", "in_")]
        r[name] = Reduce(dp, some[0], out, *some[1:])
    r["norms"] = Reduce(
        dp, it.g_norms, it.shared_norms.at[tensor.me], it.held_norms, it.last_norms, it.send_norms, it.recv_norms
    )
    r["mixed"] = Reduce(tensor, it.mixed, it.mixed_sum, it.held_mixed, it.last_mixed, it.send_mixed, it.recv_mixed)
    r["pack"] = Reduce(
        tensor, core.d_keyvalue, it.pack_sum, it.held_pack, it.last_pack, it.send_pack, it.recv_pack
    )
    scaled = Stream(
        tensor, it.mixed, it.scaled_sum, it.held_scaled, it.last_scaled,
        it.pair_send, it.pair_recv, it.line_send, it.line_recv,
    )

    def weight_grad(name, left, right):
        half = model // 2

        @pl.loop(0, 2)
        def _(index):
            at = pl.ds(pl.multiple_of(index * half, 128), half)
            r[name].part[at] = dot_rows(left[:used, at], right[:used]).astype(BF16)

    weight_grad("w_down", core.grad, core.hidden)
    r["w_down"].start()
    weight_grad("w_out", core.grad, core.attended)
    r["w_out"].start()
    g["w_out"].arrive()

    @pl.loop(0, tensor.size)
    def _(index):
        row = lax.rem(index, tensor.half)
        par = jnp.where(index < tensor.half, 1 - tensor.par, tensor.par)
        at = pl.ds(pl.multiple_of((2 * row + par) * slots, slots), slots)
        it.mixed[at] = core.mix(at).astype(BF16)

        @pl.when(index < tensor.half)
        def _():
            r["mixed"].first(row).start()

    @pl.loop(0, 4)
    def _(index):
        core.feed_back(pl.ds(pl.multiple_of(index * quarter, quarter), quarter))

    weight_grad("w_up", core.normed2, core.slope)
    r["w_up"].start()
    r["mixed"].middle()

    @pl.loop(0, used // BLOCK)
    def _(block):
        core.attend_grad(block)

    r["w_down"].middle()
    for ref in (core.d_keys, core.d_values, core.d_norms, it.scaled_sum):
        ref[...] = jnp.zeros_like(ref)
    chunks = used // BLOCK

    def turn(index):
        return jnp.where(lax.rem(index, 2) == 0, chunks // 2, chunks - 1) - index // 2

    @pl.loop(0, chunks)
    def _(index):
        block = turn(index)
        core.attend_back(block)

        @pl.when(index > 0)
        def _():
            scaled.take(turn(index - 1))

        part_of(it.mixed, block, BLOCK)[...] = core.input_grad(block).astype(BF16)
        scaled.give(block)

        @pl.when(index == 1)
        def _():
            r["w_out"].middle()

        @pl.when(index == 3)
        def _():
            r["w_up"].middle()

    core.keyvalue_grad()
    r["pack"].start()
    weight_grad("w_keyvalue", core.normed1, core.d_keyvalue)
    r["w_keyvalue"].start()
    scaled.take(turn(chunks - 1))
    part = model // dp.size
    sums = [jnp.sum(core.d_norms[i], axis=0, keepdims=True) for i in range(4)]
    for i, more in enumerate(core.keyvalue_norms()):
        sums[i] = sums[i] + more
    sums = jnp.concatenate(sums + [jnp.zeros((4, model), F32)])
    for i in range(dp.size):
        it.g_norms[i * 8 : (i + 1) * 8] = sums[:, i * part : (i + 1) * part]
    r["norms"].start()
    r["pack"].middle()
    weight_grad("w_query", core.normed1, core.d_query)
    r["w_query"].start()
    stores = []

    def store(*some):
        for name in some:
            index = OUTPUTS.index(name)
            stores.append(pltpu.make_async_copy(getattr(it, name), getattr(it, "o_" + name), it.store.at[index]))
            stores[-1].start()

    r["mixed"].end()
    store("mixed_sum")
    for name in ("w_keyvalue", "norms"):
        r[name].middle()
    r["w_down"].end()
    r["w_query"].middle()
    r["w_out"].end()
    r["w_up"].end()
    store("s_w_down", "s_w_out", "s_w_up")
    for name in ("w_keyvalue", "norms"):
        r[name].end()
    copies = []
    for i, ref in enumerate((it.shared_kv, it.shared_norms)):
        for step in range(1, tensor.size):
            peer = lax.rem(tensor.me + step, tensor.size)
            sems = [s.at[i * tensor.size + step] for s in (it.share_send, it.share_recv)]
            copies.append(remote(ref.at[tensor.me], ref.at[tensor.me], *sems, tensor, peer))
            copies[-1].start()
    r["w_query"].end()
    store("s_w_query")

    @pl.loop(0, chunks)
    def _(index):
        scaled.end(turn(index))

    r["pack"].end()

    @pl.loop(0, slots // 128)
    def _(index):
        at = pl.ds(pl.multiple_of(index * 128, 128), 128)
        it.scaled_sum[at] += dot_cols(it.pack_sum[at].astype(BF16), core.w_keyvalue[...]) * core.params[0:1]

    store("scaled_sum")
    for copy in copies:
        copy.wait()
    store("shared_kv", "shared_norms")
    for name in WEIGHTS:
        g[name].leave()
    for copy in stores:
        copy.wait()


def finish_kernel(z, seq, tokens, cotangent, *refs):
    sums = Names(OUTPUTS, refs[: len(OUTPUTS)])
    out_tokens, d_tokens, d_query, d_keyvalue, d_out, d_up, d_down, *d_norms = refs[len(OUTPUTS) :]
    rows = tokens.shape[0]
    token = tokens[...].astype(F32)
    out_tokens[...] = (token + sums.mixed_sum[...]).astype(BF16)
    centered = token - jnp.mean(token, axis=1, keepdims=True)
    inv_std = lax.rsqrt(jnp.mean(centered * centered, axis=1, keepdims=True) + EPS)
    scaled = centered * inv_std
    grad = sums.scaled_sum[...]
    first_row = lax.axis_index("tensor") * z.slots + pl.program_id(0) * rows
    row = lax.broadcasted_iota(jnp.int32, (rows, 1), 0) + first_row
    own = jnp.where(row < seq[0, 0], cotangent[...].astype(F32), 0.0)
    inner = jnp.mean(grad * scaled, axis=1, keepdims=True)
    d_tokens[...] = own + inv_std * (grad - jnp.mean(grad, axis=1, keepdims=True) - scaled * inner)
    d_query[...] = sums.s_w_query[:, : z.heads * 64]
    d_out[...] = sums.s_w_out[:, : z.heads * 64]
    d_up[...] = sums.s_w_up[...]
    d_down[...] = sums.s_w_down[...]
    kv, norms = sums.shared_kv[0], sums.shared_norms[0]
    for t in range(1, z.nt):
        kv, norms = kv + sums.shared_kv[t], norms + sums.shared_norms[t]
    d_keyvalue[...] = kv
    for i in range(4):
        d_norms[i][...] = norms[i]


def plain_kernel(z, seq, *refs):
    named = dict(zip(INPUTS, refs))
    mixed, scaled_grad, g_query, g_keyvalue, g_out, g_up, g_down, g_norms = refs[len(INPUTS) : len(INPUTS) + 8]
    *own, grad, scaled = refs[len(INPUTS) + 8 :]
    named.update(zip(own_shapes(z), own), grad=grad, scaled=scaled)
    core = Core(z.heads, seq[0, 0], z.used, **named)
    rows, model, used = z.rows, z.model, z.used
    core.tables(0)
    core.tables(1)
    core.unpack_params()

    @pl.loop(0, rows // BLOCK)
    def _(block):
        core.normalize(block)
        core.project(block)

    for block in range(rows // BLOCK):
        core.attend(block)

    @pl.loop(0, rows // 512)
    def _(index):
        at = pl.ds(pl.multiple_of(index * 512, 512), 512)
        core.feed(at)
        mixed[at] = core.mix(at).astype(BF16)

    @pl.loop(0, 4)
    def _(index):
        first = pl.multiple_of(index * (used // 4), used // 4)
        core.mask(pl.ds(first, used // 4), first, used // 4)
        core.feed_back(pl.ds(first, used // 4))

    @pl.loop(0, model // BLOCK)
    def _(index):
        at = pl.ds(pl.multiple_of(index * BLOCK, BLOCK), BLOCK)
        grad = core.grad[:used, at]
        g_down[at] = dot_rows(grad, core.hidden[:used]).astype(BF16)
        g_out[at] = dot_rows(grad, core.attended[:used]).astype(BF16)
        g_up[at] = dot_rows(core.normed2[:used, at], core.slope[:used]).astype(BF16)

    @pl.loop(0, used // BLOCK)
    def _(block):
        core.attend_grad(block)

    for ref in (core.d_keys, core.d_values, core.d_norms):
        ref[...] = jnp.zeros_like(ref)
    @pl.loop(0, used // BLOCK)
    def _(index):
        block = used // BLOCK - 1 - index
        core.attend_back(block)
        part_of(scaled_grad, block, BLOCK)[...] = core.input_grad(block).astype(BF16)

    core.keyvalue_grad()

    @pl.loop(0, used // BLOCK)
    def _(block):
        at = pl.ds(pl.multiple_of(block * BLOCK, BLOCK), BLOCK)
        more = dot_cols(core.d_keyvalue[at], core.w_keyvalue[...]) * core.params[0:1]
        scaled_grad[at] = (scaled_grad[at].astype(F32) + more).astype(BF16)

    scaled_grad[used:] = jnp.zeros((rows - used, model), BF16)

    @pl.loop(0, model // BLOCK)
    def _(index):
        at = pl.ds(pl.multiple_of(index * BLOCK, BLOCK), BLOCK)
        normed = core.normed1[:used, at]
        g_query[at] = dot_rows(normed, core.d_query[:used]).astype(BF16)
        g_keyvalue[at] = dot_rows(normed, core.d_keyvalue[:used]).astype(BF16)

    for i in range(4):
        g_norms[i : i + 1] = jnp.sum(core.d_norms[i], axis=0, keepdims=True)
    for i, more in enumerate(core.keyvalue_norms()):
        g_norms[i : i + 1] += more


def run_plain(seq_lengths, norms, arrays, z):
    tokens, cotangent, w_query, w_keyvalue, w_up, w_down, w_out = arrays
    width, model = w_query.shape[1], tokens.shape[1]
    wide = z.wide
    pad = jnp.pad(w_query[:, width // 128 * 128 :], ((0, 0), (0, wide - width)))
    lane, start = lax.iota(jnp.int32, 128)[None], width % 128
    vectors = jnp.pad(jnp.stack(norms, axis=1), ((0, 0), (start, 124 - start)))
    tail = jnp.where(lane < start, pad, vectors)
    query = jnp.concatenate([w_query[:, : width // 128 * 128], tail], axis=1)
    out = jnp.pad(w_out, ((0, 0), (0, wide - width)))
    gathered = [lax.all_gather(a, "tensor", axis=0, tiled=True) for a in (tokens, cotangent)]
    gathered += [lax.all_gather(a, "dp", axis=0, tiled=True) for a in (query, w_keyvalue, w_up, w_down, out)]
    shape = jax.ShapeDtypeStruct
    results = pl.pallas_call(
        functools.partial(plain_kernel, z),
        out_shape=[shape((z.rows, model), BF16)] * 2
        + [shape((model, n), BF16) for n in (wide, 128, wide, z.units, z.units)]
        + [shape((4, model), F32)],
        in_specs=[pl.BlockSpec(memory_space=pltpu.SMEM)] + [INVMEM] * len(gathered),
        out_specs=[INVMEM] * 8,
        scratch_shapes=[pltpu.VMEM(*entry) for entry in own_shapes(z).values()] + [pltpu.VMEM((n, model), BF16) for n in (z.used, z.rows)],
        compiler_params=pltpu.CompilerParams(vmem_limit_bytes=67043328),
        name="plain_layer",
    )(seq_lengths, *gathered)
    names = ("tensor", "tensor") + ("dp",) * 5
    sums = [
        lax.psum_scatter(p.astype(F32), n, scatter_dimension=0, tiled=True) for p, n in zip(results[:7], names)
    ]
    norm_sums = lax.psum_scatter(results[7], "dp", scatter_dimension=1, tiled=True)
    shared_kv = lax.all_gather(sums[3], "tensor")
    shared_norms = lax.all_gather(jnp.pad(norm_sums, ((0, 4), (0, 0))), "tensor")
    return sums[0], sums[1], sums[2], sums[4], sums[5], sums[6], shared_kv, shared_norms


def run_whole(seq_lengths, norms, arrays, z):
    arrays_of, semaphores = fused_specs(z)
    scratch = [pltpu.VMEM(*entry) for entry in arrays_of.values()]
    scratch += [pltpu.SemaphoreType.DMA(shape) for shape in semaphores.values()]
    return pl.pallas_call(
        functools.partial(fused_kernel, z, tuple(arrays_of) + tuple(semaphores)),
        out_shape=[jax.ShapeDtypeStruct(shape, F32) for shape in output_shapes(z)],
        in_specs=[pl.BlockSpec(memory_space=pltpu.SMEM)]
        + [INVMEM] * 4
        + [INVMEM if packed else ANY for packed in (False, False, True, False, False, False, True)],
        out_specs=[ANY] * len(OUTPUTS),
        scratch_shapes=scratch,
        compiler_params=pltpu.CompilerParams(collective_id=0, has_side_effects=True, vmem_limit_bytes=67043328),
        name="layer",
    )(seq_lengths, *norms, *arrays)


def run_layer(seq_lengths, norms, arrays, nd, nt):
    tokens, _, w_query, w_keyvalue, w_up, _, _ = arrays
    heads, own, units = w_query.shape[1] // 64, w_query.shape[0], w_up.shape[1]
    slots, model = tokens.shape
    z = types.SimpleNamespace(
        nd=nd, nt=nt, heads=heads, rows=slots * nt, model=model, stack=heads * BLOCK, units=units, used=SEQ_MOST,
        wide=(heads * 64 + 4 + 127) // 128 * 128, own=own, slots=slots,
    )
    run = run_whole if own % 32 == 0 and slots == 2 * BLOCK and nt == 4 and SEQ_MOST == 7 * BLOCK else run_plain
    sums = run(seq_lengths, norms, arrays, z)
    steps = 2 if own % 16 == 0 else 1
    shape = jax.ShapeDtypeStruct

    def block(rows, columns):
        return pl.BlockSpec((rows // steps, columns), lambda i: (i, 0))

    width = heads * 64
    token_rows = block(slots, model)
    weights = [block(own, n) for n in (z.wide, z.wide, units, units)]
    shared = [
        pl.BlockSpec((nt, own // steps, 128), lambda i: (0, i, 0)),
        pl.BlockSpec((nt, 8, own), lambda i: (0, 0, 0)),
    ]
    results = pl.pallas_call(
        functools.partial(finish_kernel, z),
        grid=(steps,),
        out_shape=[shape((slots, model), BF16), shape((slots, model), F32)]
        + [shape((own, n), F32) for n in (width, 128, width, units, units)]
        + [shape((own,), F32)] * 4,
        in_specs=[pl.BlockSpec(memory_space=pltpu.SMEM)] + [token_rows] * 4 + weights + shared,
        out_specs=[token_rows] * 2
        + [block(own, n) for n in (width, 128, width, units, units)]
        + [pl.BlockSpec((own,), lambda i: (0,))] * 4,
        compiler_params=pltpu.CompilerParams(vmem_limit_bytes=67043328),
        name="finish",
    )(seq_lengths, *arrays[:2], *sums)
    return tuple(results)


def shards(
    tokens,
    cotangent,
    seq_lengths,
    w_query,
    w_keyvalue,
    w_out,
    w_up,
    w_down,
    norm1_gain,
    norm1_bias,
    norm2_gain,
    norm2_bias,
):
    norms = (norm1_gain, norm1_bias, norm2_gain, norm2_bias)
    arrays = (tokens, cotangent, w_query, w_keyvalue, w_up, w_down, w_out)
    return run_layer(seq_lengths, norms, arrays, lax.axis_size("dp"), lax.axis_size("tensor"))


def solution(mesh):
    return jax.shard_map(
        shards,
        mesh=mesh,
        in_specs=(
            P(("dp", "tensor"), None),
            P(("dp", "tensor"), None),
            P("dp", None),
            P("dp", "tensor"),
            P("dp", None),
            P("dp", "tensor"),
            P("dp", "tensor"),
            P("dp", "tensor"),
            P("dp"),
            P("dp"),
            P("dp"),
            P("dp"),
        ),
        out_specs=(
            P(("dp", "tensor"), None),
            P(("dp", "tensor"), None),
            P("dp", "tensor"),
            P("dp", None),
            P("dp", "tensor"),
            P("dp", "tensor"),
            P("dp", "tensor"),
            P("dp"),
            P("dp"),
            P("dp"),
            P("dp"),
        ),
        check_vma=False,
    )
```

```python
import functools
import math
import types

import jax
import jax.numpy as jnp
from jax import lax
from jax.experimental import pallas as pl
from jax.experimental.pallas import tpu as pltpu
from jax.sharding import PartitionSpec as P

ROT = 16
SEQ_LEAST = 1024
SEQ_MOST = 1792
BLOCK = 256
WIDE = 3
EPS = 1e-05
NEG = -1e30
F32 = jnp.float32
BF16 = jnp.bfloat16


def dot(left, right):
    return jnp.dot(left, right, preferred_element_type=F32)


def dot_rows(left, right):
    return lax.dot_general(left, right, (((0,), (0,)), ((), ())), preferred_element_type=F32)


def dot_cols(left, right):
    return lax.dot_general(left, right, (((1,), (1,)), ((), ())), preferred_element_type=F32)


def lanes_of(rows):
    return lax.broadcasted_iota(jnp.int32, (rows, 128), 1)


def swap_halves(x, lane):
    return jnp.where(lane < ROT // 2, pltpu.roll(x, 128 - ROT // 2, 1), pltpu.roll(x, ROT // 2, 1))


def three_parts(x):
    high = x.astype(BF16).astype(F32)
    middle = (x - high).astype(BF16).astype(F32)
    return high, middle, x - high - middle


def unit_heads(wide, heads):
    pieces = []
    for h in range(heads):
        piece = wide[:, h // 2 * 128 : h // 2 * 128 + 128]
        pieces.append(piece if h % 2 == 0 else pltpu.roll(piece, 64, 1))
    return pieces


def join_heads(pieces, lane):
    wide = []
    for h in range(0, len(pieces), 2):
        second = pltpu.roll(pieces[h + 1], 64, 1) if h + 1 < len(pieces) else jnp.zeros_like(pieces[h])
        wide.append(jnp.where(lane < 64, pieces[h], second))
    return jnp.concatenate(wide, axis=1)


class Core:
    def __init__(self, heads, length, used, **refs):
        self.heads, self.length, self.used = heads, length, used
        self.__dict__.update(refs)
        stack = heads * BLOCK
        self.d_query = self.attended
        self.d_stack = self.scores.at[0:stack, 0:128]
        self.d_keys = self.scores.at[stack : stack + used, 0:128]
        self.d_values = self.scores.at[stack : stack + used, 128:256]

    def past(self, first, shape, axis):
        return lax.broadcasted_iota(jnp.int32, shape, axis) + first >= self.length

    def tables(self, part):
        count = self.cosine.shape[0] // BLOCK // 2

        @pl.loop(part * count, part * count + count)
        def _(index):
            at = pl.ds(pl.multiple_of(index * BLOCK, BLOCK), BLOCK)
            lane = lanes_of(BLOCK)
            row = lax.broadcasted_iota(jnp.int32, (BLOCK, 128), 0) + index * BLOCK
            position = jnp.where(row >= self.length, row - self.length, row).astype(F32)
            exponent = jnp.where(lane < ROT // 2, lane, lane - ROT // 2).astype(F32) * (-2.0 / ROT)
            angle = position * jnp.exp(exponent * math.log(10000.0))
            sine = jnp.sin(angle)
            self.cosine[at] = jnp.where(lane < ROT, jnp.cos(angle), 1.0)
            self.sine[at] = jnp.where(lane < ROT // 2, -sine, jnp.where(lane < ROT, sine, 0.0))

    def unpack_params(self):
        start = self.heads * 64
        turned = self.w_query[:, start // 128 * 128 : start // 128 * 128 + 128].T.astype(F32)
        self.params[0:4] = turned[start % 128 : start % 128 + 4]

    def normalize(self, block):
        at = pl.ds(pl.multiple_of(block * BLOCK, BLOCK), BLOCK)
        x = self.tokens[at].astype(F32)
        centered = x - jnp.mean(x, axis=1, keepdims=True)
        scaled = centered * lax.rsqrt(jnp.mean(centered * centered, axis=1, keepdims=True) + EPS)
        gain1, bias1, gain2, bias2 = (self.params[i : i + 1] for i in range(4))
        self.scaled[at] = scaled.astype(BF16)
        self.normed1[at] = (scaled * gain1 + bias1).astype(BF16)
        self.normed2[at] = (scaled * gain2 + bias2).astype(BF16)

    def project(self, block):
        first = pl.multiple_of(block * BLOCK, BLOCK)
        at = pl.ds(first, BLOCK)
        lane = lanes_of(BLOCK)
        cosine, sine = self.cosine[at], self.sine[at]
        past = self.past(first, (BLOCK, 128), 0)
        normed = self.normed1[at]
        key_value = dot(normed, self.w_keyvalue[...])
        keys = key_value * cosine + swap_halves(key_value, lane) * sine
        hidden_key = jnp.where(past, 0.0, NEG)
        extra = jnp.where(lane == 64, hidden_key, jnp.where(lane < 68, -1.0, 0.0))
        self.keys[at] = jnp.where(lane < 64, keys, extra).astype(BF16)
        ones = jnp.where(lane < 67, 1.0, 0.0)
        self.values[at] = jnp.where(lane < 64, pltpu.roll(key_value, 64, 1), ones).astype(BF16)
        query = dot(normed, self.w_query[...])
        flag = jnp.where((lane == 64) & past, 1.0, 0.0)
        for h, piece in enumerate(unit_heads(query, self.heads)):
            turned = (piece * cosine + swap_halves(piece, lane) * sine).astype(BF16).astype(F32)
            turned = turned * (64 ** (-0.5))
            self.queries[block, h * BLOCK : (h + 1) * BLOCK] = jnp.where(lane < 64, turned, flag).astype(BF16)

    def key_blocks(self, block):
        first = SEQ_LEAST // BLOCK if block * BLOCK >= SEQ_MOST else 0
        return range(first, block + 1)

    def attend(self, block):
        rows = self.heads * BLOCK
        query = self.queries[block]
        lane = lanes_of(rows)
        top = jnp.full((rows, BLOCK), -3e38, F32)
        for index, j in enumerate(self.key_blocks(block)):
            scores = dot_cols(query, self.keys[j * BLOCK : (j + 1) * BLOCK])
            if j == block:
                row = lax.rem(lax.broadcasted_iota(jnp.int32, (rows, BLOCK), 0), BLOCK)
                column = lax.broadcasted_iota(jnp.int32, (rows, BLOCK), 1)
                scores = jnp.where(column <= row, scores, NEG)
            self.scores[index * rows : (index + 1) * rows] = scores
            top = jnp.maximum(top, scores)
        top = jnp.max(top, axis=1, keepdims=True)
        total = jnp.zeros((rows, 128), F32)
        for index, j in enumerate(self.key_blocks(block)):
            probs = jnp.exp(self.scores[index * rows : (index + 1) * rows] - top).astype(BF16)
            total = total + dot(probs, self.values[j * BLOCK : (j + 1) * BLOCK])
        weight = jnp.sum(jnp.where(lane == 64, total, 0.0), axis=1, keepdims=True)
        output = total / weight
        pieces = [output[h * BLOCK : (h + 1) * BLOCK] for h in range(self.heads)]
        self.attended[block * BLOCK : (block + 1) * BLOCK] = join_heads(pieces, lanes_of(BLOCK)).astype(BF16)
        high, middle, low = three_parts(top + jnp.log(weight))
        parts = jnp.where(lane == 65, high, jnp.where(lane == 66, middle, low))
        self.queries[block] = jnp.where((lane >= 65) & (lane < 68), parts, query.astype(F32)).astype(BF16)

    def feed(self, at):
        up = dot(self.normed2[at], self.w_up[...])
        normal = 0.5 * (1.0 + lax.erf(up * (1.0 / math.sqrt(2.0))))
        self.hidden[at] = (up * normal).astype(BF16)
        density = jnp.exp(-0.5 * up * up) * (1.0 / math.sqrt(2.0 * math.pi))
        self.slope[at] = (normal + up * density).astype(BF16)

    def mix(self, at):
        return dot_cols(self.attended[at], self.w_out[...]) + dot_cols(self.hidden[at], self.w_down[...])

    def mask(self, at, first, rows):
        past = self.past(first, (rows, 1), 0)
        self.grad[at] = jnp.where(past, 0.0, self.cotangent[at].astype(F32)).astype(BF16)

    def feed_back(self, at):
        d_hidden = dot(self.grad[at], self.w_down[...])
        self.slope[at] = (d_hidden * self.slope[at].astype(F32)).astype(BF16)

    def d_attended(self, block, first, size):
        across = self.hidden.shape[1] // 128
        row = block // across * (self.heads * BLOCK) + first
        lane = lax.rem(block, across) * 128
        return self.hidden.at[pl.ds(pl.multiple_of(row, BLOCK), size), pl.ds(pl.multiple_of(lane, 128), 128)]

    def attend_grad(self, block):
        first = pl.multiple_of(block * BLOCK, BLOCK)
        at = pl.ds(first, BLOCK)
        lane = lanes_of(BLOCK)
        grads = unit_heads(dot(self.grad[at], self.w_out[...]), self.heads)
        outputs = unit_heads(self.attended[at].astype(F32), self.heads)
        for h in range(self.heads):
            grad = grads[h].astype(BF16).astype(F32)
            delta = jnp.sum(jnp.where(lane < 64, grad * outputs[h], 0.0), axis=1, keepdims=True)
            high, middle, low = three_parts(-delta)
            parts = jnp.where(lane == 64, high, jnp.where(lane == 65, middle, jnp.where(lane == 66, low, 0.0)))
            self.d_attended(block, h * BLOCK, BLOCK)[...] = jnp.where(lane < 64, grad, parts).astype(BF16)

    def attend_back(self, block):
        rows = self.heads * BLOCK
        query, grad = self.queries[block], self.d_attended(block, 0, rows)[...]

        def span(first, size, diagonal):
            at = pl.ds(pl.multiple_of(first, BLOCK), size)
            keys, values = self.keys[at], self.values[at]
            scores, d_probs = dot_cols(keys, query), dot_cols(values, grad)
            if diagonal:
                key = lax.broadcasted_iota(jnp.int32, (size, rows), 0)
                row = lax.rem(lax.broadcasted_iota(jnp.int32, (size, rows), 1), BLOCK) + (size - BLOCK)
                scores = jnp.where(key <= row, scores, NEG)
            probs = jnp.exp(scores)
            d_scores = (probs * d_probs).astype(BF16)
            self.d_values[at] += dot(probs.astype(BF16), grad)
            self.d_keys[at] += dot(d_scores, query)
            d_query = dot_rows(d_scores, keys)
            if diagonal:
                self.d_stack[...] = d_query
            else:
                self.d_stack[...] += d_query

        last = lax.rem(block, WIDE)
        for size in range(WIDE):

            @pl.when(last == size)
            def _():
                span((block - size) * BLOCK, (size + 1) * BLOCK, True)

        @pl.loop(0, block // WIDE)
        def _(index):
            span(index * WIDE * BLOCK, WIDE * BLOCK, False)

        at = pl.ds(pl.multiple_of(block * BLOCK, BLOCK), BLOCK)
        pieces = [
            self.turn_back(self.d_stack[h * BLOCK : (h + 1) * BLOCK], at) * (64 ** (-0.5)) for h in range(self.heads)
        ]
        self.d_query[at] = join_heads(pieces, lanes_of(BLOCK)).astype(BF16)

    def turn_back(self, x, at):
        return x * self.cosine[at] - swap_halves(x, lanes_of(BLOCK)) * self.sine[at]

    def keyvalue_grad(self):
        rows = self.d_keyvalue.shape[0]

        @pl.loop(0, self.used // BLOCK)
        def _(block):
            at = pl.ds(pl.multiple_of(block * BLOCK, BLOCK), BLOCK)
            d_keys = self.turn_back(self.d_keys[at], at)
            d_values = pltpu.roll(self.d_values[at], 64, 1)
            self.d_keyvalue[at] = jnp.where(lanes_of(BLOCK) < 64, d_keys, d_values).astype(BF16)

        self.d_keyvalue[self.used :] = jnp.zeros((rows - self.used, 128), BF16)

    def keyvalue_norms(self):
        weight = self.w_keyvalue[...].astype(F32)
        grad = self.d_keyvalue[: self.used]
        gain = jnp.sum(dot_rows(self.scaled[: self.used], grad) * weight, axis=1, keepdims=True)
        bias = jnp.sum(jnp.sum(grad.astype(F32), axis=0, keepdims=True) * weight, axis=1, keepdims=True)
        lane = lanes_of(weight.shape[0])
        turned = jnp.where(lane == 0, gain, bias).T
        return turned[0:1], turned[1:2]

    def input_grad(self, block):
        at = pl.ds(pl.multiple_of(block * BLOCK, BLOCK), BLOCK)
        d_normed1 = dot_cols(self.d_query[at], self.w_query[...])
        d_normed2 = dot_cols(self.slope[at], self.w_up[...])
        scaled = self.scaled[at].astype(F32)
        for i, value in enumerate((d_normed1 * scaled, d_normed1, d_normed2 * scaled, d_normed2)):
            self.d_norms[i] += jnp.sum(value.reshape(BLOCK // 8, 8, -1), axis=0)
        return d_normed1 * self.params[0:1] + d_normed2 * self.params[2:3]


MESH = pl.DeviceIdType.MESH
INVMEM = pl.BlockSpec(memory_space=pltpu.VMEM)
ANY = pl.BlockSpec(memory_space=pl.ANY)


class Axis:
    def __init__(self, name, size):
        self.name, self.size, self.half = name, size, size // 2
        self.me = lax.axis_index(name)
        self.row, self.par = self.me // 2, self.me % 2
        self.pair = self.me + 1 - 2 * self.par

    def other_row(self, step):
        return lax.rem(self.row + step + self.half, self.half)

    def line(self, step):
        return self.other_row(step) * 2 + self.par

    def greet(self, barrier, peers):
        for peer in peers:
            pl.semaphore_signal(barrier, inc=1, device_id={self.name: peer}, device_id_type=MESH)
        return len(peers)


def remote(src, dst, send, recv, axis, peer):
    return pltpu.make_async_remote_copy(
        src_ref=src, dst_ref=dst, send_sem=send, recv_sem=recv, device_id={axis.name: peer}, device_id_type=MESH
    )


def part_of(ref, index, rows):
    return ref.at[pl.ds(pl.multiple_of(index * rows, rows), rows)]


class Gather:
    def __init__(self, axis, src, dst, send, recv, local, part=0, parts=1):
        self.axis, self.dst, self.send, self.recv = axis, dst, send, recv
        self.half, self.part, self.parts = axis.half, part, parts
        self.src = part_of(src, part, src.shape[0] // parts)
        self.copy = pltpu.make_async_copy(self.src, self.slot(axis.me), local)

    def slot(self, index):
        return part_of(self.dst, index * self.parts + self.part, self.src.shape[0])

    def along(self, row, way, own=False):
        slot = self.slot(2 * row + self.axis.par)
        send = self.send.at[row if way > 0 else self.half + row]
        peer = self.axis.me + 2 * way
        return remote(self.src if own else slot, slot, send, self.recv.at[row], self.axis, peer)

    def across(self, row, own=False):
        slot = self.slot(2 * row + self.axis.par)
        sems = self.send.at[2 * self.half + row], self.recv.at[self.half + row]
        return remote(self.src if own else slot, slot, *sems, self.axis, self.axis.pair)

    def start_line(self):
        @pl.when(self.axis.row + 1 < self.half)
        def _():
            self.along(self.axis.row, 1, own=True).start()

        @pl.when(self.axis.row > 0)
        def _():
            self.along(self.axis.row, -1, own=True).start()

    def start_pair(self):
        self.across(self.axis.row, own=True).start()

    def pass_on(self, distance):
        if distance >= self.half:
            return
        me = self.axis.row

        @pl.when(me >= distance)
        def _():
            row = me - distance
            self.along(row, 1).wait_recv()

            @pl.when(me + 1 < self.half)
            def _():
                self.along(row, 1).start()

            self.across(row).start()

        @pl.when(me + distance < self.half)
        def _():
            row = me + distance
            self.along(row, -1).wait_recv()

            @pl.when(me > 0)
            def _():
                self.along(row, -1).start()

            self.across(row).start()

    def pair_arrived(self, row):
        slot = self.slot(2 * row + 1 - self.axis.par)
        sems = self.send.at[2 * self.half + row], self.recv.at[self.half + row]
        remote(slot, slot, *sems, self.axis, self.axis.pair).wait_recv()

    def arrive(self):
        self.copy.wait()
        for row in range(self.half):
            self.pair_arrived(row)

    def leave(self):
        for row in range(self.half):
            self.across(row).wait_send()

            @pl.when((self.axis.row >= row) & (self.axis.row + 1 < self.half))
            def _():
                self.along(row, 1).wait_send()

            @pl.when((self.axis.row <= row) & (self.axis.row > 0))
            def _():
                self.along(row, -1).wait_send()


class Reduce:
    def __init__(self, axis, part, out, held, last, send, recv):
        self.axis, self.part, self.out, self.held, self.last = axis, part, out, held, last
        self.send, self.recv, self.rows = send, recv, out.shape[0]
        self.chunk = 32 if self.rows % 32 == 0 else self.rows

    def first(self, row):
        block = part_of(self.part, 2 * row + 1 - self.axis.par, self.rows)
        held = part_of(self.held, row, self.rows)
        return remote(block, held, self.send.at[row], self.recv.at[row], self.axis, self.axis.pair)

    def second(self, step):
        index = self.axis.half + step
        block = part_of(self.held, self.axis.other_row(step), self.rows)
        last = part_of(self.last, step - 1, self.rows)
        return remote(block, last, self.send.at[index], self.recv.at[index], self.axis, self.axis.line(step))

    def start(self):
        for step in range(self.axis.half):
            self.first(self.axis.other_row(step + 1)).start()

    def chunks(self, body):
        @pl.loop(0, self.rows // self.chunk)
        def _(index):
            body(pl.multiple_of(index * self.chunk, self.chunk))

    def total(self, row, at):
        part = self.part[pl.ds((2 * row + self.axis.par) * self.rows + at, self.chunk)].astype(F32)
        return part + self.held[pl.ds(row * self.rows + at, self.chunk)].astype(F32)

    def middle(self):
        for step in range(1, self.axis.half):
            row = self.axis.other_row(step)
            self.first(row).wait()

            def add(at, row=row):
                self.held[pl.ds(row * self.rows + at, self.chunk)] = self.total(row, at).astype(self.held.dtype)

            self.chunks(add)
            self.second(step).start()

        self.first(self.axis.row).wait()

        def keep(at):
            self.out[pl.ds(at, self.chunk)] = self.total(self.axis.row, at)

        self.chunks(keep)

    def end(self):
        for step in range(1, self.axis.half):
            self.second(step).wait()

        def add(at):
            total = self.out[pl.ds(at, self.chunk)]
            for step in range(1, self.axis.half):
                total = total + self.last[pl.ds((step - 1) * self.rows + at, self.chunk)].astype(F32)
            self.out[pl.ds(at, self.chunk)] = total

        self.chunks(add)


class Stream:
    def __init__(self, axis, part, out, held, last, pair_send, pair_recv, line_send, line_recv):
        self.axis, self.part, self.out, self.held, self.last = axis, part, out, held, last
        self.pair_sems, self.line_sems = (pair_send, pair_recv), (line_send, line_recv)

    def split(self, chunk):
        return chunk // 4, chunk // 2 % 2, chunk % 2

    def pair_copy(self, chunk):
        row, _, half = self.split(chunk)
        index = 2 * row + half
        send, recv = (sems.at[index] for sems in self.pair_sems)
        held = part_of(self.held, index, BLOCK)
        return remote(part_of(self.part, chunk, BLOCK), held, send, recv, self.axis, self.axis.pair)

    def line_copy(self, chunk):
        row, _, half = self.split(chunk)
        send, recv = (sems.at[half] for sems in self.line_sems)
        held = part_of(self.held, 2 * row + half, BLOCK)
        return remote(held, part_of(self.last, half, BLOCK), send, recv, self.axis, self.axis.line(1))

    def give(self, chunk):
        @pl.when(self.axis.par != self.split(chunk)[1])
        def _():
            self.pair_copy(chunk).start()

    def take(self, chunk):
        row, par, half = self.split(chunk)

        @pl.when(self.axis.par == par)
        def _():
            self.pair_copy(chunk).wait_recv()

            def total(at):
                part = self.part[pl.ds(chunk * BLOCK + at, 32)].astype(F32)
                return part + self.held[pl.ds((2 * row + half) * BLOCK + at, 32)].astype(F32)

            @pl.when(self.axis.row == row)
            def _():
                @pl.loop(0, BLOCK // 32)
                def _(index):
                    at = pl.multiple_of(index * 32, 32)
                    self.out[pl.ds(half * BLOCK + at, 32)] = total(at)

            @pl.when(self.axis.row != row)
            def _():
                @pl.loop(0, BLOCK // 32)
                def _(index):
                    at = pl.multiple_of(index * 32, 32)
                    self.held[pl.ds((2 * row + half) * BLOCK + at, 32)] = total(at).astype(BF16)

                self.line_copy(chunk).start()

    def end(self, chunk):
        row, par, half = self.split(chunk)

        @pl.when(self.axis.par != par)
        def _():
            self.pair_copy(chunk).wait_send()

        @pl.when((self.axis.par == par) & (self.axis.row != row))
        def _():
            self.line_copy(chunk).wait_send()

        @pl.when((self.axis.par == par) & (self.axis.row == row))
        def _():
            self.line_copy(chunk).wait_recv()

            @pl.loop(0, BLOCK // 32)
            def _(index):
                at = pl.multiple_of(index * 32, 32)
                rows = pl.ds(half * BLOCK + at, 32)
                self.out[rows] += self.last[rows].astype(F32)

WEIGHTS = ("w_query", "w_keyvalue", "w_up", "w_down", "w_out")
INPUTS = ("tokens", "cotangent") + WEIGHTS
OUTPUTS = ("mixed_sum", "scaled_sum", "s_w_query", "s_w_out", "s_w_up", "s_w_down", "shared_kv", "shared_norms")


def own_shapes(z):
    wide_rows = (z.rows, z.model)
    return dict(
        params=((8, z.model), F32), cosine=((z.rows, 128), F32), sine=((z.rows, 128), F32),
        normed1=(wide_rows, BF16), normed2=(wide_rows, BF16),
        queries=((z.rows // BLOCK, z.stack, 128), BF16), keys=((z.rows, 128), BF16), values=((z.rows, 128), BF16),
        scores=((z.used // BLOCK * z.stack, BLOCK), F32), attended=((z.rows, z.wide), BF16), hidden=((z.rows, z.units), BF16),
        slope=((z.rows, z.units), BF16), d_keyvalue=((z.rows, 128), BF16), d_norms=((4, 8, z.model), F32),
    )


class Names:
    def __init__(self, names, refs):
        self.__dict__.update(zip(names, refs, strict=True))


def output_shapes(z):
    return [
        (z.slots, z.model), (z.slots, z.model), (z.own, z.wide), (z.own, z.wide), (z.own, z.units), (z.own, z.units),
        (z.nt, z.own, 128), (z.nt, 8, z.own),
    ]


def fused_specs(z):
    half, model = z.nd // 2, z.model
    columns = dict(zip(WEIGHTS, (z.wide, 128, z.units, z.units, z.wide)))
    arrays = own_shapes(z)
    arrays.update({name: (shape, F32) for name, shape in zip(OUTPUTS, output_shapes(z))})
    arrays.update(pack_query=((z.own, z.wide), BF16), pack_out=((z.own, z.wide), BF16))
    arrays.update(tokens=((z.rows, model), BF16), cotangent=((z.rows, model), BF16))
    arrays.update({name: ((model, columns[name]), BF16) for name in WEIGHTS})
    arrays.update(mixed=((z.rows, model), BF16), held_mixed=((z.rows // 2, model), BF16))
    arrays.update(last_mixed=((z.slots, model), BF16), held_scaled=((z.rows // 2, model), BF16))
    arrays.update(last_scaled=((z.slots, model), BF16))
    for name in WEIGHTS:
        arrays["g_" + name] = ((model, columns[name]), BF16)
        arrays["held_" + name] = ((half * z.own, columns[name]), BF16)
        arrays["last_" + name] = ((max(half - 1, 1) * z.own, columns[name]), BF16)
    arrays.update(held_pack=((z.rows // 2, 128), BF16), last_pack=((z.slots, 128), BF16), pack_sum=((z.slots, 128), F32))
    arrays.update(g_norms=((z.nd * 8, z.own), F32), held_norms=((half * 8, z.own), F32))
    arrays.update(last_norms=((max(half - 1, 1) * 8, z.own), F32))
    semaphores = dict(send_mixed=(z.nt,), recv_mixed=(z.nt,), send_pack=(z.nt,), recv_pack=(z.nt,), send_norms=(z.nd,), recv_norms=(z.nd,))
    for name in INPUTS:
        count = z.nd if name in WEIGHTS else z.nt
        shape = (2, count) if name == "tokens" else (count,)
        semaphores.update({"send_" + name: shape[:-1] + (count // 2 * 3,), "recv_" + name: shape})
    for name in WEIGHTS:
        semaphores.update({"out_" + name: (z.nd,), "in_" + name: (z.nd,)})
    semaphores.update(pair_send=(4,), pair_recv=(4,), line_send=(2,), line_recv=(2,), local=(len(INPUTS) + 1,))
    semaphores.update(share_send=(2 * z.nt,), share_recv=(2 * z.nt,), store=(len(OUTPUTS),))
    return arrays, semaphores


def fused_kernel(z, names, *refs):
    vectors, refs = refs[1:5], refs[:1] + refs[5:]
    it = Names(("seq",) + tuple("i_" + n for n in INPUTS) + tuple("o_" + n for n in OUTPUTS) + names, refs)
    dp, tensor = Axis("dp", z.nd), Axis("tensor", z.nt)
    rows, model, used, slots = z.rows, z.model, z.used, z.slots
    core = Core(z.heads, it.seq[0, 0], z.used, **{n: getattr(it, n) for n in tuple(own_shapes(z)) + INPUTS}, grad=it.cotangent, scaled=it.tokens)
    barrier = pltpu.get_barrier_semaphore()
    expected = dp.greet(barrier, [dp.pair] + [dp.line(step) for step in range(1, dp.half)])
    expected += tensor.greet(barrier, [lax.rem(tensor.me + step, tensor.size) for step in range(1, tensor.size)])

    width = z.heads * 64
    pad = jnp.zeros((z.own, z.wide - width), BF16)
    lane = lanes_of(z.own)
    first = width // 128 * 128
    tail = jnp.concatenate([it.i_w_query[:, first:].astype(F32), pad.astype(F32)], axis=1)
    it.pack_query[:, :first] = it.i_w_query[:, :first]
    start = width - first
    turned = [v[...].astype(F32).reshape(1, z.own) for v in vectors]
    turned = jnp.concatenate([jnp.zeros((start, z.own), F32)] + turned + [jnp.zeros((124 - start, z.own), F32)])
    turned = jnp.concatenate([turned, jnp.zeros((128, 128 - z.own), F32)], axis=1).T[: z.own]
    it.pack_query[:, first:] = jnp.where(lane < start, tail, turned).astype(BF16)
    it.pack_out[:, :first] = it.i_w_out[:, :first]
    it.pack_out[:, first:] = jnp.concatenate([it.i_w_out[:, first:], pad], axis=1)
    sources = dict(w_query=it.pack_query, w_out=it.pack_out)
    g = {}
    for i, name in enumerate(INPUTS):
        axis = dp if name in WEIGHTS else tensor
        source = sources.get(name, getattr(it, "i_" + name))
        send, recv = getattr(it, "send_" + name), getattr(it, "recv_" + name)
        g[name] = Gather(axis, source, getattr(it, name), send, recv, it.local.at[i])
    tokens = [
        Gather(tensor, it.i_tokens, it.tokens, it.send_tokens.at[h], it.recv_tokens.at[h], it.local.at[len(INPUTS) * h], h, 2)
        for h in range(2)
    ]
    pl.semaphore_wait(barrier, expected)

    def hand_on(names, distance):
        for name in names:
            g[name].pass_on(distance)

    small = ("w_query", "w_keyvalue")
    for gather in tokens + [g["cotangent"]]:
        gather.start_line()
        gather.start_pair()
    for name in small:
        g[name].start_line()
        g[name].start_pair()
    g["w_up"].start_pair()
    for gather in tokens + [g[name] for name in INPUTS[1:]]:
        gather.copy.start()
    core.tables(0)
    hand_on(small, 1)
    g["w_up"].start_line()
    core.tables(1)
    hand_on(small, 2)
    hand_on(small, 3)
    hand_on(("w_up",), 1)
    g["w_down"].start_line()
    for name in small:
        g[name].arrive()
    core.unpack_params()

    for gather in tokens:
        gather.copy.wait()
    other, other_pair = tensor.line(1), tensor.line(1) + tensor.pair - tensor.me

    @pl.loop(0, 4)
    def _(index):
        @pl.when(index == 1)
        def _():
            for gather in tokens:
                gather.pair_arrived(tensor.row)
            hand_on(("w_up",), 2)
            g["w_down"].start_pair()
            g["w_out"].start_line()

        for half in range(2):

            @pl.when(index == 2 + half)
            def _():
                tokens[half].pass_on(1)
                if half == 0:
                    hand_on(("w_up",), 3)
                tokens[half].pair_arrived(1 - tensor.row)
                tokens[half].leave()

        late = index // 2
        first = jnp.where(index == 0, 2 * tensor.me, 2 * tensor.pair)
        blocks = [
            (1 - late) * first + late * (2 * other + index - 2),
            (1 - late) * (first + 1) + late * (2 * other_pair + index - 2),
        ]
        for block in blocks:
            core.normalize(block)
            core.project(block)

        @pl.when(index == 2)
        def _():
            hand_on(("w_down",), 1)
            g["w_out"].start_pair()

    hand_on(("w_down",), 2)
    g["w_up"].arrive()

    @pl.loop(0, rows // slots)
    def _(index):
        core.feed(pl.ds(pl.multiple_of(index * slots, slots), slots))
        for step, (name, distance) in enumerate((("w_down", 3), ("w_out", 1), ("w_out", 2), ("w_out", 3))):

            @pl.when(index == step)
            def _():
                hand_on((name,), distance)

    for block in range(rows // BLOCK):
        core.attend(block)
    g["cotangent"].pass_on(1)
    g["w_down"].arrive()
    g["cotangent"].arrive()
    g["cotangent"].leave()

    quarter = used // 4

    @pl.loop(0, 4)
    def _(index):
        first = pl.multiple_of(index * quarter, quarter)
        core.mask(pl.ds(first, quarter), first, quarter)

    r = {}
    for name in WEIGHTS:
        out = getattr(it, "s_" + name) if name != "w_keyvalue" else it.shared_kv.at[tensor.me]
        some = [getattr(it, kind + name) for kind in ("g_", "held_", "last_", "out_", "in_")]
        r[name] = Reduce(dp, some[0], out, *some[1:])
    r["norms"] = Reduce(
        dp, it.g_norms, it.shared_norms.at[tensor.me], it.held_norms, it.last_norms, it.send_norms, it.recv_norms
    )
    r["mixed"] = Reduce(tensor, it.mixed, it.mixed_sum, it.held_mixed, it.last_mixed, it.send_mixed, it.recv_mixed)
    r["pack"] = Reduce(
        tensor, core.d_keyvalue, it.pack_sum, it.held_pack, it.last_pack, it.send_pack, it.recv_pack
    )
    scaled = Stream(
        tensor, it.mixed, it.scaled_sum, it.held_scaled, it.last_scaled,
        it.pair_send, it.pair_recv, it.line_send, it.line_recv,
    )

    def weight_grad(name, left, right):
        half = model // 2

        @pl.loop(0, 2)
        def _(index):
            at = pl.ds(pl.multiple_of(index * half, 128), half)
            r[name].part[at] = dot_rows(left[:used, at], right[:used]).astype(BF16)

    weight_grad("w_down", core.grad, core.hidden)
    r["w_down"].start()
    weight_grad("w_out", core.grad, core.attended)
    r["w_out"].start()
    g["w_out"].arrive()

    @pl.loop(0, tensor.size)
    def _(index):
        row = lax.rem(index, tensor.half)
        par = jnp.where(index < tensor.half, 1 - tensor.par, tensor.par)
        at = pl.ds(pl.multiple_of((2 * row + par) * slots, slots), slots)
        it.mixed[at] = core.mix(at).astype(BF16)

        @pl.when(index < tensor.half)
        def _():
            r["mixed"].first(row).start()

    @pl.loop(0, 4)
    def _(index):
        core.feed_back(pl.ds(pl.multiple_of(index * quarter, quarter), quarter))

    weight_grad("w_up", core.normed2, core.slope)
    r["w_up"].start()
    r["mixed"].middle()

    @pl.loop(0, used // BLOCK)
    def _(block):
        core.attend_grad(block)

    r["w_down"].middle()
    for ref in (core.d_keys, core.d_values, core.d_norms, it.scaled_sum):
        ref[...] = jnp.zeros_like(ref)
    chunks = used // BLOCK

    def turn(index):
        return jnp.where(lax.rem(index, 2) == 0, chunks // 2, chunks - 1) - index // 2

    @pl.loop(0, chunks)
    def _(index):
        block = turn(index)
        core.attend_back(block)

        @pl.when(index > 0)
        def _():
            scaled.take(turn(index - 1))

        part_of(it.mixed, block, BLOCK)[...] = core.input_grad(block).astype(BF16)
        scaled.give(block)

        @pl.when(index == 1)
        def _():
            r["w_out"].middle()

        @pl.when(index == 3)
        def _():
            r["w_up"].middle()

    core.keyvalue_grad()
    scaled.take(turn(chunks - 1))
    r["pack"].start()
    weight_grad("w_keyvalue", core.normed1, core.d_keyvalue)
    r["w_keyvalue"].start()
    part = model // dp.size
    sums = [jnp.sum(core.d_norms[i], axis=0, keepdims=True) for i in range(4)]
    for i, more in enumerate(core.keyvalue_norms()):
        sums[i] = sums[i] + more
    sums = jnp.concatenate(sums + [jnp.zeros((4, model), F32)])
    for i in range(dp.size):
        it.g_norms[i * 8 : (i + 1) * 8] = sums[:, i * part : (i + 1) * part]
    r["norms"].start()
    r["pack"].middle()
    weight_grad("w_query", core.normed1, core.d_query)
    r["w_query"].start()
    stores = []

    def store(*some):
        for name in some:
            index = OUTPUTS.index(name)
            stores.append(pltpu.make_async_copy(getattr(it, name), getattr(it, "o_" + name), it.store.at[index]))
            stores[-1].start()

    for name in ("w_keyvalue", "norms", "w_query"):
        r[name].middle()
    for name in ("w_keyvalue", "norms"):
        r[name].end()
    copies = []
    for i, ref in enumerate((it.shared_kv, it.shared_norms)):
        for step in range(1, tensor.size):
            peer = lax.rem(tensor.me + step, tensor.size)
            sems = [s.at[i * tensor.size + step] for s in (it.share_send, it.share_recv)]
            copies.append(remote(ref.at[tensor.me], ref.at[tensor.me], *sems, tensor, peer))
            copies[-1].start()
    r["mixed"].end()
    store("mixed_sum")
    r["w_down"].end()
    r["w_out"].end()
    r["w_up"].end()
    store("s_w_down", "s_w_out", "s_w_up")
    r["w_query"].end()
    store("s_w_query")

    @pl.loop(0, chunks)
    def _(index):
        scaled.end(turn(index))

    r["pack"].end()

    @pl.loop(0, slots // 128)
    def _(index):
        at = pl.ds(pl.multiple_of(index * 128, 128), 128)
        it.scaled_sum[at] += dot_cols(it.pack_sum[at].astype(BF16), core.w_keyvalue[...]) * core.params[0:1]

    store("scaled_sum")
    for copy in copies:
        copy.wait()
    store("shared_kv", "shared_norms")
    for name in WEIGHTS:
        g[name].leave()
    for copy in stores:
        copy.wait()


def finish_kernel(z, seq, tokens, cotangent, *refs):
    sums = Names(OUTPUTS, refs[: len(OUTPUTS)])
    out_tokens, d_tokens, d_query, d_keyvalue, d_out, d_up, d_down, *d_norms = refs[len(OUTPUTS) :]
    rows = tokens.shape[0]
    token = tokens[...].astype(F32)
    out_tokens[...] = (token + sums.mixed_sum[...]).astype(BF16)
    centered = token - jnp.mean(token, axis=1, keepdims=True)
    inv_std = lax.rsqrt(jnp.mean(centered * centered, axis=1, keepdims=True) + EPS)
    scaled = centered * inv_std
    grad = sums.scaled_sum[...]
    first_row = lax.axis_index("tensor") * z.slots + pl.program_id(0) * rows
    row = lax.broadcasted_iota(jnp.int32, (rows, 1), 0) + first_row
    own = jnp.where(row < seq[0, 0], cotangent[...].astype(F32), 0.0)
    inner = jnp.mean(grad * scaled, axis=1, keepdims=True)
    d_tokens[...] = own + inv_std * (grad - jnp.mean(grad, axis=1, keepdims=True) - scaled * inner)
    d_query[...] = sums.s_w_query[:, : z.heads * 64]
    d_out[...] = sums.s_w_out[:, : z.heads * 64]
    d_up[...] = sums.s_w_up[...]
    d_down[...] = sums.s_w_down[...]
    kv, norms = sums.shared_kv[0], sums.shared_norms[0]
    for t in range(1, z.nt):
        kv, norms = kv + sums.shared_kv[t], norms + sums.shared_norms[t]
    d_keyvalue[...] = kv
    for i in range(4):
        d_norms[i][...] = norms[i]


def plain_kernel(z, seq, *refs):
    named = dict(zip(INPUTS, refs))
    mixed, scaled_grad, g_query, g_keyvalue, g_out, g_up, g_down, g_norms = refs[len(INPUTS) : len(INPUTS) + 8]
    *own, grad, scaled = refs[len(INPUTS) + 8 :]
    named.update(zip(own_shapes(z), own), grad=grad, scaled=scaled)
    core = Core(z.heads, seq[0, 0], z.used, **named)
    rows, model, used = z.rows, z.model, z.used
    core.tables(0)
    core.tables(1)
    core.unpack_params()

    @pl.loop(0, rows // BLOCK)
    def _(block):
        core.normalize(block)
        core.project(block)

    for block in range(rows // BLOCK):
        core.attend(block)

    @pl.loop(0, rows // 512)
    def _(index):
        at = pl.ds(pl.multiple_of(index * 512, 512), 512)
        core.feed(at)
        mixed[at] = core.mix(at).astype(BF16)

    @pl.loop(0, 4)
    def _(index):
        first = pl.multiple_of(index * (used // 4), used // 4)
        core.mask(pl.ds(first, used // 4), first, used // 4)
        core.feed_back(pl.ds(first, used // 4))

    @pl.loop(0, model // BLOCK)
    def _(index):
        at = pl.ds(pl.multiple_of(index * BLOCK, BLOCK), BLOCK)
        grad = core.grad[:used, at]
        g_down[at] = dot_rows(grad, core.hidden[:used]).astype(BF16)
        g_out[at] = dot_rows(grad, core.attended[:used]).astype(BF16)
        g_up[at] = dot_rows(core.normed2[:used, at], core.slope[:used]).astype(BF16)

    @pl.loop(0, used // BLOCK)
    def _(block):
        core.attend_grad(block)

    for ref in (core.d_keys, core.d_values, core.d_norms):
        ref[...] = jnp.zeros_like(ref)
    @pl.loop(0, used // BLOCK)
    def _(index):
        block = used // BLOCK - 1 - index
        core.attend_back(block)
        part_of(scaled_grad, block, BLOCK)[...] = core.input_grad(block).astype(BF16)

    core.keyvalue_grad()

    @pl.loop(0, used // BLOCK)
    def _(block):
        at = pl.ds(pl.multiple_of(block * BLOCK, BLOCK), BLOCK)
        more = dot_cols(core.d_keyvalue[at], core.w_keyvalue[...]) * core.params[0:1]
        scaled_grad[at] = (scaled_grad[at].astype(F32) + more).astype(BF16)

    scaled_grad[used:] = jnp.zeros((rows - used, model), BF16)

    @pl.loop(0, model // BLOCK)
    def _(index):
        at = pl.ds(pl.multiple_of(index * BLOCK, BLOCK), BLOCK)
        normed = core.normed1[:used, at]
        g_query[at] = dot_rows(normed, core.d_query[:used]).astype(BF16)
        g_keyvalue[at] = dot_rows(normed, core.d_keyvalue[:used]).astype(BF16)

    for i in range(4):
        g_norms[i : i + 1] = jnp.sum(core.d_norms[i], axis=0, keepdims=True)
    for i, more in enumerate(core.keyvalue_norms()):
        g_norms[i : i + 1] += more


def run_plain(seq_lengths, norms, arrays, z):
    tokens, cotangent, w_query, w_keyvalue, w_up, w_down, w_out = arrays
    width, model = w_query.shape[1], tokens.shape[1]
    wide = z.wide
    pad = jnp.pad(w_query[:, width // 128 * 128 :], ((0, 0), (0, wide - width)))
    lane, start = lax.iota(jnp.int32, 128)[None], width % 128
    vectors = jnp.pad(jnp.stack(norms, axis=1), ((0, 0), (start, 124 - start)))
    tail = jnp.where(lane < start, pad, vectors)
    query = jnp.concatenate([w_query[:, : width // 128 * 128], tail], axis=1)
    out = jnp.pad(w_out, ((0, 0), (0, wide - width)))
    gathered = [lax.all_gather(a, "tensor", axis=0, tiled=True) for a in (tokens, cotangent)]
    gathered += [lax.all_gather(a, "dp", axis=0, tiled=True) for a in (query, w_keyvalue, w_up, w_down, out)]
    shape = jax.ShapeDtypeStruct
    results = pl.pallas_call(
        functools.partial(plain_kernel, z),
        out_shape=[shape((z.rows, model), BF16)] * 2
        + [shape((model, n), BF16) for n in (wide, 128, wide, z.units, z.units)]
        + [shape((4, model), F32)],
        in_specs=[pl.BlockSpec(memory_space=pltpu.SMEM)] + [INVMEM] * len(gathered),
        out_specs=[INVMEM] * 8,
        scratch_shapes=[pltpu.VMEM(*entry) for entry in own_shapes(z).values()] + [pltpu.VMEM((n, model), BF16) for n in (z.used, z.rows)],
        compiler_params=pltpu.CompilerParams(vmem_limit_bytes=67043328),
        name="plain_layer",
    )(seq_lengths, *gathered)
    names = ("tensor", "tensor") + ("dp",) * 5
    sums = [
        lax.psum_scatter(p.astype(F32), n, scatter_dimension=0, tiled=True) for p, n in zip(results[:7], names)
    ]
    norm_sums = lax.psum_scatter(results[7], "dp", scatter_dimension=1, tiled=True)
    shared_kv = lax.all_gather(sums[3], "tensor")
    shared_norms = lax.all_gather(jnp.pad(norm_sums, ((0, 4), (0, 0))), "tensor")
    return sums[0], sums[1], sums[2], sums[4], sums[5], sums[6], shared_kv, shared_norms


def run_whole(seq_lengths, norms, arrays, z):
    arrays_of, semaphores = fused_specs(z)
    scratch = [pltpu.VMEM(*entry) for entry in arrays_of.values()]
    scratch += [pltpu.SemaphoreType.DMA(shape) for shape in semaphores.values()]
    return pl.pallas_call(
        functools.partial(fused_kernel, z, tuple(arrays_of) + tuple(semaphores)),
        out_shape=[jax.ShapeDtypeStruct(shape, F32) for shape in output_shapes(z)],
        in_specs=[pl.BlockSpec(memory_space=pltpu.SMEM)]
        + [INVMEM] * 4
        + [INVMEM if packed else ANY for packed in (False, False, True, False, False, False, True)],
        out_specs=[ANY] * len(OUTPUTS),
        scratch_shapes=scratch,
        compiler_params=pltpu.CompilerParams(collective_id=0, has_side_effects=True, vmem_limit_bytes=67043328),
        name="layer",
    )(seq_lengths, *norms, *arrays)


def run_layer(seq_lengths, norms, arrays, nd, nt):
    tokens, _, w_query, w_keyvalue, w_up, _, _ = arrays
    heads, own, units = w_query.shape[1] // 64, w_query.shape[0], w_up.shape[1]
    slots, model = tokens.shape
    z = types.SimpleNamespace(
        nd=nd, nt=nt, heads=heads, rows=slots * nt, model=model, stack=heads * BLOCK, units=units, used=SEQ_MOST,
        wide=(heads * 64 + 4 + 127) // 128 * 128, own=own, slots=slots,
    )
    run = run_whole if own % 32 == 0 and slots == 2 * BLOCK and nt == 4 and SEQ_MOST == 7 * BLOCK else run_plain
    sums = run(seq_lengths, norms, arrays, z)
    steps = 2 if own % 16 == 0 else 1
    shape = jax.ShapeDtypeStruct

    def block(rows, columns):
        return pl.BlockSpec((rows // steps, columns), lambda i: (i, 0))

    width = heads * 64
    token_rows = block(slots, model)
    weights = [block(own, n) for n in (z.wide, z.wide, units, units)]
    shared = [
        pl.BlockSpec((nt, own // steps, 128), lambda i: (0, i, 0)),
        pl.BlockSpec((nt, 8, own), lambda i: (0, 0, 0)),
    ]
    results = pl.pallas_call(
        functools.partial(finish_kernel, z),
        grid=(steps,),
        out_shape=[shape((slots, model), BF16), shape((slots, model), F32)]
        + [shape((own, n), F32) for n in (width, 128, width, units, units)]
        + [shape((own,), F32)] * 4,
        in_specs=[pl.BlockSpec(memory_space=pltpu.SMEM)] + [token_rows] * 4 + weights + shared,
        out_specs=[token_rows] * 2
        + [block(own, n) for n in (width, 128, width, units, units)]
        + [pl.BlockSpec((own,), lambda i: (0,))] * 4,
        compiler_params=pltpu.CompilerParams(vmem_limit_bytes=67043328),
        name="finish",
    )(seq_lengths, *arrays[:2], *sums)
    return tuple(results)


def shards(
    tokens,
    cotangent,
    seq_lengths,
    w_query,
    w_keyvalue,
    w_out,
    w_up,
    w_down,
    norm1_gain,
    norm1_bias,
    norm2_gain,
    norm2_bias,
):
    norms = (norm1_gain, norm1_bias, norm2_gain, norm2_bias)
    arrays = (tokens, cotangent, w_query, w_keyvalue, w_up, w_down, w_out)
    return run_layer(seq_lengths, norms, arrays, lax.axis_size("dp"), lax.axis_size("tensor"))


def solution(mesh):
    return jax.shard_map(
        shards,
        mesh=mesh,
        in_specs=(
            P(("dp", "tensor"), None),
            P(("dp", "tensor"), None),
            P("dp", None),
            P("dp", "tensor"),
            P("dp", None),
            P("dp", "tensor"),
            P("dp", "tensor"),
            P("dp", "tensor"),
            P("dp"),
            P("dp"),
            P("dp"),
            P("dp"),
        ),
        out_specs=(
            P(("dp", "tensor"), None),
            P(("dp", "tensor"), None),
            P("dp", "tensor"),
            P("dp", None),
            P("dp", "tensor"),
            P("dp", "tensor"),
            P("dp", "tensor"),
            P("dp"),
            P("dp"),
            P("dp"),
            P("dp"),
        ),
        check_vma=False,
    )
```

```python
import functools
import math
import types

import jax
import jax.numpy as jnp
from jax import lax
from jax.experimental import pallas as pl
from jax.experimental.pallas import tpu as pltpu
from jax.sharding import PartitionSpec as P

ROT = 16
SEQ_LEAST = 1024
SEQ_MOST = 1792
BLOCK = 256
WIDE = 3
EPS = 1e-05
NEG = -1e30
F32 = jnp.float32
BF16 = jnp.bfloat16


def dot(left, right):
    return jnp.dot(left, right, preferred_element_type=F32)


def dot_rows(left, right):
    return lax.dot_general(left, right, (((0,), (0,)), ((), ())), preferred_element_type=F32)


def dot_cols(left, right):
    return lax.dot_general(left, right, (((1,), (1,)), ((), ())), preferred_element_type=F32)


def lanes_of(rows):
    return lax.broadcasted_iota(jnp.int32, (rows, 128), 1)


def swap_halves(x, lane):
    return jnp.where(lane < ROT // 2, pltpu.roll(x, 128 - ROT // 2, 1), pltpu.roll(x, ROT // 2, 1))


def three_parts(x):
    high = x.astype(BF16).astype(F32)
    middle = (x - high).astype(BF16).astype(F32)
    return high, middle, x - high - middle


def unit_heads(wide, heads):
    pieces = []
    for h in range(heads):
        piece = wide[:, h // 2 * 128 : h // 2 * 128 + 128]
        pieces.append(piece if h % 2 == 0 else pltpu.roll(piece, 64, 1))
    return pieces


def join_heads(pieces, lane):
    wide = []
    for h in range(0, len(pieces), 2):
        second = pltpu.roll(pieces[h + 1], 64, 1) if h + 1 < len(pieces) else jnp.zeros_like(pieces[h])
        wide.append(jnp.where(lane < 64, pieces[h], second))
    return jnp.concatenate(wide, axis=1)


class Core:
    def __init__(self, heads, length, used, **refs):
        self.heads, self.length, self.used = heads, length, used
        self.__dict__.update(refs)
        stack = heads * BLOCK
        self.d_query = self.attended
        self.d_stack = self.scores.at[0:stack, 0:128]
        self.d_keys = self.scores.at[stack : stack + used, 0:128]
        self.d_values = self.scores.at[stack : stack + used, 128:256]

    def past(self, first, shape, axis):
        return lax.broadcasted_iota(jnp.int32, shape, axis) + first >= self.length

    def tables(self, part):
        count = self.cosine.shape[0] // BLOCK // 2

        @pl.loop(part * count, part * count + count)
        def _(index):
            at = pl.ds(pl.multiple_of(index * BLOCK, BLOCK), BLOCK)
            lane = lanes_of(BLOCK)
            row = lax.broadcasted_iota(jnp.int32, (BLOCK, 128), 0) + index * BLOCK
            position = jnp.where(row >= self.length, row - self.length, row).astype(F32)
            exponent = jnp.where(lane < ROT // 2, lane, lane - ROT // 2).astype(F32) * (-2.0 / ROT)
            angle = position * jnp.exp(exponent * math.log(10000.0))
            sine = jnp.sin(angle)
            self.cosine[at] = jnp.where(lane < ROT, jnp.cos(angle), 1.0)
            self.sine[at] = jnp.where(lane < ROT // 2, -sine, jnp.where(lane < ROT, sine, 0.0))

    def unpack_params(self):
        start = self.heads * 64
        turned = self.w_query[:, start // 128 * 128 : start // 128 * 128 + 128].T.astype(F32)
        self.params[0:4] = turned[start % 128 : start % 128 + 4]

    def normalize(self, block):
        at = pl.ds(pl.multiple_of(block * BLOCK, BLOCK), BLOCK)
        x = self.tokens[at].astype(F32)
        centered = x - jnp.mean(x, axis=1, keepdims=True)
        scaled = centered * lax.rsqrt(jnp.mean(centered * centered, axis=1, keepdims=True) + EPS)
        gain1, bias1, gain2, bias2 = (self.params[i : i + 1] for i in range(4))
        self.scaled[at] = scaled.astype(BF16)
        self.normed1[at] = (scaled * gain1 + bias1).astype(BF16)
        self.normed2[at] = (scaled * gain2 + bias2).astype(BF16)

    def project(self, block):
        first = pl.multiple_of(block * BLOCK, BLOCK)
        at = pl.ds(first, BLOCK)
        lane = lanes_of(BLOCK)
        cosine, sine = self.cosine[at], self.sine[at]
        past = self.past(first, (BLOCK, 128), 0)
        normed = self.normed1[at]
        key_value = dot(normed, self.w_keyvalue[...])
        keys = key_value * cosine + swap_halves(key_value, lane) * sine
        hidden_key = jnp.where(past, 0.0, NEG)
        extra = jnp.where(lane == 64, hidden_key, jnp.where(lane < 68, -1.0, 0.0))
        self.keys[at] = jnp.where(lane < 64, keys, extra).astype(BF16)
        ones = jnp.where(lane < 67, 1.0, 0.0)
        self.values[at] = jnp.where(lane < 64, pltpu.roll(key_value, 64, 1), ones).astype(BF16)
        query = dot(normed, self.w_query[...])
        flag = jnp.where((lane == 64) & past, 1.0, 0.0)
        for h, piece in enumerate(unit_heads(query, self.heads)):
            turned = (piece * cosine + swap_halves(piece, lane) * sine).astype(BF16).astype(F32)
            turned = turned * (64 ** (-0.5))
            self.queries[block, h * BLOCK : (h + 1) * BLOCK] = jnp.where(lane < 64, turned, flag).astype(BF16)

    def key_blocks(self, block):
        first = SEQ_LEAST // BLOCK if block * BLOCK >= SEQ_MOST else 0
        return range(first, block + 1)

    def attend(self, block):
        rows = self.heads * BLOCK
        query = self.queries[block]
        lane = lanes_of(rows)
        top = jnp.full((rows, BLOCK), -3e38, F32)
        for index, j in enumerate(self.key_blocks(block)):
            scores = dot_cols(query, self.keys[j * BLOCK : (j + 1) * BLOCK])
            if j == block:
                row = lax.rem(lax.broadcasted_iota(jnp.int32, (rows, BLOCK), 0), BLOCK)
                column = lax.broadcasted_iota(jnp.int32, (rows, BLOCK), 1)
                scores = jnp.where(column <= row, scores, NEG)
            self.scores[index * rows : (index + 1) * rows] = scores
            top = jnp.maximum(top, scores)
        top = jnp.max(top, axis=1, keepdims=True)
        total = jnp.zeros((rows, 128), F32)
        for index, j in enumerate(self.key_blocks(block)):
            probs = jnp.exp(self.scores[index * rows : (index + 1) * rows] - top).astype(BF16)
            total = total + dot(probs, self.values[j * BLOCK : (j + 1) * BLOCK])
        weight = jnp.sum(jnp.where(lane == 64, total, 0.0), axis=1, keepdims=True)
        output = total / weight
        pieces = [output[h * BLOCK : (h + 1) * BLOCK] for h in range(self.heads)]
        self.attended[block * BLOCK : (block + 1) * BLOCK] = join_heads(pieces, lanes_of(BLOCK)).astype(BF16)
        high, middle, low = three_parts(top + jnp.log(weight))
        parts = jnp.where(lane == 65, high, jnp.where(lane == 66, middle, low))
        self.queries[block] = jnp.where((lane >= 65) & (lane < 68), parts, query.astype(F32)).astype(BF16)

    def feed(self, at):
        up = dot(self.normed2[at], self.w_up[...])
        normal = 0.5 * (1.0 + lax.erf(up * (1.0 / math.sqrt(2.0))))
        self.hidden[at] = (up * normal).astype(BF16)
        density = jnp.exp(-0.5 * up * up) * (1.0 / math.sqrt(2.0 * math.pi))
        self.slope[at] = (normal + up * density).astype(BF16)

    def mix(self, at):
        return dot_cols(self.attended[at], self.w_out[...]) + dot_cols(self.hidden[at], self.w_down[...])

    def mask(self, at, first, rows):
        past = self.past(first, (rows, 1), 0)
        self.grad[at] = jnp.where(past, 0.0, self.cotangent[at].astype(F32)).astype(BF16)

    def feed_back(self, at):
        d_hidden = dot(self.grad[at], self.w_down[...])
        self.slope[at] = (d_hidden * self.slope[at].astype(F32)).astype(BF16)

    def d_attended(self, block, first, size):
        across = self.hidden.shape[1] // 128
        row = block // across * (self.heads * BLOCK) + first
        lane = lax.rem(block, across) * 128
        return self.hidden.at[pl.ds(pl.multiple_of(row, BLOCK), size), pl.ds(pl.multiple_of(lane, 128), 128)]

    def attend_grad(self, block):
        first = pl.multiple_of(block * BLOCK, BLOCK)
        at = pl.ds(first, BLOCK)
        lane = lanes_of(BLOCK)
        grads = unit_heads(dot(self.grad[at], self.w_out[...]), self.heads)
        outputs = unit_heads(self.attended[at].astype(F32), self.heads)
        for h in range(self.heads):
            grad = grads[h].astype(BF16).astype(F32)
            delta = jnp.sum(jnp.where(lane < 64, grad * outputs[h], 0.0), axis=1, keepdims=True)
            high, middle, low = three_parts(-delta)
            parts = jnp.where(lane == 64, high, jnp.where(lane == 65, middle, jnp.where(lane == 66, low, 0.0)))
            self.d_attended(block, h * BLOCK, BLOCK)[...] = jnp.where(lane < 64, grad, parts).astype(BF16)

    def attend_back(self, block):
        rows = self.heads * BLOCK
        query, grad = self.queries[block], self.d_attended(block, 0, rows)[...]

        def span(first, size, diagonal):
            at = pl.ds(pl.multiple_of(first, BLOCK), size)
            keys, values = self.keys[at], self.values[at]
            scores, d_probs = dot_cols(keys, query), dot_cols(values, grad)
            if diagonal:
                key = lax.broadcasted_iota(jnp.int32, (size, rows), 0)
                row = lax.rem(lax.broadcasted_iota(jnp.int32, (size, rows), 1), BLOCK) + (size - BLOCK)
                scores = jnp.where(key <= row, scores, NEG)
            probs = jnp.exp(scores)
            d_scores = (probs * d_probs).astype(BF16)
            self.d_values[at] += dot(probs.astype(BF16), grad)
            self.d_keys[at] += dot(d_scores, query)
            d_query = dot_rows(d_scores, keys)
            if diagonal:
                self.d_stack[...] = d_query
            else:
                self.d_stack[...] += d_query

        last = lax.rem(block, WIDE)
        for size in range(WIDE):

            @pl.when(last == size)
            def _():
                span((block - size) * BLOCK, (size + 1) * BLOCK, True)

        @pl.loop(0, block // WIDE)
        def _(index):
            span(index * WIDE * BLOCK, WIDE * BLOCK, False)

        at = pl.ds(pl.multiple_of(block * BLOCK, BLOCK), BLOCK)
        pieces = [
            self.turn_back(self.d_stack[h * BLOCK : (h + 1) * BLOCK], at) * (64 ** (-0.5)) for h in range(self.heads)
        ]
        self.d_query[at] = join_heads(pieces, lanes_of(BLOCK)).astype(BF16)

    def turn_back(self, x, at):
        return x * self.cosine[at] - swap_halves(x, lanes_of(BLOCK)) * self.sine[at]

    def keyvalue_grad(self):
        rows = self.d_keyvalue.shape[0]

        @pl.loop(0, self.used // BLOCK)
        def _(block):
            at = pl.ds(pl.multiple_of(block * BLOCK, BLOCK), BLOCK)
            d_keys = self.turn_back(self.d_keys[at], at)
            d_values = pltpu.roll(self.d_values[at], 64, 1)
            self.d_keyvalue[at] = jnp.where(lanes_of(BLOCK) < 64, d_keys, d_values).astype(BF16)

        self.d_keyvalue[self.used :] = jnp.zeros((rows - self.used, 128), BF16)

    def keyvalue_norms(self):
        weight = self.w_keyvalue[...].astype(F32)
        grad = self.d_keyvalue[: self.used]
        gain = jnp.sum(dot_rows(self.scaled[: self.used], grad) * weight, axis=1, keepdims=True)
        bias = jnp.sum(jnp.sum(grad.astype(F32), axis=0, keepdims=True) * weight, axis=1, keepdims=True)
        lane = lanes_of(weight.shape[0])
        turned = jnp.where(lane == 0, gain, bias).T
        return turned[0:1], turned[1:2]

    def input_grad(self, block):
        at = pl.ds(pl.multiple_of(block * BLOCK, BLOCK), BLOCK)
        d_normed1 = dot_cols(self.d_query[at], self.w_query[...])
        d_normed2 = dot_cols(self.slope[at], self.w_up[...])
        scaled = self.scaled[at].astype(F32)
        for i, value in enumerate((d_normed1 * scaled, d_normed1, d_normed2 * scaled, d_normed2)):
            self.d_norms[i] += jnp.sum(value.reshape(BLOCK // 8, 8, -1), axis=0)
        return d_normed1 * self.params[0:1] + d_normed2 * self.params[2:3]


MESH = pl.DeviceIdType.MESH
INVMEM = pl.BlockSpec(memory_space=pltpu.VMEM)
ANY = pl.BlockSpec(memory_space=pl.ANY)


class Axis:
    def __init__(self, name, size):
        self.name, self.size, self.half = name, size, size // 2
        self.me = lax.axis_index(name)
        self.row, self.par = self.me // 2, self.me % 2
        self.pair = self.me + 1 - 2 * self.par

    def other_row(self, step):
        return lax.rem(self.row + step + self.half, self.half)

    def line(self, step):
        return self.other_row(step) * 2 + self.par

    def greet(self, barrier, peers):
        for peer in peers:
            pl.semaphore_signal(barrier, inc=1, device_id={self.name: peer}, device_id_type=MESH)
        return len(peers)


def remote(src, dst, send, recv, axis, peer):
    return pltpu.make_async_remote_copy(
        src_ref=src, dst_ref=dst, send_sem=send, recv_sem=recv, device_id={axis.name: peer}, device_id_type=MESH
    )


def part_of(ref, index, rows):
    return ref.at[pl.ds(pl.multiple_of(index * rows, rows), rows)]


class Gather:
    def __init__(self, axis, src, dst, send, recv, local, part=0, parts=1):
        self.axis, self.dst, self.send, self.recv = axis, dst, send, recv
        self.half, self.part, self.parts = axis.half, part, parts
        self.src = part_of(src, part, src.shape[0] // parts)
        self.copy = pltpu.make_async_copy(self.src, self.slot(axis.me), local)

    def slot(self, index):
        return part_of(self.dst, index * self.parts + self.part, self.src.shape[0])

    def along(self, row, way, own=False):
        slot = self.slot(2 * row + self.axis.par)
        send = self.send.at[row if way > 0 else self.half + row]
        peer = self.axis.me + 2 * way
        return remote(self.src if own else slot, slot, send, self.recv.at[row], self.axis, peer)

    def across(self, row, own=False):
        slot = self.slot(2 * row + self.axis.par)
        sems = self.send.at[2 * self.half + row], self.recv.at[self.half + row]
        return remote(self.src if own else slot, slot, *sems, self.axis, self.axis.pair)

    def start_line(self):
        @pl.when(self.axis.row + 1 < self.half)
        def _():
            self.along(self.axis.row, 1, own=True).start()

        @pl.when(self.axis.row > 0)
        def _():
            self.along(self.axis.row, -1, own=True).start()

    def start_pair(self):
        self.across(self.axis.row, own=True).start()

    def pass_on(self, distance):
        if distance >= self.half:
            return
        me = self.axis.row

        @pl.when(me >= distance)
        def _():
            row = me - distance
            self.along(row, 1).wait_recv()

            @pl.when(me + 1 < self.half)
            def _():
                self.along(row, 1).start()

            self.across(row).start()

        @pl.when(me + distance < self.half)
        def _():
            row = me + distance
            self.along(row, -1).wait_recv()

            @pl.when(me > 0)
            def _():
                self.along(row, -1).start()

            self.across(row).start()

    def pair_arrived(self, row):
        slot = self.slot(2 * row + 1 - self.axis.par)
        sems = self.send.at[2 * self.half + row], self.recv.at[self.half + row]
        remote(slot, slot, *sems, self.axis, self.axis.pair).wait_recv()

    def arrive(self):
        self.copy.wait()
        for row in range(self.half):
            self.pair_arrived(row)

    def leave(self):
        for row in range(self.half):
            self.across(row).wait_send()

            @pl.when((self.axis.row >= row) & (self.axis.row + 1 < self.half))
            def _():
                self.along(row, 1).wait_send()

            @pl.when((self.axis.row <= row) & (self.axis.row > 0))
            def _():
                self.along(row, -1).wait_send()


class Reduce:
    def __init__(self, axis, part, out, held, last, send, recv):
        self.axis, self.part, self.out, self.held, self.last = axis, part, out, held, last
        self.send, self.recv, self.rows = send, recv, out.shape[0]
        self.chunk = 64 if self.rows % 64 == 0 else self.rows

    def first(self, row):
        block = part_of(self.part, 2 * row + 1 - self.axis.par, self.rows)
        held = part_of(self.held, row, self.rows)
        return remote(block, held, self.send.at[row], self.recv.at[row], self.axis, self.axis.pair)

    def second(self, step):
        index = self.axis.half + step
        block = part_of(self.held, self.axis.other_row(step), self.rows)
        last = part_of(self.last, step - 1, self.rows)
        return remote(block, last, self.send.at[index], self.recv.at[index], self.axis, self.axis.line(step))

    def start(self):
        for step in range(self.axis.half):
            self.first(self.axis.other_row(step + 1)).start()

    def chunks(self, body):
        @pl.loop(0, self.rows // self.chunk)
        def _(index):
            body(pl.multiple_of(index * self.chunk, self.chunk))

    def total(self, row, at):
        part = self.part[pl.ds((2 * row + self.axis.par) * self.rows + at, self.chunk)].astype(F32)
        return part + self.held[pl.ds(row * self.rows + at, self.chunk)].astype(F32)

    def middle(self):
        for step in range(1, self.axis.half):
            row = self.axis.other_row(step)
            self.first(row).wait()

            def add(at, row=row):
                self.held[pl.ds(row * self.rows + at, self.chunk)] = self.total(row, at).astype(self.held.dtype)

            self.chunks(add)
            self.second(step).start()

        self.first(self.axis.row).wait()

        def keep(at):
            self.out[pl.ds(at, self.chunk)] = self.total(self.axis.row, at)

        self.chunks(keep)

    def end(self):
        for step in range(1, self.axis.half):
            self.second(step).wait()

        def add(at):
            total = self.out[pl.ds(at, self.chunk)]
            for step in range(1, self.axis.half):
                total = total + self.last[pl.ds((step - 1) * self.rows + at, self.chunk)].astype(F32)
            self.out[pl.ds(at, self.chunk)] = total

        self.chunks(add)


class Stream:
    def __init__(self, axis, part, out, held, last, pair_send, pair_recv, line_send, line_recv):
        self.axis, self.part, self.out, self.held, self.last = axis, part, out, held, last
        self.pair_sems, self.line_sems = (pair_send, pair_recv), (line_send, line_recv)

    def split(self, chunk):
        return chunk // 4, chunk // 2 % 2, chunk % 2

    def pair_copy(self, chunk):
        row, _, half = self.split(chunk)
        index = 2 * row + half
        send, recv = (sems.at[index] for sems in self.pair_sems)
        held = part_of(self.held, index, BLOCK)
        return remote(part_of(self.part, chunk, BLOCK), held, send, recv, self.axis, self.axis.pair)

    def line_copy(self, chunk):
        row, _, half = self.split(chunk)
        send, recv = (sems.at[half] for sems in self.line_sems)
        held = part_of(self.held, 2 * row + half, BLOCK)
        return remote(held, part_of(self.last, half, BLOCK), send, recv, self.axis, self.axis.line(1))

    def give(self, chunk):
        @pl.when(self.axis.par != self.split(chunk)[1])
        def _():
            self.pair_copy(chunk).start()

    def take(self, chunk):
        row, par, half = self.split(chunk)

        @pl.when(self.axis.par == par)
        def _():
            self.pair_copy(chunk).wait_recv()

            def total(at):
                part = self.part[pl.ds(chunk * BLOCK + at, 32)].astype(F32)
                return part + self.held[pl.ds((2 * row + half) * BLOCK + at, 32)].astype(F32)

            @pl.when(self.axis.row == row)
            def _():
                @pl.loop(0, BLOCK // 32)
                def _(index):
                    at = pl.multiple_of(index * 32, 32)
                    self.out[pl.ds(half * BLOCK + at, 32)] = total(at)

            @pl.when(self.axis.row != row)
            def _():
                @pl.loop(0, BLOCK // 32)
                def _(index):
                    at = pl.multiple_of(index * 32, 32)
                    self.held[pl.ds((2 * row + half) * BLOCK + at, 32)] = total(at).astype(BF16)

                self.line_copy(chunk).start()

    def end(self, chunk):
        row, par, half = self.split(chunk)

        @pl.when(self.axis.par != par)
        def _():
            self.pair_copy(chunk).wait_send()

        @pl.when((self.axis.par == par) & (self.axis.row != row))
        def _():
            self.line_copy(chunk).wait_send()

        @pl.when((self.axis.par == par) & (self.axis.row == row))
        def _():
            self.line_copy(chunk).wait_recv()

            @pl.loop(0, BLOCK // 32)
            def _(index):
                at = pl.multiple_of(index * 32, 32)
                rows = pl.ds(half * BLOCK + at, 32)
                self.out[rows] += self.last[rows].astype(F32)

WEIGHTS = ("w_query", "w_keyvalue", "w_up", "w_down", "w_out")
INPUTS = ("tokens", "cotangent") + WEIGHTS
OUTPUTS = ("mixed_sum", "scaled_sum", "s_w_query", "s_w_out", "s_w_up", "s_w_down", "shared_kv", "shared_norms")


def own_shapes(z):
    wide_rows = (z.rows, z.model)
    return dict(
        params=((8, z.model), F32), cosine=((z.rows, 128), F32), sine=((z.rows, 128), F32),
        normed1=(wide_rows, BF16), normed2=(wide_rows, BF16),
        queries=((z.rows // BLOCK, z.stack, 128), BF16), keys=((z.rows, 128), BF16), values=((z.rows, 128), BF16),
        scores=((z.used // BLOCK * z.stack, BLOCK), F32), attended=((z.rows, z.wide), BF16), hidden=((z.rows, z.units), BF16),
        slope=((z.rows, z.units), BF16), d_keyvalue=((z.rows, 128), BF16), d_norms=((4, 8, z.model), F32),
    )


class Names:
    def __init__(self, names, refs):
        self.__dict__.update(zip(names, refs, strict=True))


def output_shapes(z):
    return [
        (z.slots, z.model), (z.slots, z.model), (z.own, z.wide), (z.own, z.wide), (z.own, z.units), (z.own, z.units),
        (z.nt, z.own, 128), (z.nt, 8, z.own),
    ]


def fused_specs(z):
    half, model = z.nd // 2, z.model
    columns = dict(zip(WEIGHTS, (z.wide, 128, z.units, z.units, z.wide)))
    arrays = own_shapes(z)
    arrays.update({name: (shape, F32) for name, shape in zip(OUTPUTS, output_shapes(z))})
    arrays.update(pack_query=((z.own, z.wide), BF16), pack_out=((z.own, z.wide), BF16))
    arrays.update(tokens=((z.rows, model), BF16), cotangent=((z.rows, model), BF16))
    arrays.update({name: ((model, columns[name]), BF16) for name in WEIGHTS})
    arrays.update(mixed=((z.rows, model), BF16), held_mixed=((z.rows // 2, model), BF16))
    arrays.update(last_mixed=((z.slots, model), BF16), held_scaled=((z.rows // 2, model), BF16))
    arrays.update(last_scaled=((z.slots, model), BF16))
    for name in WEIGHTS:
        arrays["g_" + name] = ((model, columns[name]), BF16)
        arrays["held_" + name] = ((half * z.own, columns[name]), BF16)
        arrays["last_" + name] = ((max(half - 1, 1) * z.own, columns[name]), BF16)
    arrays.update(held_pack=((z.rows // 2, 128), BF16), last_pack=((z.slots, 128), BF16), pack_sum=((z.slots, 128), F32))
    arrays.update(g_norms=((z.nd * 8, z.own), F32), held_norms=((half * 8, z.own), F32))
    arrays.update(last_norms=((max(half - 1, 1) * 8, z.own), F32))
    semaphores = dict(send_mixed=(z.nt,), recv_mixed=(z.nt,), send_pack=(z.nt,), recv_pack=(z.nt,), send_norms=(z.nd,), recv_norms=(z.nd,))
    for name in INPUTS:
        count = z.nd if name in WEIGHTS else z.nt
        shape = (2, count) if name == "tokens" else (count,)
        semaphores.update({"send_" + name: shape[:-1] + (count // 2 * 3,), "recv_" + name: shape})
    for name in WEIGHTS:
        semaphores.update({"out_" + name: (z.nd,), "in_" + name: (z.nd,)})
    semaphores.update(pair_send=(4,), pair_recv=(4,), line_send=(2,), line_recv=(2,), local=(len(INPUTS) + 1,))
    semaphores.update(share_send=(2 * z.nt,), share_recv=(2 * z.nt,), store=(len(OUTPUTS),))
    return arrays, semaphores


def fused_kernel(z, names, *refs):
    vectors, refs = refs[1:5], refs[:1] + refs[5:]
    it = Names(("seq",) + tuple("i_" + n for n in INPUTS) + tuple("o_" + n for n in OUTPUTS) + names, refs)
    dp, tensor = Axis("dp", z.nd), Axis("tensor", z.nt)
    rows, model, used, slots = z.rows, z.model, z.used, z.slots
    core = Core(z.heads, it.seq[0, 0], z.used, **{n: getattr(it, n) for n in tuple(own_shapes(z)) + INPUTS}, grad=it.cotangent, scaled=it.tokens)
    barrier = pltpu.get_barrier_semaphore()
    expected = dp.greet(barrier, [dp.pair] + [dp.line(step) for step in range(1, dp.half)])
    expected += tensor.greet(barrier, [lax.rem(tensor.me + step, tensor.size) for step in range(1, tensor.size)])

    width = z.heads * 64
    pad = jnp.zeros((z.own, z.wide - width), BF16)
    lane = lanes_of(z.own)
    first = width // 128 * 128
    tail = jnp.concatenate([it.i_w_query[:, first:].astype(F32), pad.astype(F32)], axis=1)
    it.pack_query[:, :first] = it.i_w_query[:, :first]
    start = width - first
    turned = [v[...].astype(F32).reshape(1, z.own) for v in vectors]
    turned = jnp.concatenate([jnp.zeros((start, z.own), F32)] + turned + [jnp.zeros((124 - start, z.own), F32)])
    turned = jnp.concatenate([turned, jnp.zeros((128, 128 - z.own), F32)], axis=1).T[: z.own]
    it.pack_query[:, first:] = jnp.where(lane < start, tail, turned).astype(BF16)
    it.pack_out[:, :first] = it.i_w_out[:, :first]
    it.pack_out[:, first:] = jnp.concatenate([it.i_w_out[:, first:], pad], axis=1)
    sources = dict(w_query=it.pack_query, w_out=it.pack_out)
    g = {}
    for i, name in enumerate(INPUTS):
        axis = dp if name in WEIGHTS else tensor
        source = sources.get(name, getattr(it, "i_" + name))
        send, recv = getattr(it, "send_" + name), getattr(it, "recv_" + name)
        g[name] = Gather(axis, source, getattr(it, name), send, recv, it.local.at[i])
    tokens = [
        Gather(tensor, it.i_tokens, it.tokens, it.send_tokens.at[h], it.recv_tokens.at[h], it.local.at[len(INPUTS) * h], h, 2)
        for h in range(2)
    ]
    pl.semaphore_wait(barrier, expected)

    def hand_on(names, distance):
        for name in names:
            g[name].pass_on(distance)

    small = ("w_query", "w_keyvalue")
    for gather in tokens + [g["cotangent"]]:
        gather.start_line()
        gather.start_pair()
    for name in small:
        g[name].start_line()
        g[name].start_pair()
    g["w_up"].start_pair()
    for gather in tokens + [g[name] for name in INPUTS[1:]]:
        gather.copy.start()
    core.tables(0)
    hand_on(small, 1)
    g["w_up"].start_line()
    core.tables(1)
    hand_on(small, 2)
    hand_on(small, 3)
    hand_on(("w_up",), 1)
    g["w_down"].start_line()
    for name in small:
        g[name].arrive()
    core.unpack_params()

    for gather in tokens:
        gather.copy.wait()
    other, other_pair = tensor.line(1), tensor.line(1) + tensor.pair - tensor.me

    @pl.loop(0, 4)
    def _(index):
        @pl.when(index == 1)
        def _():
            for gather in tokens:
                gather.pair_arrived(tensor.row)
            hand_on(("w_up",), 2)
            g["w_down"].start_pair()
            g["w_out"].start_line()

        for half in range(2):

            @pl.when(index == 2 + half)
            def _():
                tokens[half].pass_on(1)
                if half == 0:
                    hand_on(("w_up",), 3)
                tokens[half].pair_arrived(1 - tensor.row)
                tokens[half].leave()

        late = index // 2
        first = jnp.where(index == 0, 2 * tensor.me, 2 * tensor.pair)
        blocks = [
            (1 - late) * first + late * (2 * other + index - 2),
            (1 - late) * (first + 1) + late * (2 * other_pair + index - 2),
        ]
        for block in blocks:
            core.normalize(block)
            core.project(block)

        @pl.when(index == 2)
        def _():
            hand_on(("w_down",), 1)
            g["w_out"].start_pair()

    hand_on(("w_down",), 2)
    g["w_up"].arrive()

    @pl.loop(0, rows // slots)
    def _(index):
        core.feed(pl.ds(pl.multiple_of(index * slots, slots), slots))
        for step, (name, distance) in enumerate((("w_down", 3), ("w_out", 1), ("w_out", 2), ("w_out", 3))):

            @pl.when(index == step)
            def _():
                hand_on((name,), distance)

    for block in range(rows // BLOCK):
        core.attend(block)
    g["cotangent"].pass_on(1)
    g["w_down"].arrive()
    g["cotangent"].arrive()
    g["cotangent"].leave()

    quarter = used // 4

    @pl.loop(0, 4)
    def _(index):
        first = pl.multiple_of(index * quarter, quarter)
        core.mask(pl.ds(first, quarter), first, quarter)

    r = {}
    for name in WEIGHTS:
        out = getattr(it, "s_" + name) if name != "w_keyvalue" else it.shared_kv.at[tensor.me]
        some = [getattr(it, kind + name) for kind in ("g_", "held_", "last_", "out_", "in_")]
        r[name] = Reduce(dp, some[0], out, *some[1:])
    r["norms"] = Reduce(
        dp, it.g_norms, it.shared_norms.at[tensor.me], it.held_norms, it.last_norms, it.send_norms, it.recv_norms
    )
    r["mixed"] = Reduce(tensor, it.mixed, it.mixed_sum, it.held_mixed, it.last_mixed, it.send_mixed, it.recv_mixed)
    r["pack"] = Reduce(
        tensor, core.d_keyvalue, it.pack_sum, it.held_pack, it.last_pack, it.send_pack, it.recv_pack
    )
    scaled = Stream(
        tensor, it.mixed, it.scaled_sum, it.held_scaled, it.last_scaled,
        it.pair_send, it.pair_recv, it.line_send, it.line_recv,
    )

    def weight_grad(name, left, right):
        half = model // 2

        @pl.loop(0, 2)
        def _(index):
            at = pl.ds(pl.multiple_of(index * half, 128), half)
            r[name].part[at] = dot_rows(left[:used, at], right[:used]).astype(BF16)

    weight_grad("w_down", core.grad, core.hidden)
    r["w_down"].start()
    weight_grad("w_out", core.grad, core.attended)
    r["w_out"].start()
    g["w_out"].arrive()

    @pl.loop(0, tensor.size)
    def _(index):
        row = lax.rem(index, tensor.half)
        par = jnp.where(index < tensor.half, 1 - tensor.par, tensor.par)
        at = pl.ds(pl.multiple_of((2 * row + par) * slots, slots), slots)
        it.mixed[at] = core.mix(at).astype(BF16)

        @pl.when(index < tensor.half)
        def _():
            r["mixed"].first(row).start()

    @pl.loop(0, 4)
    def _(index):
        core.feed_back(pl.ds(pl.multiple_of(index * quarter, quarter), quarter))

    weight_grad("w_up", core.normed2, core.slope)
    r["w_up"].start()
    r["mixed"].middle()

    @pl.loop(0, used // BLOCK)
    def _(block):
        core.attend_grad(block)

    r["w_down"].middle()
    for ref in (core.d_keys, core.d_values, core.d_norms, it.scaled_sum):
        ref[...] = jnp.zeros_like(ref)
    chunks = used // BLOCK

    def turn(index):
        return jnp.where(lax.rem(index, 2) == 0, chunks // 2, chunks - 1) - index // 2

    @pl.loop(0, chunks)
    def _(index):
        block = turn(index)
        core.attend_back(block)

        @pl.when(index > 0)
        def _():
            scaled.take(turn(index - 1))

        part_of(it.mixed, block, BLOCK)[...] = core.input_grad(block).astype(BF16)
        scaled.give(block)

        @pl.when(index == 1)
        def _():
            r["w_out"].middle()

        @pl.when(index == 3)
        def _():
            r["w_up"].middle()

    core.keyvalue_grad()
    scaled.take(turn(chunks - 1))
    r["pack"].start()
    weight_grad("w_keyvalue", core.normed1, core.d_keyvalue)
    r["w_keyvalue"].start()
    part = model // dp.size
    sums = [jnp.sum(core.d_norms[i], axis=0, keepdims=True) for i in range(4)]
    for i, more in enumerate(core.keyvalue_norms()):
        sums[i] = sums[i] + more
    sums = jnp.concatenate(sums + [jnp.zeros((4, model), F32)])
    for i in range(dp.size):
        it.g_norms[i * 8 : (i + 1) * 8] = sums[:, i * part : (i + 1) * part]
    r["norms"].start()
    r["pack"].middle()
    weight_grad("w_query", core.normed1, core.d_query)
    r["w_query"].start()
    stores = []

    def store(*some):
        for name in some:
            index = OUTPUTS.index(name)
            stores.append(pltpu.make_async_copy(getattr(it, name), getattr(it, "o_" + name), it.store.at[index]))
            stores[-1].start()

    for name in ("w_keyvalue", "norms", "w_query"):
        r[name].middle()
    for name in ("w_keyvalue", "norms"):
        r[name].end()
    copies = []
    for i, ref in enumerate((it.shared_kv, it.shared_norms)):
        for step in range(1, tensor.size):
            peer = lax.rem(tensor.me + step, tensor.size)
            sems = [s.at[i * tensor.size + step] for s in (it.share_send, it.share_recv)]
            copies.append(remote(ref.at[tensor.me], ref.at[tensor.me], *sems, tensor, peer))
            copies[-1].start()
    r["mixed"].end()
    store("mixed_sum")
    r["w_down"].end()
    r["w_out"].end()
    r["w_up"].end()
    store("s_w_down", "s_w_out", "s_w_up")
    r["w_query"].end()
    store("s_w_query")

    @pl.loop(0, chunks)
    def _(index):
        scaled.end(turn(index))

    r["pack"].end()

    @pl.loop(0, slots // 128)
    def _(index):
        at = pl.ds(pl.multiple_of(index * 128, 128), 128)
        it.scaled_sum[at] += dot_cols(it.pack_sum[at].astype(BF16), core.w_keyvalue[...]) * core.params[0:1]

    store("scaled_sum")
    for copy in copies:
        copy.wait()
    store("shared_kv", "shared_norms")
    for name in WEIGHTS:
        g[name].leave()
    for copy in stores:
        copy.wait()


def finish_kernel(z, seq, tokens, cotangent, *refs):
    sums = Names(OUTPUTS, refs[: len(OUTPUTS)])
    out_tokens, d_tokens, d_query, d_keyvalue, d_out, d_up, d_down, *d_norms = refs[len(OUTPUTS) :]
    rows = tokens.shape[0]
    token = tokens[...].astype(F32)
    out_tokens[...] = (token + sums.mixed_sum[...]).astype(BF16)
    centered = token - jnp.mean(token, axis=1, keepdims=True)
    inv_std = lax.rsqrt(jnp.mean(centered * centered, axis=1, keepdims=True) + EPS)
    scaled = centered * inv_std
    grad = sums.scaled_sum[...]
    first_row = lax.axis_index("tensor") * z.slots + pl.program_id(0) * rows
    row = lax.broadcasted_iota(jnp.int32, (rows, 1), 0) + first_row
    own = jnp.where(row < seq[0, 0], cotangent[...].astype(F32), 0.0)
    inner = jnp.mean(grad * scaled, axis=1, keepdims=True)
    d_tokens[...] = own + inv_std * (grad - jnp.mean(grad, axis=1, keepdims=True) - scaled * inner)
    d_query[...] = sums.s_w_query[:, : z.heads * 64]
    d_out[...] = sums.s_w_out[:, : z.heads * 64]
    d_up[...] = sums.s_w_up[...]
    d_down[...] = sums.s_w_down[...]
    kv, norms = sums.shared_kv[0], sums.shared_norms[0]
    for t in range(1, z.nt):
        kv, norms = kv + sums.shared_kv[t], norms + sums.shared_norms[t]
    d_keyvalue[...] = kv
    for i in range(4):
        d_norms[i][...] = norms[i]


def plain_kernel(z, seq, *refs):
    named = dict(zip(INPUTS, refs))
    mixed, scaled_grad, g_query, g_keyvalue, g_out, g_up, g_down, g_norms = refs[len(INPUTS) : len(INPUTS) + 8]
    *own, grad, scaled = refs[len(INPUTS) + 8 :]
    named.update(zip(own_shapes(z), own), grad=grad, scaled=scaled)
    core = Core(z.heads, seq[0, 0], z.used, **named)
    rows, model, used = z.rows, z.model, z.used
    core.tables(0)
    core.tables(1)
    core.unpack_params()

    @pl.loop(0, rows // BLOCK)
    def _(block):
        core.normalize(block)
        core.project(block)

    for block in range(rows // BLOCK):
        core.attend(block)

    @pl.loop(0, rows // 512)
    def _(index):
        at = pl.ds(pl.multiple_of(index * 512, 512), 512)
        core.feed(at)
        mixed[at] = core.mix(at).astype(BF16)

    @pl.loop(0, 4)
    def _(index):
        first = pl.multiple_of(index * (used // 4), used // 4)
        core.mask(pl.ds(first, used // 4), first, used // 4)
        core.feed_back(pl.ds(first, used // 4))

    @pl.loop(0, model // BLOCK)
    def _(index):
        at = pl.ds(pl.multiple_of(index * BLOCK, BLOCK), BLOCK)
        grad = core.grad[:used, at]
        g_down[at] = dot_rows(grad, core.hidden[:used]).astype(BF16)
        g_out[at] = dot_rows(grad, core.attended[:used]).astype(BF16)
        g_up[at] = dot_rows(core.normed2[:used, at], core.slope[:used]).astype(BF16)

    @pl.loop(0, used // BLOCK)
    def _(block):
        core.attend_grad(block)

    for ref in (core.d_keys, core.d_values, core.d_norms):
        ref[...] = jnp.zeros_like(ref)
    @pl.loop(0, used // BLOCK)
    def _(index):
        block = used // BLOCK - 1 - index
        core.attend_back(block)
        part_of(scaled_grad, block, BLOCK)[...] = core.input_grad(block).astype(BF16)

    core.keyvalue_grad()

    @pl.loop(0, used // BLOCK)
    def _(block):
        at = pl.ds(pl.multiple_of(block * BLOCK, BLOCK), BLOCK)
        more = dot_cols(core.d_keyvalue[at], core.w_keyvalue[...]) * core.params[0:1]
        scaled_grad[at] = (scaled_grad[at].astype(F32) + more).astype(BF16)

    scaled_grad[used:] = jnp.zeros((rows - used, model), BF16)

    @pl.loop(0, model // BLOCK)
    def _(index):
        at = pl.ds(pl.multiple_of(index * BLOCK, BLOCK), BLOCK)
        normed = core.normed1[:used, at]
        g_query[at] = dot_rows(normed, core.d_query[:used]).astype(BF16)
        g_keyvalue[at] = dot_rows(normed, core.d_keyvalue[:used]).astype(BF16)

    for i in range(4):
        g_norms[i : i + 1] = jnp.sum(core.d_norms[i], axis=0, keepdims=True)
    for i, more in enumerate(core.keyvalue_norms()):
        g_norms[i : i + 1] += more


def run_plain(seq_lengths, norms, arrays, z):
    tokens, cotangent, w_query, w_keyvalue, w_up, w_down, w_out = arrays
    width, model = w_query.shape[1], tokens.shape[1]
    wide = z.wide
    pad = jnp.pad(w_query[:, width // 128 * 128 :], ((0, 0), (0, wide - width)))
    lane, start = lax.iota(jnp.int32, 128)[None], width % 128
    vectors = jnp.pad(jnp.stack(norms, axis=1), ((0, 0), (start, 124 - start)))
    tail = jnp.where(lane < start, pad, vectors)
    query = jnp.concatenate([w_query[:, : width // 128 * 128], tail], axis=1)
    out = jnp.pad(w_out, ((0, 0), (0, wide - width)))
    gathered = [lax.all_gather(a, "tensor", axis=0, tiled=True) for a in (tokens, cotangent)]
    gathered += [lax.all_gather(a, "dp", axis=0, tiled=True) for a in (query, w_keyvalue, w_up, w_down, out)]
    shape = jax.ShapeDtypeStruct
    results = pl.pallas_call(
        functools.partial(plain_kernel, z),
        out_shape=[shape((z.rows, model), BF16)] * 2
        + [shape((model, n), BF16) for n in (wide, 128, wide, z.units, z.units)]
        + [shape((4, model), F32)],
        in_specs=[pl.BlockSpec(memory_space=pltpu.SMEM)] + [INVMEM] * len(gathered),
        out_specs=[INVMEM] * 8,
        scratch_shapes=[pltpu.VMEM(*entry) for entry in own_shapes(z).values()] + [pltpu.VMEM((n, model), BF16) for n in (z.used, z.rows)],
        compiler_params=pltpu.CompilerParams(vmem_limit_bytes=67043328),
        name="plain_layer",
    )(seq_lengths, *gathered)
    names = ("tensor", "tensor") + ("dp",) * 5
    sums = [
        lax.psum_scatter(p.astype(F32), n, scatter_dimension=0, tiled=True) for p, n in zip(results[:7], names)
    ]
    norm_sums = lax.psum_scatter(results[7], "dp", scatter_dimension=1, tiled=True)
    shared_kv = lax.all_gather(sums[3], "tensor")
    shared_norms = lax.all_gather(jnp.pad(norm_sums, ((0, 4), (0, 0))), "tensor")
    return sums[0], sums[1], sums[2], sums[4], sums[5], sums[6], shared_kv, shared_norms


def run_whole(seq_lengths, norms, arrays, z):
    arrays_of, semaphores = fused_specs(z)
    scratch = [pltpu.VMEM(*entry) for entry in arrays_of.values()]
    scratch += [pltpu.SemaphoreType.DMA(shape) for shape in semaphores.values()]
    return pl.pallas_call(
        functools.partial(fused_kernel, z, tuple(arrays_of) + tuple(semaphores)),
        out_shape=[jax.ShapeDtypeStruct(shape, F32) for shape in output_shapes(z)],
        in_specs=[pl.BlockSpec(memory_space=pltpu.SMEM)]
        + [INVMEM] * 4
        + [INVMEM if packed else ANY for packed in (False, False, True, False, False, False, True)],
        out_specs=[ANY] * len(OUTPUTS),
        scratch_shapes=scratch,
        compiler_params=pltpu.CompilerParams(collective_id=0, has_side_effects=True, vmem_limit_bytes=67043328),
        name="layer",
    )(seq_lengths, *norms, *arrays)


def run_layer(seq_lengths, norms, arrays, nd, nt):
    tokens, _, w_query, w_keyvalue, w_up, _, _ = arrays
    heads, own, units = w_query.shape[1] // 64, w_query.shape[0], w_up.shape[1]
    slots, model = tokens.shape
    z = types.SimpleNamespace(
        nd=nd, nt=nt, heads=heads, rows=slots * nt, model=model, stack=heads * BLOCK, units=units, used=SEQ_MOST,
        wide=(heads * 64 + 4 + 127) // 128 * 128, own=own, slots=slots,
    )
    run = run_whole if own % 32 == 0 and slots == 2 * BLOCK and nt == 4 and SEQ_MOST == 7 * BLOCK else run_plain
    sums = run(seq_lengths, norms, arrays, z)
    steps = 2 if own % 16 == 0 else 1
    shape = jax.ShapeDtypeStruct

    def block(rows, columns):
        return pl.BlockSpec((rows // steps, columns), lambda i: (i, 0))

    width = heads * 64
    token_rows = block(slots, model)
    weights = [block(own, n) for n in (z.wide, z.wide, units, units)]
    shared = [
        pl.BlockSpec((nt, own // steps, 128), lambda i: (0, i, 0)),
        pl.BlockSpec((nt, 8, own), lambda i: (0, 0, 0)),
    ]
    results = pl.pallas_call(
        functools.partial(finish_kernel, z),
        grid=(steps,),
        out_shape=[shape((slots, model), BF16), shape((slots, model), F32)]
        + [shape((own, n), F32) for n in (width, 128, width, units, units)]
        + [shape((own,), F32)] * 4,
        in_specs=[pl.BlockSpec(memory_space=pltpu.SMEM)] + [token_rows] * 4 + weights + shared,
        out_specs=[token_rows] * 2
        + [block(own, n) for n in (width, 128, width, units, units)]
        + [pl.BlockSpec((own,), lambda i: (0,))] * 4,
        compiler_params=pltpu.CompilerParams(vmem_limit_bytes=67043328),
        name="finish",
    )(seq_lengths, *arrays[:2], *sums)
    return tuple(results)


def shards(
    tokens,
    cotangent,
    seq_lengths,
    w_query,
    w_keyvalue,
    w_out,
    w_up,
    w_down,
    norm1_gain,
    norm1_bias,
    norm2_gain,
    norm2_bias,
):
    norms = (norm1_gain, norm1_bias, norm2_gain, norm2_bias)
    arrays = (tokens, cotangent, w_query, w_keyvalue, w_up, w_down, w_out)
    return run_layer(seq_lengths, norms, arrays, lax.axis_size("dp"), lax.axis_size("tensor"))


def solution(mesh):
    return jax.shard_map(
        shards,
        mesh=mesh,
        in_specs=(
            P(("dp", "tensor"), None),
            P(("dp", "tensor"), None),
            P("dp", None),
            P("dp", "tensor"),
            P("dp", None),
            P("dp", "tensor"),
            P("dp", "tensor"),
            P("dp", "tensor"),
            P("dp"),
            P("dp"),
            P("dp"),
            P("dp"),
        ),
        out_specs=(
            P(("dp", "tensor"), None),
            P(("dp", "tensor"), None),
            P("dp", "tensor"),
            P("dp", None),
            P("dp", "tensor"),
            P("dp", "tensor"),
            P("dp", "tensor"),
            P("dp"),
            P("dp"),
            P("dp"),
            P("dp"),
        ),
        check_vma=False,
    )
```

```python
import functools
import math
import types

import jax
import jax.numpy as jnp
from jax import lax
from jax.experimental import pallas as pl
from jax.experimental.pallas import tpu as pltpu
from jax.sharding import PartitionSpec as P

ROT = 16
SEQ_LEAST = 1024
SEQ_MOST = 1792
BLOCK = 256
WIDE = 3
EPS = 1e-05
NEG = -1e30
F32 = jnp.float32
BF16 = jnp.bfloat16


def dot(left, right):
    return jnp.dot(left, right, preferred_element_type=F32)


def dot_rows(left, right):
    return lax.dot_general(left, right, (((0,), (0,)), ((), ())), preferred_element_type=F32)


def dot_cols(left, right):
    return lax.dot_general(left, right, (((1,), (1,)), ((), ())), preferred_element_type=F32)


def lanes_of(rows):
    return lax.broadcasted_iota(jnp.int32, (rows, 128), 1)


def swap_halves(x, lane):
    return jnp.where(lane < ROT // 2, pltpu.roll(x, 128 - ROT // 2, 1), pltpu.roll(x, ROT // 2, 1))


def three_parts(x):
    high = x.astype(BF16).astype(F32)
    middle = (x - high).astype(BF16).astype(F32)
    return high, middle, x - high - middle


def unit_heads(wide, heads):
    pieces = []
    for h in range(heads):
        piece = wide[:, h // 2 * 128 : h // 2 * 128 + 128]
        pieces.append(piece if h % 2 == 0 else pltpu.roll(piece, 64, 1))
    return pieces


def join_heads(pieces, lane):
    wide = []
    for h in range(0, len(pieces), 2):
        second = pltpu.roll(pieces[h + 1], 64, 1) if h + 1 < len(pieces) else jnp.zeros_like(pieces[h])
        wide.append(jnp.where(lane < 64, pieces[h], second))
    return jnp.concatenate(wide, axis=1)


class Core:
    def __init__(self, heads, length, used, **refs):
        self.heads, self.length, self.used = heads, length, used
        self.__dict__.update(refs)
        stack = heads * BLOCK
        self.d_query = self.attended
        self.d_stack = self.scores.at[0:stack, 0:128]
        self.d_keys = self.scores.at[stack : stack + used, 0:128]
        self.d_values = self.scores.at[stack : stack + used, 128:256]

    def past(self, first, shape, axis):
        return lax.broadcasted_iota(jnp.int32, shape, axis) + first >= self.length

    def tables(self, part):
        count = self.cosine.shape[0] // BLOCK // 2

        @pl.loop(part * count, part * count + count)
        def _(index):
            at = pl.ds(pl.multiple_of(index * BLOCK, BLOCK), BLOCK)
            lane = lanes_of(BLOCK)
            row = lax.broadcasted_iota(jnp.int32, (BLOCK, 128), 0) + index * BLOCK
            position = jnp.where(row >= self.length, row - self.length, row).astype(F32)
            exponent = jnp.where(lane < ROT // 2, lane, lane - ROT // 2).astype(F32) * (-2.0 / ROT)
            angle = position * jnp.exp(exponent * math.log(10000.0))
            sine = jnp.sin(angle)
            self.cosine[at] = jnp.where(lane < ROT, jnp.cos(angle), 1.0)
            self.sine[at] = jnp.where(lane < ROT // 2, -sine, jnp.where(lane < ROT, sine, 0.0))

    def unpack_params(self):
        start = self.heads * 64
        turned = self.w_query[:, start // 128 * 128 : start // 128 * 128 + 128].T.astype(F32)
        self.params[0:4] = turned[start % 128 : start % 128 + 4]

    def normalize(self, block):
        at = pl.ds(pl.multiple_of(block * BLOCK, BLOCK), BLOCK)
        x = self.tokens[at].astype(F32)
        centered = x - jnp.mean(x, axis=1, keepdims=True)
        scaled = centered * lax.rsqrt(jnp.mean(centered * centered, axis=1, keepdims=True) + EPS)
        gain1, bias1, gain2, bias2 = (self.params[i : i + 1] for i in range(4))
        self.scaled[at] = scaled.astype(BF16)
        self.normed1[at] = (scaled * gain1 + bias1).astype(BF16)
        self.normed2[at] = (scaled * gain2 + bias2).astype(BF16)

    def project(self, block):
        first = pl.multiple_of(block * BLOCK, BLOCK)
        at = pl.ds(first, BLOCK)
        lane = lanes_of(BLOCK)
        cosine, sine = self.cosine[at], self.sine[at]
        past = self.past(first, (BLOCK, 128), 0)
        normed = self.normed1[at]
        key_value = dot(normed, self.w_keyvalue[...])
        keys = key_value * cosine + swap_halves(key_value, lane) * sine
        hidden_key = jnp.where(past, 0.0, NEG)
        extra = jnp.where(lane == 64, hidden_key, jnp.where(lane < 68, -1.0, 0.0))
        self.keys[at] = jnp.where(lane < 64, keys, extra).astype(BF16)
        ones = jnp.where(lane < 67, 1.0, 0.0)
        self.values[at] = jnp.where(lane < 64, pltpu.roll(key_value, 64, 1), ones).astype(BF16)
        query = dot(normed, self.w_query[...])
        flag = jnp.where((lane == 64) & past, 1.0, 0.0)
        for h, piece in enumerate(unit_heads(query, self.heads)):
            turned = (piece * cosine + swap_halves(piece, lane) * sine).astype(BF16).astype(F32)
            turned = turned * (64 ** (-0.5))
            self.queries[block, h * BLOCK : (h + 1) * BLOCK] = jnp.where(lane < 64, turned, flag).astype(BF16)

    def key_blocks(self, block):
        first = SEQ_LEAST // BLOCK if block * BLOCK >= SEQ_MOST else 0
        return range(first, block + 1)

    def attend(self, block):
        rows = self.heads * BLOCK
        query = self.queries[block]
        lane = lanes_of(rows)
        top = jnp.full((rows, BLOCK), -3e38, F32)
        for index, j in enumerate(self.key_blocks(block)):
            scores = dot_cols(query, self.keys[j * BLOCK : (j + 1) * BLOCK])
            if j == block:
                row = lax.rem(lax.broadcasted_iota(jnp.int32, (rows, BLOCK), 0), BLOCK)
                column = lax.broadcasted_iota(jnp.int32, (rows, BLOCK), 1)
                scores = jnp.where(column <= row, scores, NEG)
            self.scores[index * rows : (index + 1) * rows] = scores
            top = jnp.maximum(top, scores)
        top = jnp.max(top, axis=1, keepdims=True)
        total = jnp.zeros((rows, 128), F32)
        for index, j in enumerate(self.key_blocks(block)):
            probs = jnp.exp(self.scores[index * rows : (index + 1) * rows] - top).astype(BF16)
            total = total + dot(probs, self.values[j * BLOCK : (j + 1) * BLOCK])
        weight = jnp.sum(jnp.where(lane == 64, total, 0.0), axis=1, keepdims=True)
        output = total / weight
        pieces = [output[h * BLOCK : (h + 1) * BLOCK] for h in range(self.heads)]
        self.attended[block * BLOCK : (block + 1) * BLOCK] = join_heads(pieces, lanes_of(BLOCK)).astype(BF16)
        high, middle, low = three_parts(top + jnp.log(weight))
        parts = jnp.where(lane == 65, high, jnp.where(lane == 66, middle, low))
        self.queries[block] = jnp.where((lane >= 65) & (lane < 68), parts, query.astype(F32)).astype(BF16)

    def feed(self, at):
        up = dot(self.normed2[at], self.w_up[...])
        normal = 0.5 * (1.0 + lax.erf(up * (1.0 / math.sqrt(2.0))))
        self.hidden[at] = (up * normal).astype(BF16)
        density = jnp.exp(-0.5 * up * up) * (1.0 / math.sqrt(2.0 * math.pi))
        self.slope[at] = (normal + up * density).astype(BF16)

    def mix(self, at):
        return dot_cols(self.attended[at], self.w_out[...]) + dot_cols(self.hidden[at], self.w_down[...])

    def mask(self, at, first, rows):
        past = self.past(first, (rows, 1), 0)
        self.grad[at] = jnp.where(past, 0.0, self.cotangent[at].astype(F32)).astype(BF16)

    def feed_back(self, at):
        d_hidden = dot(self.grad[at], self.w_down[...])
        self.slope[at] = (d_hidden * self.slope[at].astype(F32)).astype(BF16)

    def d_attended(self, block, first, size):
        across = self.hidden.shape[1] // 128
        row = block // across * (self.heads * BLOCK) + first
        lane = lax.rem(block, across) * 128
        return self.hidden.at[pl.ds(pl.multiple_of(row, BLOCK), size), pl.ds(pl.multiple_of(lane, 128), 128)]

    def attend_grad(self, block):
        first = pl.multiple_of(block * BLOCK, BLOCK)
        at = pl.ds(first, BLOCK)
        lane = lanes_of(BLOCK)
        grads = unit_heads(dot(self.grad[at], self.w_out[...]), self.heads)
        outputs = unit_heads(self.attended[at].astype(F32), self.heads)
        for h in range(self.heads):
            grad = grads[h].astype(BF16).astype(F32)
            delta = jnp.sum(jnp.where(lane < 64, grad * outputs[h], 0.0), axis=1, keepdims=True)
            high, middle, low = three_parts(-delta)
            parts = jnp.where(lane == 64, high, jnp.where(lane == 65, middle, jnp.where(lane == 66, low, 0.0)))
            self.d_attended(block, h * BLOCK, BLOCK)[...] = jnp.where(lane < 64, grad, parts).astype(BF16)

    def attend_back(self, block):
        rows = self.heads * BLOCK
        query, grad = self.queries[block], self.d_attended(block, 0, rows)[...]

        def span(first, size, diagonal):
            at = pl.ds(pl.multiple_of(first, BLOCK), size)
            keys, values = self.keys[at], self.values[at]
            scores, d_probs = dot_cols(keys, query), dot_cols(values, grad)
            if diagonal:
                key = lax.broadcasted_iota(jnp.int32, (size, rows), 0)
                row = lax.rem(lax.broadcasted_iota(jnp.int32, (size, rows), 1), BLOCK) + (size - BLOCK)
                scores = jnp.where(key <= row, scores, NEG)
            probs = jnp.exp(scores)
            d_scores = (probs * d_probs).astype(BF16)
            self.d_values[at] += dot(probs.astype(BF16), grad)
            self.d_keys[at] += dot(d_scores, query)
            d_query = dot_rows(d_scores, keys)
            if diagonal:
                self.d_stack[...] = d_query
            else:
                self.d_stack[...] += d_query

        last = lax.rem(block, WIDE)
        for size in range(WIDE):

            @pl.when(last == size)
            def _():
                span((block - size) * BLOCK, (size + 1) * BLOCK, True)

        @pl.loop(0, block // WIDE)
        def _(index):
            span(index * WIDE * BLOCK, WIDE * BLOCK, False)

        at = pl.ds(pl.multiple_of(block * BLOCK, BLOCK), BLOCK)
        pieces = [
            self.turn_back(self.d_stack[h * BLOCK : (h + 1) * BLOCK], at) * (64 ** (-0.5)) for h in range(self.heads)
        ]
        self.d_query[at] = join_heads(pieces, lanes_of(BLOCK)).astype(BF16)

    def turn_back(self, x, at):
        return x * self.cosine[at] - swap_halves(x, lanes_of(BLOCK)) * self.sine[at]

    def keyvalue_grad(self):
        rows = self.d_keyvalue.shape[0]

        @pl.loop(0, self.used // BLOCK)
        def _(block):
            at = pl.ds(pl.multiple_of(block * BLOCK, BLOCK), BLOCK)
            d_keys = self.turn_back(self.d_keys[at], at)
            d_values = pltpu.roll(self.d_values[at], 64, 1)
            self.d_keyvalue[at] = jnp.where(lanes_of(BLOCK) < 64, d_keys, d_values).astype(BF16)

        self.d_keyvalue[self.used :] = jnp.zeros((rows - self.used, 128), BF16)

    def keyvalue_norms(self):
        weight = self.w_keyvalue[...].astype(F32)
        grad = self.d_keyvalue[: self.used]
        gain = jnp.sum(dot_rows(self.scaled[: self.used], grad) * weight, axis=1, keepdims=True)
        bias = jnp.sum(jnp.sum(grad.astype(F32), axis=0, keepdims=True) * weight, axis=1, keepdims=True)
        lane = lanes_of(weight.shape[0])
        turned = jnp.where(lane == 0, gain, bias).T
        return turned[0:1], turned[1:2]

    def input_grad(self, block):
        at = pl.ds(pl.multiple_of(block * BLOCK, BLOCK), BLOCK)
        d_normed1 = dot_cols(self.d_query[at], self.w_query[...])
        d_normed2 = dot_cols(self.slope[at], self.w_up[...])
        scaled = self.scaled[at].astype(F32)
        for i, value in enumerate((d_normed1 * scaled, d_normed1, d_normed2 * scaled, d_normed2)):
            self.d_norms[i] += jnp.sum(value.reshape(BLOCK // 8, 8, -1), axis=0)
        return d_normed1 * self.params[0:1] + d_normed2 * self.params[2:3]


MESH = pl.DeviceIdType.MESH
INVMEM = pl.BlockSpec(memory_space=pltpu.VMEM)
ANY = pl.BlockSpec(memory_space=pl.ANY)


class Axis:
    def __init__(self, name, size):
        self.name, self.size, self.half = name, size, size // 2
        self.me = lax.axis_index(name)
        self.row, self.par = self.me // 2, self.me % 2
        self.pair = self.me + 1 - 2 * self.par

    def other_row(self, step):
        return lax.rem(self.row + step + self.half, self.half)

    def line(self, step):
        return self.other_row(step) * 2 + self.par

    def greet(self, barrier, peers):
        for peer in peers:
            pl.semaphore_signal(barrier, inc=1, device_id={self.name: peer}, device_id_type=MESH)
        return len(peers)


def remote(src, dst, send, recv, axis, peer):
    return pltpu.make_async_remote_copy(
        src_ref=src, dst_ref=dst, send_sem=send, recv_sem=recv, device_id={axis.name: peer}, device_id_type=MESH
    )


def part_of(ref, index, rows):
    return ref.at[pl.ds(pl.multiple_of(index * rows, rows), rows)]


class Gather:
    def __init__(self, axis, src, dst, send, recv, local, part=0, parts=1):
        self.axis, self.dst, self.send, self.recv = axis, dst, send, recv
        self.half, self.part, self.parts = axis.half, part, parts
        self.src = part_of(src, part, src.shape[0] // parts)
        self.copy = pltpu.make_async_copy(self.src, self.slot(axis.me), local)

    def slot(self, index):
        return part_of(self.dst, index * self.parts + self.part, self.src.shape[0])

    def along(self, row, way, own=False):
        slot = self.slot(2 * row + self.axis.par)
        send = self.send.at[row if way > 0 else self.half + row]
        peer = self.axis.me + 2 * way
        return remote(self.src if own else slot, slot, send, self.recv.at[row], self.axis, peer)

    def across(self, row, own=False):
        slot = self.slot(2 * row + self.axis.par)
        sems = self.send.at[2 * self.half + row], self.recv.at[self.half + row]
        return remote(self.src if own else slot, slot, *sems, self.axis, self.axis.pair)

    def start_line(self):
        @pl.when(self.axis.row + 1 < self.half)
        def _():
            self.along(self.axis.row, 1, own=True).start()

        @pl.when(self.axis.row > 0)
        def _():
            self.along(self.axis.row, -1, own=True).start()

    def start_pair(self):
        self.across(self.axis.row, own=True).start()

    def pass_on(self, distance):
        if distance >= self.half:
            return
        me = self.axis.row

        @pl.when(me >= distance)
        def _():
            row = me - distance
            self.along(row, 1).wait_recv()

            @pl.when(me + 1 < self.half)
            def _():
                self.along(row, 1).start()

            self.across(row).start()

        @pl.when(me + distance < self.half)
        def _():
            row = me + distance
            self.along(row, -1).wait_recv()

            @pl.when(me > 0)
            def _():
                self.along(row, -1).start()

            self.across(row).start()

    def pair_arrived(self, row):
        slot = self.slot(2 * row + 1 - self.axis.par)
        sems = self.send.at[2 * self.half + row], self.recv.at[self.half + row]
        remote(slot, slot, *sems, self.axis, self.axis.pair).wait_recv()

    def arrive(self):
        self.copy.wait()
        for row in range(self.half):
            self.pair_arrived(row)

    def leave(self):
        for row in range(self.half):
            self.across(row).wait_send()

            @pl.when((self.axis.row >= row) & (self.axis.row + 1 < self.half))
            def _():
                self.along(row, 1).wait_send()

            @pl.when((self.axis.row <= row) & (self.axis.row > 0))
            def _():
                self.along(row, -1).wait_send()


class Reduce:
    def __init__(self, axis, part, out, held, last, send, recv):
        self.axis, self.part, self.out, self.held, self.last = axis, part, out, held, last
        self.send, self.recv, self.rows = send, recv, out.shape[0]
        self.chunk = 64 if self.rows % 64 == 0 else self.rows

    def first(self, row):
        block = part_of(self.part, 2 * row + 1 - self.axis.par, self.rows)
        held = part_of(self.held, row, self.rows)
        return remote(block, held, self.send.at[row], self.recv.at[row], self.axis, self.axis.pair)

    def second(self, step):
        index = self.axis.half + step
        block = part_of(self.held, self.axis.other_row(step), self.rows)
        last = part_of(self.last, step - 1, self.rows)
        return remote(block, last, self.send.at[index], self.recv.at[index], self.axis, self.axis.line(step))

    def start(self):
        for step in range(self.axis.half):
            self.first(self.axis.other_row(step + 1)).start()

    def chunks(self, body):
        @pl.loop(0, self.rows // self.chunk)
        def _(index):
            body(pl.multiple_of(index * self.chunk, self.chunk))

    def total(self, row, at):
        part = self.part[pl.ds((2 * row + self.axis.par) * self.rows + at, self.chunk)].astype(F32)
        return part + self.held[pl.ds(row * self.rows + at, self.chunk)].astype(F32)

    def middle(self):
        for step in range(1, self.axis.half):
            row = self.axis.other_row(step)
            self.first(row).wait()

            def add(at, row=row):
                self.held[pl.ds(row * self.rows + at, self.chunk)] = self.total(row, at).astype(self.held.dtype)

            self.chunks(add)
            self.second(step).start()

        self.first(self.axis.row).wait()

        def keep(at):
            self.out[pl.ds(at, self.chunk)] = self.total(self.axis.row, at)

        self.chunks(keep)

    def end(self):
        for step in range(1, self.axis.half):
            self.second(step).wait()

        def add(at):
            total = self.out[pl.ds(at, self.chunk)]
            for step in range(1, self.axis.half):
                total = total + self.last[pl.ds((step - 1) * self.rows + at, self.chunk)].astype(F32)
            self.out[pl.ds(at, self.chunk)] = total

        self.chunks(add)


class Stream:
    def __init__(self, axis, part, out, held, last, pair_send, pair_recv, line_send, line_recv):
        self.axis, self.part, self.out, self.held, self.last = axis, part, out, held, last
        self.pair_sems, self.line_sems = (pair_send, pair_recv), (line_send, line_recv)

    def split(self, chunk):
        return chunk // 4, chunk // 2 % 2, chunk % 2

    def pair_copy(self, chunk):
        row, _, half = self.split(chunk)
        index = 2 * row + half
        send, recv = (sems.at[index] for sems in self.pair_sems)
        held = part_of(self.held, index, BLOCK)
        return remote(part_of(self.part, chunk, BLOCK), held, send, recv, self.axis, self.axis.pair)

    def line_copy(self, chunk):
        row, _, half = self.split(chunk)
        send, recv = (sems.at[half] for sems in self.line_sems)
        held = part_of(self.held, 2 * row + half, BLOCK)
        return remote(held, part_of(self.last, half, BLOCK), send, recv, self.axis, self.axis.line(1))

    def give(self, chunk):
        @pl.when(self.axis.par != self.split(chunk)[1])
        def _():
            self.pair_copy(chunk).start()

    def take(self, chunk):
        row, par, half = self.split(chunk)

        @pl.when(self.axis.par == par)
        def _():
            self.pair_copy(chunk).wait_recv()

            def total(at):
                part = self.part[pl.ds(chunk * BLOCK + at, 64)].astype(F32)
                return part + self.held[pl.ds((2 * row + half) * BLOCK + at, 64)].astype(F32)

            @pl.when(self.axis.row == row)
            def _():
                @pl.loop(0, BLOCK // 64)
                def _(index):
                    at = pl.multiple_of(index * 64, 64)
                    self.out[pl.ds(half * BLOCK + at, 64)] = total(at)

            @pl.when(self.axis.row != row)
            def _():
                @pl.loop(0, BLOCK // 64)
                def _(index):
                    at = pl.multiple_of(index * 64, 64)
                    self.held[pl.ds((2 * row + half) * BLOCK + at, 64)] = total(at).astype(BF16)

                self.line_copy(chunk).start()

    def end(self, chunk):
        row, par, half = self.split(chunk)

        @pl.when(self.axis.par != par)
        def _():
            self.pair_copy(chunk).wait_send()

        @pl.when((self.axis.par == par) & (self.axis.row != row))
        def _():
            self.line_copy(chunk).wait_send()

        @pl.when((self.axis.par == par) & (self.axis.row == row))
        def _():
            self.line_copy(chunk).wait_recv()

            @pl.loop(0, BLOCK // 64)
            def _(index):
                at = pl.multiple_of(index * 64, 64)
                rows = pl.ds(half * BLOCK + at, 64)
                self.out[rows] += self.last[rows].astype(F32)

WEIGHTS = ("w_query", "w_keyvalue", "w_up", "w_down", "w_out")
INPUTS = ("tokens", "cotangent") + WEIGHTS
OUTPUTS = ("mixed_sum", "scaled_sum", "s_w_query", "s_w_out", "s_w_up", "s_w_down", "shared_kv", "shared_norms")


def own_shapes(z):
    wide_rows = (z.rows, z.model)
    return dict(
        params=((8, z.model), F32), cosine=((z.rows, 128), F32), sine=((z.rows, 128), F32),
        normed1=(wide_rows, BF16), normed2=(wide_rows, BF16),
        queries=((z.rows // BLOCK, z.stack, 128), BF16), keys=((z.rows, 128), BF16), values=((z.rows, 128), BF16),
        scores=((z.used // BLOCK * z.stack, BLOCK), F32), attended=((z.rows, z.wide), BF16), hidden=((z.rows, z.units), BF16),
        slope=((z.rows, z.units), BF16), d_keyvalue=((z.rows, 128), BF16), d_norms=((4, 8, z.model), F32),
    )


class Names:
    def __init__(self, names, refs):
        self.__dict__.update(zip(names, refs, strict=True))


def output_shapes(z):
    return [
        (z.slots, z.model), (z.slots, z.model), (z.own, z.wide), (z.own, z.wide), (z.own, z.units), (z.own, z.units),
        (z.nt, z.own, 128), (z.nt, 8, z.own),
    ]


def fused_specs(z):
    half, model = z.nd // 2, z.model
    columns = dict(zip(WEIGHTS, (z.wide, 128, z.units, z.units, z.wide)))
    arrays = own_shapes(z)
    arrays.update({name: (shape, F32) for name, shape in zip(OUTPUTS, output_shapes(z))})
    arrays.update(pack_query=((z.own, z.wide), BF16), pack_out=((z.own, z.wide), BF16))
    arrays.update(tokens=((z.rows, model), BF16), cotangent=((z.rows, model), BF16))
    arrays.update({name: ((model, columns[name]), BF16) for name in WEIGHTS})
    arrays.update(mixed=((z.rows, model), BF16), held_mixed=((z.rows // 2, model), BF16))
    arrays.update(last_mixed=((z.slots, model), BF16), held_scaled=((z.rows // 2, model), BF16))
    arrays.update(last_scaled=((z.slots, model), BF16))
    for name in WEIGHTS:
        arrays["g_" + name] = ((model, columns[name]), BF16)
        arrays["held_" + name] = ((half * z.own, columns[name]), BF16)
        arrays["last_" + name] = ((max(half - 1, 1) * z.own, columns[name]), BF16)
    arrays.update(held_pack=((z.rows // 2, 128), BF16), last_pack=((z.slots, 128), BF16), pack_sum=((z.slots, 128), F32))
    arrays.update(g_norms=((z.nd * 8, z.own), F32), held_norms=((half * 8, z.own), F32))
    arrays.update(last_norms=((max(half - 1, 1) * 8, z.own), F32))
    semaphores = dict(send_mixed=(z.nt,), recv_mixed=(z.nt,), send_pack=(z.nt,), recv_pack=(z.nt,), send_norms=(z.nd,), recv_norms=(z.nd,))
    for name in INPUTS:
        count = z.nd if name in WEIGHTS else z.nt
        shape = (2, count) if name == "tokens" else (count,)
        semaphores.update({"send_" + name: shape[:-1] + (count // 2 * 3,), "recv_" + name: shape})
    for name in WEIGHTS:
        semaphores.update({"out_" + name: (z.nd,), "in_" + name: (z.nd,)})
    semaphores.update(pair_send=(4,), pair_recv=(4,), line_send=(2,), line_recv=(2,), local=(len(INPUTS) + 1,))
    semaphores.update(share_send=(2 * z.nt,), share_recv=(2 * z.nt,), store=(len(OUTPUTS),))
    return arrays, semaphores


def fused_kernel(z, names, *refs):
    vectors, refs = refs[1:5], refs[:1] + refs[5:]
    it = Names(("seq",) + tuple("i_" + n for n in INPUTS) + tuple("o_" + n for n in OUTPUTS) + names, refs)
    dp, tensor = Axis("dp", z.nd), Axis("tensor", z.nt)
    rows, model, used, slots = z.rows, z.model, z.used, z.slots
    core = Core(z.heads, it.seq[0, 0], z.used, **{n: getattr(it, n) for n in tuple(own_shapes(z)) + INPUTS}, grad=it.cotangent, scaled=it.tokens)
    barrier = pltpu.get_barrier_semaphore()
    expected = dp.greet(barrier, [dp.pair] + [dp.line(step) for step in range(1, dp.half)])
    expected += tensor.greet(barrier, [lax.rem(tensor.me + step, tensor.size) for step in range(1, tensor.size)])

    width = z.heads * 64
    pad = jnp.zeros((z.own, z.wide - width), BF16)
    lane = lanes_of(z.own)
    first = width // 128 * 128
    tail = jnp.concatenate([it.i_w_query[:, first:].astype(F32), pad.astype(F32)], axis=1)
    it.pack_query[:, :first] = it.i_w_query[:, :first]
    start = width - first
    turned = [v[...].astype(F32).reshape(1, z.own) for v in vectors]
    turned = jnp.concatenate([jnp.zeros((start, z.own), F32)] + turned + [jnp.zeros((124 - start, z.own), F32)])
    turned = jnp.concatenate([turned, jnp.zeros((128, 128 - z.own), F32)], axis=1).T[: z.own]
    it.pack_query[:, first:] = jnp.where(lane < start, tail, turned).astype(BF16)
    it.pack_out[:, :first] = it.i_w_out[:, :first]
    it.pack_out[:, first:] = jnp.concatenate([it.i_w_out[:, first:], pad], axis=1)
    sources = dict(w_query=it.pack_query, w_out=it.pack_out)
    g = {}
    for i, name in enumerate(INPUTS):
        axis = dp if name in WEIGHTS else tensor
        source = sources.get(name, getattr(it, "i_" + name))
        send, recv = getattr(it, "send_" + name), getattr(it, "recv_" + name)
        g[name] = Gather(axis, source, getattr(it, name), send, recv, it.local.at[i])
    tokens = [
        Gather(tensor, it.i_tokens, it.tokens, it.send_tokens.at[h], it.recv_tokens.at[h], it.local.at[len(INPUTS) * h], h, 2)
        for h in range(2)
    ]
    pl.semaphore_wait(barrier, expected)

    def hand_on(names, distance):
        for name in names:
            g[name].pass_on(distance)

    small = ("w_query", "w_keyvalue")
    for gather in tokens + [g["cotangent"]]:
        gather.start_line()
        gather.start_pair()
    for name in small:
        g[name].start_line()
        g[name].start_pair()
    g["w_up"].start_pair()
    for gather in tokens + [g[name] for name in INPUTS[1:]]:
        gather.copy.start()
    core.tables(0)
    hand_on(small, 1)
    g["w_up"].start_line()
    core.tables(1)
    hand_on(small, 2)
    hand_on(small, 3)
    hand_on(("w_up",), 1)
    g["w_down"].start_line()
    for name in small:
        g[name].arrive()
    core.unpack_params()

    for gather in tokens:
        gather.copy.wait()
    other, other_pair = tensor.line(1), tensor.line(1) + tensor.pair - tensor.me

    @pl.loop(0, 4)
    def _(index):
        @pl.when(index == 1)
        def _():
            for gather in tokens:
                gather.pair_arrived(tensor.row)
            hand_on(("w_up",), 2)
            g["w_down"].start_pair()
            g["w_out"].start_line()

        for half in range(2):

            @pl.when(index == 2 + half)
            def _():
                tokens[half].pass_on(1)
                if half == 0:
                    hand_on(("w_up",), 3)
                tokens[half].pair_arrived(1 - tensor.row)
                tokens[half].leave()

        late = index // 2
        first = jnp.where(index == 0, 2 * tensor.me, 2 * tensor.pair)
        blocks = [
            (1 - late) * first + late * (2 * other + index - 2),
            (1 - late) * (first + 1) + late * (2 * other_pair + index - 2),
        ]
        for block in blocks:
            core.normalize(block)
            core.project(block)

        @pl.when(index == 2)
        def _():
            hand_on(("w_down",), 1)
            g["w_out"].start_pair()

    hand_on(("w_down",), 2)
    g["w_up"].arrive()

    @pl.loop(0, rows // slots)
    def _(index):
        core.feed(pl.ds(pl.multiple_of(index * slots, slots), slots))
        for step, (name, distance) in enumerate((("w_down", 3), ("w_out", 1), ("w_out", 2), ("w_out", 3))):

            @pl.when(index == step)
            def _():
                hand_on((name,), distance)

    for block in range(rows // BLOCK):
        core.attend(block)
    g["cotangent"].pass_on(1)
    g["w_down"].arrive()
    g["cotangent"].arrive()
    g["cotangent"].leave()

    quarter = used // 4

    @pl.loop(0, 4)
    def _(index):
        first = pl.multiple_of(index * quarter, quarter)
        core.mask(pl.ds(first, quarter), first, quarter)

    r = {}
    for name in WEIGHTS:
        out = getattr(it, "s_" + name) if name != "w_keyvalue" else it.shared_kv.at[tensor.me]
        some = [getattr(it, kind + name) for kind in ("g_", "held_", "last_", "out_", "in_")]
        r[name] = Reduce(dp, some[0], out, *some[1:])
    r["norms"] = Reduce(
        dp, it.g_norms, it.shared_norms.at[tensor.me], it.held_norms, it.last_norms, it.send_norms, it.recv_norms
    )
    r["mixed"] = Reduce(tensor, it.mixed, it.mixed_sum, it.held_mixed, it.last_mixed, it.send_mixed, it.recv_mixed)
    r["pack"] = Reduce(
        tensor, core.d_keyvalue, it.pack_sum, it.held_pack, it.last_pack, it.send_pack, it.recv_pack
    )
    scaled = Stream(
        tensor, it.mixed, it.scaled_sum, it.held_scaled, it.last_scaled,
        it.pair_send, it.pair_recv, it.line_send, it.line_recv,
    )

    def weight_grad(name, left, right):
        half = model // 2

        @pl.loop(0, 2)
        def _(index):
            at = pl.ds(pl.multiple_of(index * half, 128), half)
            r[name].part[at] = dot_rows(left[:used, at], right[:used]).astype(BF16)

    weight_grad("w_down", core.grad, core.hidden)
    r["w_down"].start()
    weight_grad("w_out", core.grad, core.attended)
    r["w_out"].start()
    g["w_out"].arrive()

    @pl.loop(0, tensor.size)
    def _(index):
        row = lax.rem(index, tensor.half)
        par = jnp.where(index < tensor.half, 1 - tensor.par, tensor.par)
        at = pl.ds(pl.multiple_of((2 * row + par) * slots, slots), slots)
        it.mixed[at] = core.mix(at).astype(BF16)

        @pl.when(index < tensor.half)
        def _():
            r["mixed"].first(row).start()

    @pl.loop(0, 4)
    def _(index):
        core.feed_back(pl.ds(pl.multiple_of(index * quarter, quarter), quarter))

    weight_grad("w_up", core.normed2, core.slope)
    r["w_up"].start()
    r["mixed"].middle()

    @pl.loop(0, used // BLOCK)
    def _(block):
        core.attend_grad(block)

    r["w_down"].middle()
    for ref in (core.d_keys, core.d_values, core.d_norms, it.scaled_sum):
        ref[...] = jnp.zeros_like(ref)
    chunks = used // BLOCK

    def turn(index):
        return jnp.where(lax.rem(index, 2) == 0, chunks // 2, chunks - 1) - index // 2

    @pl.loop(0, chunks)
    def _(index):
        block = turn(index)
        core.attend_back(block)

        @pl.when(index > 0)
        def _():
            scaled.take(turn(index - 1))

        part_of(it.mixed, block, BLOCK)[...] = core.input_grad(block).astype(BF16)
        scaled.give(block)

        @pl.when(index == 1)
        def _():
            r["w_out"].middle()

        @pl.when(index == 3)
        def _():
            r["w_up"].middle()

    core.keyvalue_grad()
    scaled.take(turn(chunks - 1))
    r["pack"].start()
    weight_grad("w_keyvalue", core.normed1, core.d_keyvalue)
    r["w_keyvalue"].start()
    part = model // dp.size
    sums = [jnp.sum(core.d_norms[i], axis=0, keepdims=True) for i in range(4)]
    for i, more in enumerate(core.keyvalue_norms()):
        sums[i] = sums[i] + more
    sums = jnp.concatenate(sums + [jnp.zeros((4, model), F32)])
    for i in range(dp.size):
        it.g_norms[i * 8 : (i + 1) * 8] = sums[:, i * part : (i + 1) * part]
    r["norms"].start()
    r["pack"].middle()
    weight_grad("w_query", core.normed1, core.d_query)
    r["w_query"].start()
    stores = []

    def store(*some):
        for name in some:
            index = OUTPUTS.index(name)
            stores.append(pltpu.make_async_copy(getattr(it, name), getattr(it, "o_" + name), it.store.at[index]))
            stores[-1].start()

    for name in ("w_keyvalue", "norms", "w_query"):
        r[name].middle()
    for name in ("w_keyvalue", "norms"):
        r[name].end()
    copies = []
    for i, ref in enumerate((it.shared_kv, it.shared_norms)):
        for step in range(1, tensor.size):
            peer = lax.rem(tensor.me + step, tensor.size)
            sems = [s.at[i * tensor.size + step] for s in (it.share_send, it.share_recv)]
            copies.append(remote(ref.at[tensor.me], ref.at[tensor.me], *sems, tensor, peer))
            copies[-1].start()
    r["mixed"].end()
    store("mixed_sum")
    r["w_down"].end()
    r["w_out"].end()
    r["w_up"].end()
    store("s_w_down", "s_w_out", "s_w_up")
    r["w_query"].end()
    store("s_w_query")

    @pl.loop(0, chunks)
    def _(index):
        scaled.end(turn(index))

    r["pack"].end()

    @pl.loop(0, slots // 128)
    def _(index):
        at = pl.ds(pl.multiple_of(index * 128, 128), 128)
        it.scaled_sum[at] += dot_cols(it.pack_sum[at].astype(BF16), core.w_keyvalue[...]) * core.params[0:1]

    store("scaled_sum")
    for copy in copies:
        copy.wait()
    store("shared_kv", "shared_norms")
    for name in WEIGHTS:
        g[name].leave()
    for copy in stores:
        copy.wait()


def finish_kernel(z, seq, tokens, cotangent, *refs):
    sums = Names(OUTPUTS, refs[: len(OUTPUTS)])
    out_tokens, d_tokens, d_query, d_keyvalue, d_out, d_up, d_down, *d_norms = refs[len(OUTPUTS) :]
    rows = tokens.shape[0]
    token = tokens[...].astype(F32)
    out_tokens[...] = (token + sums.mixed_sum[...]).astype(BF16)
    centered = token - jnp.mean(token, axis=1, keepdims=True)
    inv_std = lax.rsqrt(jnp.mean(centered * centered, axis=1, keepdims=True) + EPS)
    scaled = centered * inv_std
    grad = sums.scaled_sum[...]
    first_row = lax.axis_index("tensor") * z.slots + pl.program_id(0) * rows
    row = lax.broadcasted_iota(jnp.int32, (rows, 1), 0) + first_row
    own = jnp.where(row < seq[0, 0], cotangent[...].astype(F32), 0.0)
    inner = jnp.mean(grad * scaled, axis=1, keepdims=True)
    d_tokens[...] = own + inv_std * (grad - jnp.mean(grad, axis=1, keepdims=True) - scaled * inner)
    d_query[...] = sums.s_w_query[:, : z.heads * 64]
    d_out[...] = sums.s_w_out[:, : z.heads * 64]
    d_up[...] = sums.s_w_up[...]
    d_down[...] = sums.s_w_down[...]
    kv, norms = sums.shared_kv[0], sums.shared_norms[0]
    for t in range(1, z.nt):
        kv, norms = kv + sums.shared_kv[t], norms + sums.shared_norms[t]
    d_keyvalue[...] = kv
    for i in range(4):
        d_norms[i][...] = norms[i]


def plain_kernel(z, seq, *refs):
    named = dict(zip(INPUTS, refs))
    mixed, scaled_grad, g_query, g_keyvalue, g_out, g_up, g_down, g_norms = refs[len(INPUTS) : len(INPUTS) + 8]
    *own, grad, scaled = refs[len(INPUTS) + 8 :]
    named.update(zip(own_shapes(z), own), grad=grad, scaled=scaled)
    core = Core(z.heads, seq[0, 0], z.used, **named)
    rows, model, used = z.rows, z.model, z.used
    core.tables(0)
    core.tables(1)
    core.unpack_params()

    @pl.loop(0, rows // BLOCK)
    def _(block):
        core.normalize(block)
        core.project(block)

    for block in range(rows // BLOCK):
        core.attend(block)

    @pl.loop(0, rows // 512)
    def _(index):
        at = pl.ds(pl.multiple_of(index * 512, 512), 512)
        core.feed(at)
        mixed[at] = core.mix(at).astype(BF16)

    @pl.loop(0, 4)
    def _(index):
        first = pl.multiple_of(index * (used // 4), used // 4)
        core.mask(pl.ds(first, used // 4), first, used // 4)
        core.feed_back(pl.ds(first, used // 4))

    @pl.loop(0, model // BLOCK)
    def _(index):
        at = pl.ds(pl.multiple_of(index * BLOCK, BLOCK), BLOCK)
        grad = core.grad[:used, at]
        g_down[at] = dot_rows(grad, core.hidden[:used]).astype(BF16)
        g_out[at] = dot_rows(grad, core.attended[:used]).astype(BF16)
        g_up[at] = dot_rows(core.normed2[:used, at], core.slope[:used]).astype(BF16)

    @pl.loop(0, used // BLOCK)
    def _(block):
        core.attend_grad(block)

    for ref in (core.d_keys, core.d_values, core.d_norms):
        ref[...] = jnp.zeros_like(ref)
    @pl.loop(0, used // BLOCK)
    def _(index):
        block = used // BLOCK - 1 - index
        core.attend_back(block)
        part_of(scaled_grad, block, BLOCK)[...] = core.input_grad(block).astype(BF16)

    core.keyvalue_grad()

    @pl.loop(0, used // BLOCK)
    def _(block):
        at = pl.ds(pl.multiple_of(block * BLOCK, BLOCK), BLOCK)
        more = dot_cols(core.d_keyvalue[at], core.w_keyvalue[...]) * core.params[0:1]
        scaled_grad[at] = (scaled_grad[at].astype(F32) + more).astype(BF16)

    scaled_grad[used:] = jnp.zeros((rows - used, model), BF16)

    @pl.loop(0, model // BLOCK)
    def _(index):
        at = pl.ds(pl.multiple_of(index * BLOCK, BLOCK), BLOCK)
        normed = core.normed1[:used, at]
        g_query[at] = dot_rows(normed, core.d_query[:used]).astype(BF16)
        g_keyvalue[at] = dot_rows(normed, core.d_keyvalue[:used]).astype(BF16)

    for i in range(4):
        g_norms[i : i + 1] = jnp.sum(core.d_norms[i], axis=0, keepdims=True)
    for i, more in enumerate(core.keyvalue_norms()):
        g_norms[i : i + 1] += more


def run_plain(seq_lengths, norms, arrays, z):
    tokens, cotangent, w_query, w_keyvalue, w_up, w_down, w_out = arrays
    width, model = w_query.shape[1], tokens.shape[1]
    wide = z.wide
    pad = jnp.pad(w_query[:, width // 128 * 128 :], ((0, 0), (0, wide - width)))
    lane, start = lax.iota(jnp.int32, 128)[None], width % 128
    vectors = jnp.pad(jnp.stack(norms, axis=1), ((0, 0), (start, 124 - start)))
    tail = jnp.where(lane < start, pad, vectors)
    query = jnp.concatenate([w_query[:, : width // 128 * 128], tail], axis=1)
    out = jnp.pad(w_out, ((0, 0), (0, wide - width)))
    gathered = [lax.all_gather(a, "tensor", axis=0, tiled=True) for a in (tokens, cotangent)]
    gathered += [lax.all_gather(a, "dp", axis=0, tiled=True) for a in (query, w_keyvalue, w_up, w_down, out)]
    shape = jax.ShapeDtypeStruct
    results = pl.pallas_call(
        functools.partial(plain_kernel, z),
        out_shape=[shape((z.rows, model), BF16)] * 2
        + [shape((model, n), BF16) for n in (wide, 128, wide, z.units, z.units)]
        + [shape((4, model), F32)],
        in_specs=[pl.BlockSpec(memory_space=pltpu.SMEM)] + [INVMEM] * len(gathered),
        out_specs=[INVMEM] * 8,
        scratch_shapes=[pltpu.VMEM(*entry) for entry in own_shapes(z).values()] + [pltpu.VMEM((n, model), BF16) for n in (z.used, z.rows)],
        compiler_params=pltpu.CompilerParams(vmem_limit_bytes=67043328),
        name="plain_layer",
    )(seq_lengths, *gathered)
    names = ("tensor", "tensor") + ("dp",) * 5
    sums = [
        lax.psum_scatter(p.astype(F32), n, scatter_dimension=0, tiled=True) for p, n in zip(results[:7], names)
    ]
    norm_sums = lax.psum_scatter(results[7], "dp", scatter_dimension=1, tiled=True)
    shared_kv = lax.all_gather(sums[3], "tensor")
    shared_norms = lax.all_gather(jnp.pad(norm_sums, ((0, 4), (0, 0))), "tensor")
    return sums[0], sums[1], sums[2], sums[4], sums[5], sums[6], shared_kv, shared_norms


def run_whole(seq_lengths, norms, arrays, z):
    arrays_of, semaphores = fused_specs(z)
    scratch = [pltpu.VMEM(*entry) for entry in arrays_of.values()]
    scratch += [pltpu.SemaphoreType.DMA(shape) for shape in semaphores.values()]
    return pl.pallas_call(
        functools.partial(fused_kernel, z, tuple(arrays_of) + tuple(semaphores)),
        out_shape=[jax.ShapeDtypeStruct(shape, F32) for shape in output_shapes(z)],
        in_specs=[pl.BlockSpec(memory_space=pltpu.SMEM)]
        + [INVMEM] * 4
        + [INVMEM if packed else ANY for packed in (False, False, True, False, False, False, True)],
        out_specs=[ANY] * len(OUTPUTS),
        scratch_shapes=scratch,
        compiler_params=pltpu.CompilerParams(collective_id=0, has_side_effects=True, vmem_limit_bytes=67043328),
        name="layer",
    )(seq_lengths, *norms, *arrays)


def run_layer(seq_lengths, norms, arrays, nd, nt):
    tokens, _, w_query, w_keyvalue, w_up, _, _ = arrays
    heads, own, units = w_query.shape[1] // 64, w_query.shape[0], w_up.shape[1]
    slots, model = tokens.shape
    z = types.SimpleNamespace(
        nd=nd, nt=nt, heads=heads, rows=slots * nt, model=model, stack=heads * BLOCK, units=units, used=SEQ_MOST,
        wide=(heads * 64 + 4 + 127) // 128 * 128, own=own, slots=slots,
    )
    run = run_whole if own % 32 == 0 and slots == 2 * BLOCK and nt == 4 and SEQ_MOST == 7 * BLOCK else run_plain
    sums = run(seq_lengths, norms, arrays, z)
    steps = 2 if own % 16 == 0 else 1
    shape = jax.ShapeDtypeStruct

    def block(rows, columns):
        return pl.BlockSpec((rows // steps, columns), lambda i: (i, 0))

    width = heads * 64
    token_rows = block(slots, model)
    weights = [block(own, n) for n in (z.wide, z.wide, units, units)]
    shared = [
        pl.BlockSpec((nt, own // steps, 128), lambda i: (0, i, 0)),
        pl.BlockSpec((nt, 8, own), lambda i: (0, 0, 0)),
    ]
    results = pl.pallas_call(
        functools.partial(finish_kernel, z),
        grid=(steps,),
        out_shape=[shape((slots, model), BF16), shape((slots, model), F32)]
        + [shape((own, n), F32) for n in (width, 128, width, units, units)]
        + [shape((own,), F32)] * 4,
        in_specs=[pl.BlockSpec(memory_space=pltpu.SMEM)] + [token_rows] * 4 + weights + shared,
        out_specs=[token_rows] * 2
        + [block(own, n) for n in (width, 128, width, units, units)]
        + [pl.BlockSpec((own,), lambda i: (0,))] * 4,
        compiler_params=pltpu.CompilerParams(vmem_limit_bytes=67043328),
        name="finish",
    )(seq_lengths, *arrays[:2], *sums)
    return tuple(results)


def shards(
    tokens,
    cotangent,
    seq_lengths,
    w_query,
    w_keyvalue,
    w_out,
    w_up,
    w_down,
    norm1_gain,
    norm1_bias,
    norm2_gain,
    norm2_bias,
):
    norms = (norm1_gain, norm1_bias, norm2_gain, norm2_bias)
    arrays = (tokens, cotangent, w_query, w_keyvalue, w_up, w_down, w_out)
    return run_layer(seq_lengths, norms, arrays, lax.axis_size("dp"), lax.axis_size("tensor"))


def solution(mesh):
    return jax.shard_map(
        shards,
        mesh=mesh,
        in_specs=(
            P(("dp", "tensor"), None),
            P(("dp", "tensor"), None),
            P("dp", None),
            P("dp", "tensor"),
            P("dp", None),
            P("dp", "tensor"),
            P("dp", "tensor"),
            P("dp", "tensor"),
            P("dp"),
            P("dp"),
            P("dp"),
            P("dp"),
        ),
        out_specs=(
            P(("dp", "tensor"), None),
            P(("dp", "tensor"), None),
            P("dp", "tensor"),
            P("dp", None),
            P("dp", "tensor"),
            P("dp", "tensor"),
            P("dp", "tensor"),
            P("dp"),
            P("dp"),
            P("dp"),
            P("dp"),
        ),
        check_vma=False,
    )
```
